32 devices in a mesh: seq: 32 (over z, y, x, core).
Axes of the slice: x: 2, y: 2, z: 4, core: 2. Of those that a mesh axis runs over, the one named last changes fastest.
Arguments:
- tokens: bfloat16 [5120, 2048], P('seq'), may hold values from -6 to 6
- cotangent: bfloat16 [5120, 2048], P('seq'), may hold values from -6 to 6
- gate_codes: int32 [5120, 256], P('seq'), may hold values from 256 to 4096, as said below
- lengths: int32 [4], replicated, may hold values from 1 to 2560, 5120 in all
- mixer_gain: bfloat16 [2048], P('seq'), may hold values from 0.099609375 to 1.8984375
- query_weight: bfloat16 [2048, 2048], P('seq'), may hold values from -0.125 to 0.125
- key_weight: bfloat16 [2048, 2048], P('seq'), may hold values from -0.125 to 0.125
- value_weight: bfloat16 [2048, 2048], P('seq'), may hold values from -0.125 to 0.125
- head_gain: bfloat16 [2048], P('seq'), may hold values from 0.099609375 to 1.8984375
- output_weight: bfloat16 [2048, 2048], P('seq'), may hold values from -0.125 to 0.125
- feed_gain: bfloat16 [2048], P('seq'), may hold values from 0.099609375 to 1.8984375
- gate_weight: bfloat16 [2048, 5632], P('seq'), may hold values from -0.125 to 0.125
- up_weight: bfloat16 [2048, 5632], P('seq'), may hold values from -0.125 to 0.125
- down_weight: bfloat16 [2048, 5632], P('seq'), may hold values from -0.078125 to 0.078125
Outputs:
- block_out: bfloat16 [5120, 2048], P('seq')
- input_grad: float32 [5120, 2048], P('seq')
- mixer_gain_grad: float32 [2048], P('seq')
- query_grad: float32 [2048, 2048], P('seq')
- key_grad: float32 [2048, 2048], P('seq')
- value_grad: float32 [2048, 2048], P('seq')
- head_gain_grad: float32 [2048], P('seq')
- output_weight_grad: float32 [2048, 2048], P('seq')
- feed_gain_grad: float32 [2048], P('seq')
- gate_grad: float32 [2048, 5632], P('seq')
- up_grad: float32 [2048, 5632], P('seq')
- down_grad: float32 [2048, 5632], P('seq')
The draws below stay inside these ranges and needn't reach their ends.
Inputs may be any that keep to these rules, and one draw needn't show every extreme that they name: `gate_codes`: whole numbers, forget-gate logits of each token and each of the 4 x 64 slots, times 256. The 4 sequences lie one after another along the tokens; the lengths add up to 5120 and the longest is exactly 2560.
All inputs are finite; a program needn't handle non-finite values.
Results may differ from the reference program's by a relative error of at most 0.017.
The reference program's roundings to bfloat16 on the way count: a program that leaves them out, or rounds other values in their place, can miss the bound.
Values may be sent and summed in bfloat16 or wider, within the bound.
A program may use at most 504 MiB of HBM per device.

```python
import math
import jax
import jax.numpy as jnp
import numpy as np
from jax import lax

D = 2048
HEADS = 4
SLOTS = 64
FF = 5632
TOK_DEV = 160
SEQS = 4
TOKEN_TOTAL = 5120
LONGEST = 2560


def draw_tokens(key, part):
    perturbation_key, direction_key = jax.random.split(jax.random.fold_in(key, 11))
    span_rows = max(LONGEST // 4, 1)
    span_count = TOKEN_TOTAL // span_rows + 1
    directions = jax.random.normal(direction_key, (span_count, D), jnp.float32)
    span_index = jnp.arange(TOKEN_TOTAL) // span_rows
    shared = directions[span_index]
    noise_part = jax.random.normal(perturbation_key, (TOKEN_TOTAL, D), jnp.float32) * 0.9
    return jnp.clip(noise_part + 0.4 * shared, -6.0, 6.0).astype(jnp.bfloat16)


def draw_gate_codes(key, part):
    category_random_key, machine_random_key, perturbation_key, spike_random_key, parent_random_key = jax.random.split(key, 5)
    channels = HEADS * SLOTS
    table = jnp.array([int(256 * math.log(max(LONGEST // 2, 2))), int(256 * math.log(2 * TOK_DEV)), int(256 * math.log(40))], jnp.int32)
    kinds = jax.random.randint(category_random_key, (channels,), 0, 3)
    channel_code = jnp.sum(jnp.where(kinds[:, None] == jnp.arange(3)[None, :], table[None, :], 0), axis=1)
    device_shift = jnp.repeat(jax.random.randint(machine_random_key, (TOKEN_TOTAL // TOK_DEV, 1), -128, 129), TOK_DEV, axis=0)
    noise = jax.random.randint(perturbation_key, (TOKEN_TOTAL, channels), -90, 91)
    codes = channel_code[None, :] + device_shift + noise
    spike_events = jax.random.randint(spike_random_key, (3,), 0, TOKEN_TOTAL)
    struck_entries = jnp.any(jnp.arange(TOKEN_TOTAL)[:, None] == spike_events[None, :], axis=1)
    codes = jnp.where(struck_entries[:, None], 256, codes)
    top_row = jax.random.randint(parent_random_key, (), 0, TOKEN_TOTAL)
    top_column = jax.random.randint(jax.random.fold_in(parent_random_key, 7), (), 0, channels)
    marked = (jnp.arange(TOKEN_TOTAL)[:, None] == top_row) & (jnp.arange(channels)[None, :] == top_column)
    return jnp.where(marked, 4096, codes).astype(jnp.int32)


def block_levels(key, shape, shards, low, high):
    level, own = 1.0, jax.random.fold_in(key, 6)
    for axis_at, shards_of in shards:
        draws = jnp.exp(jax.random.uniform(jax.random.fold_in(own, axis_at), (shards_of,), jnp.float32, low / len(shards), high / len(shards)))
        level = level * jnp.repeat(draws, shape[axis_at] // shards_of).reshape([-1 if axis == axis_at else 1 for axis in range(len(shape))])
    return level


def profile(count, total, limit, slope):
    portions = [(1 << 20) // math.isqrt(grade ** slope) + 1 for grade in range(2, count + 1)]
    rest, holding = total - limit - (count - 1), [1] * (count - 1)
    while rest > 0:
        candidates = [i for i in range(count - 1) if holding[i] < limit]
        whole, remaining = sum([portions[i] for i in candidates]), rest
        for i in candidates:
            extra = min(limit - holding[i], max(1, remaining * portions[i] // whole), rest)
            holding[i] = holding[i] + extra
            rest = rest - extra
    return np.array([limit] + holding)


def uneven(key, amount, total, limit, skew):
    if amount == 2:
        one = jax.random.randint(key, (), max(1, total - limit), min(limit, total - 1) + 1)
        return jnp.stack([one, total - one])
    tallies = jnp.asarray(profile(amount, total, limit, skew), jnp.int32)
    couples = (amount - 1) // 2
    giver, taker = tallies[1:1 + 2 * couples:2], tallies[2:2 + 2 * couples:2]
    room = jnp.minimum(giver - 1, limit - taker)
    moved = jax.random.randint(jax.random.fold_in(key, 1), (couples,), 0, 1 << 20) % (room + 1)
    tallies = tallies.at[1:1 + 2 * couples:2].set(giver - moved).at[2:2 + 2 * couples:2].set(taker + moved)
    return tallies[jax.random.permutation(jax.random.fold_in(key, 2), amount)]


def centred(own_key, dims, scale, reach, shards=(), kind=jnp.bfloat16):
    entries = jax.random.normal(own_key, dims, jnp.float32) * scale
    if len(shards) > 0:
        entries = block_levels(own_key, dims, shards, -0.22, 0.18) * entries
    return jnp.clip(entries, min=-reach, max=reach).astype(kind)


def setup_inputs(seed: int = 0) -> dict:
    arg_keys = jax.random.split(jax.random.key(seed), 15)
    tokens = draw_tokens(jax.random.fold_in(arg_keys[14], 71), 0)
    cotangent = centred(arg_keys[1], (TOKEN_TOTAL, D), 1.0, 6.0, ((0, 32),))
    gate_codes = draw_gate_codes(jax.random.fold_in(arg_keys[14], 71), 0)
    lengths = uneven(arg_keys[3], SEQS, TOKEN_TOTAL, LONGEST, 1).astype(jnp.int32)
    mixer_gain = jnp.clip(1.0 + 0.18 * jax.random.normal(arg_keys[4], (D,), jnp.float32), 0.099609375, 1.8984375).astype(jnp.bfloat16)
    query_weight = centred(arg_keys[5], (D, D), D ** -0.5, 0.125, ((0, 32),))
    key_weight = centred(arg_keys[6], (D, D), D ** -0.5, 0.125, ((0, 32),))
    value_weight = centred(arg_keys[7], (D, D), D ** -0.5, 0.125, ((0, 32),))
    head_gain = jnp.clip(1.0 + 0.18 * jax.random.normal(arg_keys[8], (D,), jnp.float32), 0.099609375, 1.8984375).astype(jnp.bfloat16)
    output_weight = centred(arg_keys[9], (D, D), D ** -0.5, 0.125, ((0, 32),))
    feed_gain = jnp.clip(1.0 + 0.18 * jax.random.normal(arg_keys[10], (D,), jnp.float32), 0.099609375, 1.8984375).astype(jnp.bfloat16)
    gate_weight = centred(arg_keys[11], (D, FF), D ** -0.5, 0.125, ((0, 32),))
    up_weight = centred(arg_keys[12], (D, FF), D ** -0.5, 0.125, ((0, 32),))
    down_weight = centred(arg_keys[13], (D, FF), FF ** -0.5, 0.078125, ((0, 32),))
    return dict(tokens=tokens, cotangent=cotangent, gate_codes=gate_codes, lengths=lengths, mixer_gain=mixer_gain, query_weight=query_weight, key_weight=key_weight, value_weight=value_weight, head_gain=head_gain, output_weight=output_weight, feed_gain=feed_gain, gate_weight=gate_weight, up_weight=up_weight, down_weight=down_weight)


@jax.custom_vjp
def low(v):
    return lax.optimization_barrier(v.astype(jnp.bfloat16)).astype(jnp.float32)

@jax.custom_vjp
def reduced_backward(v):
    return v

def low_keep(v):
    return (low(v), None)

def low_pass(kept, grad):
    return (grad,)

def back_keep(v):
    return (v, None)

def back_low(kept, grad):
    return (low(grad),)
low.defvjp(low_keep, low_pass)
reduced_backward.defvjp(back_keep, back_low)
epsilon = 1e-06
highest = lax.Precision.HIGHEST

def rms_factor(value_rows):
    return lax.rsqrt(lax.optimization_barrier(jnp.mean(value_rows * value_rows, axis=-1, keepdims=True)) + epsilon)

def precise_result(form, left, right):
    return jnp.einsum(form, left, right, precision=highest, preferred_element_type=jnp.float32)

def matmul(left, right):
    return jnp.dot(left, right, precision=highest, preferred_element_type=jnp.float32)

def block_tables(decay, starts):
    count = jnp.cumsum(starts)
    length = decay.shape[0]
    places = jnp.arange(length)
    before = places[:, None] >= places[None, :]
    same = jnp.where(before & (count[:, None] == count[None, :]), 1.0, 0.0).astype(jnp.float32)
    fresh_state = jnp.where(count == 0, 1.0, 0.0).astype(jnp.float32)
    logsum = jnp.cumsum(decay, axis=0)
    growth_factor = jnp.exp(logsum)
    backward_pass = jnp.exp(-logsum) * -jnp.expm1(decay)
    tail = jnp.where(count == count[-1], 1.0, 0.0).astype(jnp.float32)
    weight_matrix = growth_factor[-1][None] * backward_pass * tail[:, None, None]
    carried_state = fresh_state[-1] * growth_factor[-1]
    return (same, fresh_state, growth_factor, backward_pass, weight_matrix, carried_state)

def mix_block(state, inputs):
    running_key_state, running_value_state = state
    query_rows, key_rows, value_rows, decay, starts = inputs
    same, fresh_state, growth_factor, backward_pass, weight_matrix, carried_state = block_tables(decay, starts)
    affinity = reduced_backward(precise_result('thd,shd->hts', query_rows, key_rows))
    masked_scores = affinity * same[None]
    score_matrix = growth_factor * precise_result('ynf,fye->nye', masked_scores, backward_pass) + growth_factor * fresh_state[:, None, None] * precise_result('egr,gjr->egj', query_rows, running_key_state)
    probs = jax.nn.softmax(score_matrix, axis=-1)
    lifted = probs * growth_factor
    mixing_matrix = low(precise_result('thm,shm->hts', lifted, backward_pass) * same[None])
    entry_point = lifted * fresh_state[:, None, None]
    final_result = reduced_backward(precise_result('via,avj->ivj', mixing_matrix, value_rows) + precise_result('xfj,fjg->xfg', entry_point, running_value_state))
    upcoming_key = carried_state[..., None] * running_key_state + precise_result('oft,ofi->fti', weight_matrix, key_rows)
    upcoming_value = carried_state[..., None] * running_value_state + precise_result('oft,ofi->fti', weight_matrix, value_rows)
    return ((upcoming_key, upcoming_value), final_result)

def forward(tokens_f, mixer_gain, query_weight, key_weight, value_weight, head_gain, output_weight, feed_gain, gate_weight, up_weight, down_weight, decay, starts):
    head_size = D // HEADS
    blocks = TOKEN_TOTAL // TOK_DEV
    h1 = low(tokens_f * rms_factor(tokens_f) * mixer_gain)
    query_rows = low(reduced_backward(matmul(h1, query_weight)))
    key_rows = low(reduced_backward(matmul(h1, key_weight)))
    value_rows = low(reduced_backward(matmul(h1, value_weight)))
    shaped = (blocks, TOK_DEV, HEADS, head_size)
    inputs = (query_rows.reshape(shaped), key_rows.reshape(shaped), value_rows.reshape(shaped), decay.reshape(blocks, TOK_DEV, HEADS, SLOTS), starts.reshape(blocks, TOK_DEV))
    empty = jnp.zeros((HEADS, SLOTS, head_size), jnp.float32)
    final, slot_output = lax.scan(jax.checkpoint(mix_block), (empty, empty), inputs)
    slot_output = slot_output.reshape(TOKEN_TOTAL, HEADS, head_size)
    normed_heads = low(slot_output * rms_factor(slot_output) * head_gain.reshape(HEADS, head_size)).reshape(TOKEN_TOTAL, D)
    residual = tokens_f + reduced_backward(matmul(normed_heads, output_weight))
    h2 = low(residual * rms_factor(residual) * feed_gain)
    gate = reduced_backward(matmul(h2, gate_weight))
    upward = reduced_backward(matmul(h2, up_weight))
    hidden = low(jax.nn.silu(gate) * upward)
    feed_out = reduced_backward(lax.dot_general(hidden, down_weight, (((1,), (1,)), ((), ())), precision=highest, preferred_element_type=jnp.float32))
    return residual + feed_out

def reference(tokens, cotangent, gate_codes, lengths, mixer_gain, query_weight, key_weight, value_weight, head_gain, output_weight, feed_gain, gate_weight, up_weight, down_weight):
    decay = jax.nn.log_sigmoid(gate_codes.astype(jnp.float32) / 256.0).reshape(TOKEN_TOTAL, HEADS, SLOTS)
    first_token = jnp.cumsum(lengths) - lengths
    position = jnp.arange(TOKEN_TOTAL, dtype=jnp.int32)
    starts = lax.optimization_barrier(jnp.sum(jnp.where(position[:, None] == first_token[None, :], 1, 0), axis=1)).astype(jnp.int32)
    floats = [tokens, mixer_gain, query_weight, key_weight, value_weight, head_gain, output_weight, feed_gain, gate_weight, up_weight, down_weight]
    floats = [item.astype(jnp.float32) for item in floats]

    def whole(*params):
        return forward(*params, decay, starts)
    final_result, pullback = jax.vjp(whole, *floats)
    grads = pullback(cotangent.astype(jnp.float32))
    return (final_result.astype(jnp.bfloat16), grads[0], grads[1], grads[2], grads[3], grads[4], grads[5], grads[6], grads[7], grads[8], grads[9], grads[10])
```

```python
import jax
import jax.numpy as jnp
from jax import lax
from jax.experimental import pallas as pl
from jax.experimental.pallas import tpu as pltpu
from jax.sharding import PartitionSpec as P

HEADS = 4
SLOTS = 64
PLANE = 8

epsilon = 1e-06
highest = lax.Precision.HIGHEST
bf16 = jnp.bfloat16
f32 = jnp.float32
MESH = pl.DeviceIdType.MESH
ANY = pl.BlockSpec(memory_space=pl.ANY)


def exchange(cid, arrays, outs, moves, plan):
    def kernel(*refs):
        ins = refs[: len(arrays)]
        dsts = refs[len(arrays) : len(arrays) + len(outs)]
        send, recv = refs[len(arrays) + len(outs) :]
        me = lax.axis_index("seq")
        peers, copies = plan(me, ins, dsts)
        barrier = pltpu.get_barrier_semaphore()
        for peer in peers:
            pl.semaphore_signal(barrier, inc=1, device_id=(peer,), device_id_type=MESH)
        pl.semaphore_wait(barrier, len(peers))
        started = []
        for k, (src, dst, device) in enumerate(copies):
            if device is None:
                copy = pltpu.make_async_copy(src, dst, send.at[k])
            else:
                copy = pltpu.make_async_remote_copy(
                    src_ref=src,
                    dst_ref=dst,
                    send_sem=send.at[k],
                    recv_sem=recv.at[k],
                    device_id=(device,),
                    device_id_type=MESH,
                )
            copy.start()
            started.append(copy)
        for copy in started:
            copy.wait()

    return pl.pallas_call(
        kernel,
        out_shape=[jax.ShapeDtypeStruct(s, d) for s, d in outs],
        in_specs=[ANY] * len(arrays),
        out_specs=[ANY] * len(outs),
        scratch_shapes=[
            pltpu.SemaphoreType.DMA((moves,)),
            pltpu.SemaphoreType.DMA((moves,)),
        ],
        compiler_params=pltpu.CompilerParams(collective_id=cid, has_side_effects=True),
    )(*arrays)


def chip_of(me):
    return lax.rem(lax.div(me, 2), HEADS)


def same_core(me, h, k):
    other = lax.rem(h + k, HEADS)
    return me + 2 * (other - h), other


def rows_at(ref, block, size):
    return ref.at[pl.ds(pl.multiple_of(block * size, size), size)]


def columns_at(ref, block, size):
    return ref.at[:, pl.ds(pl.multiple_of(block * size, 128), size)]


def gather_plane(cid, x):
    rows = x.shape[0]

    def plan(me, ins, outs):
        h = chip_of(me)
        peers = [same_core(me, h, k)[0] for k in (1, 2, 3)]
        dst = rows_at(outs[0], h, rows)
        return peers, [(ins[0], dst, p) for p in peers] + [(ins[0], dst, None)]

    return exchange(cid, [x], [((HEADS * rows, *x.shape[1:]), x.dtype)], 4, plan)[0]


def swap_plane(cid, x):
    rows = x.shape[0] // HEADS

    def plan(me, ins, outs):
        h = chip_of(me)
        dst = rows_at(outs[0], h, rows)
        pairs = [same_core(me, h, k) for k in (1, 2, 3)]
        moves = [(rows_at(ins[0], o, rows), dst, p) for p, o in pairs]
        return [p for p, _ in pairs], moves + [(rows_at(ins[0], h, rows), dst, None)]

    return exchange(cid, [x], [(x.shape, x.dtype)], 4, plan)[0]


def swap_core(cid, x):
    def plan(me, ins, outs):
        peer = me + 1 - 2 * lax.rem(me, 2)
        return [peer], [(ins[0], outs[0], peer)]

    return exchange(cid, [x], [(x.shape, x.dtype)], 1, plan)[0]


def gather_planes(cid, x, count):
    def plan(me, ins, outs):
        z = lax.div(me, PLANE)
        peers = [me + PLANE * (lax.rem(z + k, count) - z) for k in range(1, count)]
        dst = outs[0].at[z]
        return peers, [(ins[0], dst, p) for p in peers] + [(ins[0], dst, None)]

    return exchange(cid, [x], [((count, *x.shape), x.dtype)], count, plan)[0]


def swap_all(cid, x, count):
    def plan(me, ins, outs):
        peers = [lax.rem(me + k, count) for k in range(1, count)]
        moves = [(ins[0].at[p], outs[0].at[me], p) for p in peers]
        return peers, moves + [(ins[0].at[me], outs[0].at[me], None)]

    return exchange(cid, [x], [(x.shape, x.dtype)], count, plan)[0]


def first_exchange(cid, gains, weights, codes, count):
    rows, width = weights[0].shape
    part = width // HEADS

    def plan(me, ins, outs):
        g_in, q_in, k_in, v_in, c_in = ins
        g_out, w_out, c_out = outs
        h = chip_of(me)
        everyone = [lax.rem(me + k, count) for k in range(1, count)]
        moves = [(g_in, g_out.at[me], p) for p in everyone] + [(g_in, g_out.at[me], None)]
        targets = [same_core(me, h, k) for k in (1, 2, 3)] + [(None, h)]
        for device, other in targets:
            moves.append((c_in.at[other], c_out.at[h], device))
            for j, w in enumerate((q_in, k_in, v_in)):
                dst = w_out.at[
                    pl.ds(pl.multiple_of(h * rows, rows), rows), pl.ds(j * part, part)
                ]
                moves.append((columns_at(w, other, part), dst, device))
        return everyone, moves

    return exchange(
        cid,
        [gains, *weights, codes],
        [
            ((count, *gains.shape), gains.dtype),
            ((HEADS * rows, 3 * part), bf16),
            (codes.shape, codes.dtype),
        ],
        count + 16,
        plan,
    )


def second_exchange(cid, gate, up, down):
    rows, width = gate.shape
    part = width // HEADS

    def plan(me, ins, outs):
        h = chip_of(me)
        targets = [same_core(me, h, k) for k in (1, 2, 3)] + [(None, h)]
        at = pl.ds(pl.multiple_of(h * rows, rows), rows)
        moves = []
        for w, out, column in ((0, 0, 0), (1, 0, part), (2, 1, 0)):
            for device, other in targets:
                dst = outs[out].at[at, pl.ds(column, part)]
                moves.append((columns_at(ins[w], other, part), dst, device))
        return [p for p, _ in targets[:3]], moves

    return exchange(
        cid,
        [gate, up, down],
        [((HEADS * rows, 2 * part), bf16), ((HEADS * rows, part), bf16)],
        12,
        plan,
    )


def return_columns(cid, x, pieces):
    rows = x.shape[0] // HEADS
    part = x.shape[1] // pieces

    def plan(me, ins, outs):
        h = chip_of(me)
        targets = [same_core(me, h, k) for k in (1, 2, 3)] + [(None, h)]
        moves = []
        for device, other in targets:
            for j in range(pieces):
                src = ins[0].at[
                    pl.ds(pl.multiple_of(other * rows, rows), rows), pl.ds(j * part, part)
                ]
                moves.append((src, columns_at(outs[j], h, part), device))
        return [p for p, _ in targets[:3]], moves

    return exchange(
        cid, [x], [((rows, HEADS * part), x.dtype)] * pieces, 4 * pieces, plan
    )


def rms_factor(value_rows):
    return lax.rsqrt(jnp.mean(value_rows * value_rows, axis=-1, keepdims=True) + epsilon)


def precise(form, left, right):
    return jnp.einsum(form, left, right, precision=highest, preferred_element_type=f32)


def plain(form, left, right):
    return jnp.einsum(form, left, right, preferred_element_type=f32)


def local(
    tokens,
    cotangent,
    gate_codes,
    lengths,
    mixer_gain,
    query_weight,
    key_weight,
    value_weight,
    head_gain,
    output_weight,
    feed_gain,
    gate_weight,
    up_weight,
    down_weight,
):
    count = lax.axis_size("seq")
    planes = count // PLANE
    me = lax.axis_index("seq")
    z, h, core = me // PLANE, (me // 2) % HEADS, me % 2
    rows, width = tokens.shape
    strip = query_weight.shape[0]
    head_size = width // HEADS
    lines = [
        [p * PLANE + c * 2 + k for p in range(planes) for k in range(2)] for c in range(HEADS)
    ]

    def gather_line(x):
        return lax.all_gather(x, "seq", axis=0, tiled=True, axis_index_groups=lines)

    def scatter_line(x):
        return lax.psum_scatter(
            x, "seq", scatter_dimension=0, tiled=True, axis_index_groups=lines
        )

    def shuffled(x):
        y = x.reshape(*x.shape[:-1], planes, HEADS, 2, strip)
        return jnp.swapaxes(y, -3, -2).reshape(x.shape)

    def restored(x):
        y = x.reshape(*x.shape[:-1], planes, 2, HEADS, strip)
        return jnp.swapaxes(y, -3, -2).reshape(x.shape)

    gains = jnp.stack([mixer_gain, head_gain, feed_gain]).astype(f32)
    gains = jnp.pad(gains, ((0, 5), (0, 128 - strip)))
    codes = gate_codes.reshape(rows, HEADS, SLOTS).swapaxes(0, 1)
    gains_all, mixer_rows, codes_all = first_exchange(
        0, gains, (query_weight, key_weight, value_weight), codes, count
    )
    mixer_weight = gather_line(mixer_rows)
    feed_rows, down_rows = second_exchange(1, gate_weight, up_weight, down_weight)
    output_line = gather_line(shuffled(output_weight))
    feed_weight = gather_line(feed_rows)
    down_line = gather_line(down_rows)
    gain_of = gains_all[:, :3, :strip].swapaxes(0, 1).reshape(3, width)
    gain_one, gain_two = shuffled(gain_of[0]), shuffled(gain_of[2])
    head_gain_f = lax.dynamic_slice(gain_of[1], (h * head_size,), (head_size,))

    tokens_f = shuffled(tokens).astype(f32)
    factor_one = rms_factor(tokens_f)
    normed_one = tokens_f * factor_one
    h1 = gather_plane(2, (normed_one * gain_one).astype(bf16))
    cotangent_own = shuffled(cotangent)
    cotangent_all = gather_plane(3, cotangent_own)

    decay = jax.nn.log_sigmoid(codes_all.astype(f32) / 256.0)
    block = z * PLANE + 2 * jnp.arange(HEADS) + core
    first = (block * rows)[:, None]
    position = first + jnp.arange(rows)[None, :]
    order = jnp.arange(lengths.shape[0])
    first_token = jnp.sum(
        jnp.where(order[:, None] > order[None, :], lengths[None, :], 0), axis=1
    )
    seen = jnp.sum(
        jnp.where(
            (first_token[None, None, :] <= position[:, :, None])
            & (first_token[None, None, :] >= first[:, :, None]),
            1,
            0,
        ),
        axis=2,
    )
    places = jnp.arange(rows)
    before = places[:, None] >= places[None, :]
    same = jnp.where(before[None] & (seen[:, :, None] == seen[:, None, :]), 1.0, 0.0).astype(f32)
    fresh = jnp.where(seen == 0, 1.0, 0.0).astype(f32)[:, :, None]
    logsum = precise("ts,bsm->btm", before.astype(f32), decay)
    grow = jnp.exp(logsum)
    back = jnp.exp(-logsum) * -jnp.expm1(decay)
    tail = jnp.where(seen == seen[:, -1:], 1.0, 0.0).astype(f32)[:, :, None]
    weights = grow[:, -1:] * back * tail
    carried = fresh[:, -1] * grow[:, -1]

    blocked = (HEADS, rows, head_size)
    projected = jnp.dot(h1, mixer_weight, preferred_element_type=f32).astype(bf16)
    query = projected[:, :head_size].reshape(blocked)
    key = projected[:, head_size : 2 * head_size].reshape(blocked)
    value = projected[:, 2 * head_size :].reshape(blocked)
    query_f = query.astype(f32)

    def pack(state, gain):
        return jnp.concatenate(
            [state, jnp.broadcast_to(gain[..., None], (*gain.shape, 128))], axis=-1
        )

    def unpack(x):
        return x[..., :-128], x[..., -128]

    own = pack(
        jnp.concatenate(
            [
                precise("bsm,bsd->bmd", weights, key.astype(f32)),
                precise("bsm,bsd->bmd", weights, value.astype(f32)),
            ],
            axis=-1,
        ),
        carried,
    )
    other = swap_core(4, own)
    even, odd = jnp.where(core == 0, own, other), jnp.where(core == 0, other, own)
    run_state, run_gain = jnp.zeros_like(own[0, :, :-128]), jnp.ones_like(carried[0])
    entries = []
    for k in range(PLANE):
        state, gain = unpack((even, odd)[k % 2][k // 2])
        entries.append((run_state, run_gain))
        run_state, run_gain = gain[:, None] * run_state + state, gain * run_gain
    summaries = gather_planes(5, pack(run_state, run_gain), planes)
    plane_state = jnp.zeros_like(run_state)
    for k in range(planes):
        state, gain = unpack(summaries[k])
        plane_state = jnp.where(k < z, gain[:, None] * plane_state + state, plane_state)

    def pick(pairs, base):
        out = []
        for k in range(HEADS):
            (s0, g0), (s1, g1) = pairs[2 * k], pairs[2 * k + 1]
            s, g = jnp.where(core == 0, s0, s1), jnp.where(core == 0, g0, g1)
            out.append(g[:, None] * base + s)
        return jnp.stack(out)

    state_in = pick(entries, plane_state)
    key_state, value_state = state_in[..., :head_size], state_in[..., head_size:]

    affinity = plain("btd,bsd->bts", query, key) * same
    score = grow * precise("bts,bsm->btm", affinity, back) + grow * fresh * precise(
        "btd,bmd->btm", query_f, key_state
    )
    probs = jax.nn.softmax(score, axis=-1)
    lifted = probs * grow
    mixing = (precise("btm,bsm->bts", lifted, back) * same).astype(bf16)
    entry = lifted * fresh
    slot_out = plain("bts,bsd->btd", mixing, value) + precise("btm,bmd->btd", entry, value_state)
    head_factor = rms_factor(slot_out)
    unit_heads = slot_out * head_factor
    normed_heads = (unit_heads * head_gain_f).astype(bf16).reshape(HEADS * rows, head_size)

    quarter = planes // HEADS
    out_rows = swap_plane(6, output_line)
    out_weight = (
        out_rows.reshape(HEADS, quarter, 2 * strip, width)
        .swapaxes(0, 1)
        .reshape(head_size, width)
    )
    mixed = jnp.dot(normed_heads, out_weight, preferred_element_type=f32).astype(bf16)

    def summed(cid, partial):
        parts = swap_plane(cid, partial).reshape(HEADS, rows, width).astype(f32)
        return parts[0] + parts[1] + parts[2] + parts[3]

    residual = tokens_f + summed(7, mixed)
    factor_two = rms_factor(residual)
    normed_two = residual * factor_two
    h2 = gather_plane(8, (normed_two * gain_two).astype(bf16))

    part = down_line.shape[1]
    both = jnp.dot(h2, feed_weight, preferred_element_type=f32)
    gate, upward = both[:, :part], both[:, part:]
    sigma = jax.nn.sigmoid(gate)
    active = gate * sigma
    hidden = (active * upward).astype(bf16)
    hidden_grad = jnp.dot(cotangent_all, down_line, preferred_element_type=f32)
    gate_back = (hidden_grad * upward * sigma * (1.0 + gate * (1.0 - sigma))).astype(bf16)
    up_back = (hidden_grad * active).astype(bf16)
    both_back = jnp.concatenate([gate_back, up_back], axis=1)
    feed_in = plain("tf,df->td", both_back, feed_weight).astype(bf16)
    feed_in_grad = summed(9, feed_in)
    feed_sums = scatter_line(plain("td,tf->df", h2, both_back).astype(bf16))
    down_sums = scatter_line(plain("td,tf->df", cotangent_all, hidden).astype(bf16))
    feed_out = plain("tf,df->td", hidden, down_line).astype(bf16)
    block_out = restored((residual + summed(10, feed_out)).astype(bf16))

    feed_gain_part = jnp.sum(normed_two * feed_in_grad, axis=0)
    scaled_two = feed_in_grad * gain_two
    residual_grad = cotangent_own.astype(f32) + factor_two * (
        scaled_two - normed_two * jnp.mean(normed_two * scaled_two, axis=-1, keepdims=True)
    )
    mixed_grad = gather_plane(11, residual_grad.astype(bf16))

    heads_grad = plain("td,fd->tf", mixed_grad, out_weight).reshape(blocked)
    head_gain_part = jnp.sum(unit_heads * heads_grad, axis=(0, 1))
    scaled_heads = heads_grad * head_gain_f
    out_back = (
        head_factor
        * (scaled_heads - unit_heads * jnp.mean(unit_heads * scaled_heads, axis=-1, keepdims=True))
    ).astype(bf16)
    out_back_f = out_back.astype(f32)
    mixing_grad = plain("btd,bsd->bts", out_back, value) * same
    local_value = plain("bts,btd->bsd", mixing, out_back)
    lifted_grad = grow * precise("bts,bsm->btm", mixing_grad, back) + grow * fresh * precise(
        "btd,bmd->btm", out_back_f, value_state
    )
    score_grad = probs * (lifted_grad - jnp.sum(probs * lifted_grad, axis=-1, keepdims=True))
    inner_grad = grow * score_grad
    state_grad = inner_grad * fresh
    affinity_grad = (precise("btm,bsm->bts", inner_grad, back) * same).astype(bf16)
    own_back = pack(
        jnp.concatenate(
            [
                precise("btm,btd->bmd", state_grad, query_f),
                precise("btm,btd->bmd", entry, out_back_f),
            ],
            axis=-1,
        ),
        carried,
    )
    other_back = swap_core(12, own_back)
    even = jnp.where(core == 0, own_back, other_back)
    odd = jnp.where(core == 0, other_back, own_back)
    run_state, run_gain = jnp.zeros_like(run_state), jnp.ones_like(run_gain)
    leaving = [None] * PLANE
    for k in reversed(range(PLANE)):
        state, gain = unpack((even, odd)[k % 2][k // 2])
        leaving[k] = (run_state, run_gain)
        run_state, run_gain = gain[:, None] * run_state + state, gain * run_gain
    summaries = gather_planes(13, pack(run_state, run_gain), planes)
    plane_state = jnp.zeros_like(run_state)
    for k in reversed(range(planes)):
        state, gain = unpack(summaries[k])
        plane_state = jnp.where(k > z, gain[:, None] * plane_state + state, plane_state)
    later = pick(leaving, plane_state)
    later_key, later_value = later[..., :head_size], later[..., head_size:]

    query_back = plain("bts,bsd->btd", affinity_grad, key) + precise(
        "btm,bmd->btd", state_grad, key_state
    )
    key_back = plain("bts,btd->bsd", affinity_grad, query) + precise(
        "bsm,bmd->bsd", weights, later_key
    )
    value_back = local_value + precise("bsm,bmd->bsd", weights, later_value)
    backs = jnp.concatenate(
        [
            x.astype(bf16).reshape(HEADS * rows, head_size)
            for x in (query_back, key_back, value_back)
        ],
        axis=1,
    )
    mixer_in_grad = summed(14, plain("tf,df->td", backs, mixer_weight).astype(bf16))
    mixer_gain_part = jnp.sum(normed_one * mixer_in_grad, axis=0)
    scaled_one = mixer_in_grad * gain_one
    input_grad = residual_grad + factor_one * (
        scaled_one - normed_one * jnp.mean(normed_one * scaled_one, axis=-1, keepdims=True)
    )

    out_part = plain("tf,td->fd", normed_heads, mixed_grad).astype(bf16)
    out_part = (
        out_part.reshape(quarter, HEADS, 2 * strip, width)
        .swapaxes(0, 1)
        .reshape(head_size, width)
    )
    out_sums = scatter_line(swap_plane(15, out_part))
    mixer_sums = scatter_line(plain("td,tf->df", h1, backs).astype(bf16))
    gate_grad, up_grad = return_columns(16, feed_sums, 2)
    (down_grad,) = return_columns(17, down_sums, 1)
    query_grad, key_grad, value_grad = return_columns(18, mixer_sums, 3)

    head_whole = lax.dynamic_update_slice(
        jnp.zeros((width,), f32), head_gain_part, (h * head_size,)
    )
    gain_parts = jnp.stack([restored(mixer_gain_part), head_whole, restored(feed_gain_part)])
    gain_parts = gain_parts.reshape(3, count, strip).swapaxes(0, 1)
    gain_parts = jnp.pad(gain_parts, ((0, 0), (0, 5), (0, 128 - strip)))
    gain_sums = jnp.sum(swap_all(19, gain_parts, count), axis=0)[:3, :strip]
    return (
        block_out,
        restored(input_grad),
        gain_sums[0],
        query_grad.astype(f32),
        key_grad.astype(f32),
        value_grad.astype(f32),
        gain_sums[1],
        restored(out_sums).astype(f32),
        gain_sums[2],
        gate_grad.astype(f32),
        up_grad.astype(f32),
        down_grad.astype(f32),
    )


def solution(mesh):
    split, line = P("seq", None), P("seq")
    return jax.shard_map(
        local,
        mesh=mesh,
        in_specs=(split, split, split, P(), line, split, split, split, line, split, line, split, split, split),
        out_specs=(split, split, line, split, split, split, line, split, line, split, split, split),
        check_vma=False,
    )
```

```python
import jax
import jax.numpy as jnp
from jax import lax
from jax.experimental import pallas as pl
from jax.experimental.pallas import tpu as pltpu
from jax.sharding import PartitionSpec as P

HEADS = 4
SLOTS = 64
PLANE = 8

epsilon = 1e-06
highest = lax.Precision.HIGHEST
bf16 = jnp.bfloat16
f32 = jnp.float32
MESH = pl.DeviceIdType.MESH
ANY = pl.BlockSpec(memory_space=pl.ANY)


def exchange(cid, arrays, outs, moves, plan):
    def kernel(*refs):
        ins = refs[: len(arrays)]
        dsts = refs[len(arrays) : len(arrays) + len(outs)]
        send, recv = refs[len(arrays) + len(outs) :]
        me = lax.axis_index("seq")
        peers, copies = plan(me, ins, dsts)
        barrier = pltpu.get_barrier_semaphore()
        for peer in peers:
            pl.semaphore_signal(barrier, inc=1, device_id=(peer,), device_id_type=MESH)
        pl.semaphore_wait(barrier, len(peers))
        started = []
        for k, (src, dst, device) in enumerate(copies):
            if device is None:
                copy = pltpu.make_async_copy(src, dst, send.at[k])
            else:
                copy = pltpu.make_async_remote_copy(
                    src_ref=src,
                    dst_ref=dst,
                    send_sem=send.at[k],
                    recv_sem=recv.at[k],
                    device_id=(device,),
                    device_id_type=MESH,
                )
            copy.start()
            started.append(copy)
        for copy in started:
            copy.wait()

    return pl.pallas_call(
        kernel,
        out_shape=[jax.ShapeDtypeStruct(s, d) for s, d in outs],
        in_specs=[ANY] * len(arrays),
        out_specs=[ANY] * len(outs),
        scratch_shapes=[
            pltpu.SemaphoreType.DMA((moves,)),
            pltpu.SemaphoreType.DMA((moves,)),
        ],
        compiler_params=pltpu.CompilerParams(collective_id=cid, has_side_effects=True),
    )(*arrays)


def chip_of(me):
    return lax.rem(lax.div(me, 2), HEADS)


def chip_on(me, h, k):
    turn = (k % 2) * (1 - 2 * lax.rem(h, 2)) + (k // 2) * (2 - 4 * lax.div(h, 2))
    return me + 2 * turn, h + turn


def rows_at(ref, block, size):
    return ref.at[pl.ds(pl.multiple_of(block * size, size), size)]


def columns_at(ref, block, size):
    return ref.at[:, pl.ds(pl.multiple_of(block * size, 128), size)]


def swap_all(cid, x, count):
    def plan(me, ins, outs):
        peers = [lax.rem(me + k, count) for k in range(1, count)]
        moves = [(ins[0].at[p], outs[0].at[me], p) for p in peers]
        return peers, moves + [(ins[0].at[me], outs[0].at[me], None)]

    return exchange(cid, [x], [(x.shape, x.dtype)], count, plan)[0]


def first_exchange(cid, weights, output_rows):
    rows, width = weights[0].shape
    part = width // HEADS

    def plan(me, ins, outs):
        h = chip_of(me)
        targets = [chip_on(me, h, k) for k in (2, 1, 3)] + [(None, h)]
        at = pl.ds(pl.multiple_of(h * rows, rows), rows)
        moves = []
        for device, other in targets:
            for j in range(3):
                dst = outs[0].at[at, pl.ds(j * part, part)]
                moves.append((columns_at(ins[j], other, part), dst, device))
        for k in range(HEADS):
            dst = outs[0].at[pl.ds(k * rows, rows), pl.ds(3 * part, part)]
            moves.append((ins[3].at[:, pl.ds(k * part, part)], dst, None))
        return [p for p, _ in targets[:3]], moves

    shape = (HEADS * rows, 4 * part)
    return exchange(cid, [*weights, output_rows], [(shape, bf16)], 16, plan)[0]


def second_exchange(cid, gains, codes, gate, up, down, count):
    rows, width = gate.shape
    part = width // HEADS

    def plan(me, ins, outs):
        h = chip_of(me)
        g_in, c_in = ins[:2]
        everyone = [lax.rem(me + k, count) for k in range(1, count)]
        targets = [chip_on(me, h, k) for k in (1, 2, 3)] + [(None, h)]
        at = pl.ds(pl.multiple_of(h * rows, rows), rows)
        moves = [(g_in, outs[0].at[me], p) for p in everyone] + [(g_in, outs[0].at[me], None)]
        for k, (device, other) in zip((1, 2, 3, 0), targets):
            moves.append((c_in.at[other], outs[1].at[k], device))
        for w, out, column in ((2, 2, 0), (3, 2, part), (4, 3, 0)):
            for device, other in targets:
                dst = outs[out].at[at, pl.ds(column, part)]
                moves.append((columns_at(ins[w], other, part), dst, device))
        return everyone, moves

    return exchange(
        cid,
        [gains, codes, gate, up, down],
        [
            ((count, *gains.shape), gains.dtype),
            (codes.shape, codes.dtype),
            ((HEADS * rows, 2 * part), bf16),
            ((HEADS * rows, part), bf16),
        ],
        count + 16,
        plan,
    )


def return_columns(cid, x, pieces):
    rows = x.shape[0] // HEADS
    part = x.shape[1] // pieces

    def plan(me, ins, outs):
        h = chip_of(me)
        targets = [chip_on(me, h, k) for k in (1, 2, 3)] + [(None, h)]
        moves = []
        for device, other in targets:
            for j in range(pieces):
                src = ins[0].at[
                    pl.ds(pl.multiple_of(other * rows, rows), rows), pl.ds(j * part, part)
                ]
                moves.append((src, columns_at(outs[j], h, part), device))
        return [p for p, _ in targets[:3]], moves

    return exchange(
        cid, [x], [((rows, HEADS * part), x.dtype)] * pieces, 4 * pieces, plan
    )


STEP = 16


def reorder(x, planes, back):
    strip = x.shape[1] // (planes * PLANE)
    pieces = []
    for p in range(planes):
        for i in range(PLANE):
            n = (i % 2) * HEADS + i // 2 if back else (i % HEADS) * 2 + i // HEADS
            at = (p * PLANE + n) * strip
            pieces.append(x[:, at : at + strip])
    return jnp.concatenate(pieces, axis=1)


def reordered(arrays, planes):
    def kernel(*refs):
        for src, dst in zip(refs[: len(arrays)], refs[len(arrays) :]):

            def step(i, carry, src=src, dst=dst):
                at = pl.ds(pl.multiple_of(i * STEP, STEP), STEP)
                dst[at, :] = reorder(src[at, :], planes, False)
                return carry

            lax.fori_loop(0, src.shape[0] // STEP, step, 0)

    vmem = pl.BlockSpec(memory_space=pltpu.VMEM)
    return pl.pallas_call(
        kernel,
        out_shape=[jax.ShapeDtypeStruct(x.shape, x.dtype) for x in arrays],
        in_specs=[vmem] * len(arrays),
        out_specs=[vmem] * len(arrays),
        compiler_params=pltpu.CompilerParams(vmem_limit_bytes=32 << 20),
    )(*arrays)


def plane_stage(cid, partial, blocks, body, own, gathered):
    rows, width = blocks[0].shape
    half = rows // 2
    has = int(partial is not None)
    low, high = pl.ds(0, half), pl.ds(half, half)

    def kernel(*refs):
        part = refs[0] if has else None
        block_refs = refs[has : has + len(blocks)]
        rest = refs[has + len(blocks) :]
        own_refs, rest = rest[: len(own)], rest[len(own) :]
        everything, rest = (rest[0], rest[1:]) if gathered else (None, rest)
        by_x, by_y, over_x, over_y, sum_x, sum_y, mine, send, recv, out_send, out_recv = rest
        me = lax.axis_index("seq")
        h = chip_of(me)
        x_side, y_side = chip_on(me, h, 1)[0], chip_on(me, h, 2)[0]
        barrier = pltpu.get_barrier_semaphore()
        for device in (x_side, y_side):
            pl.semaphore_signal(barrier, inc=1, device_id=(device,), device_id_type=MESH)
        pl.semaphore_wait(barrier, 2)

        def to(device, src, dst, sends, recvs, n):
            return pltpu.make_async_remote_copy(
                src_ref=src, dst_ref=dst, send_sem=sends.at[n], recv_sem=recvs.at[n],
                device_id=(device,), device_id_type=MESH,
            )

        def block(k, first):
            return pl.ds(k * rows + (0 if first else half), half)

        if has:
            copies = [
                to(x_side, part.at[block(3, True)], over_x, send, recv, 0),
                to(y_side, part.at[block(3, False)], over_y, send, recv, 1),
                to(x_side, part.at[block(1, True)], by_x.at[low], send, recv, 2),
                to(y_side, part.at[block(2, False)], by_y.at[high], send, recv, 3),
                to(y_side, sum_y, by_y.at[low], send, recv, 4),
                to(x_side, sum_x, by_x.at[high], send, recv, 5),
            ]
            for copy in copies[:4]:
                copy.start()
            copies[0].wait_recv()
            sum_y[...] = (part[block(2, True), :].astype(f32) + over_x[...].astype(f32)).astype(bf16)
            copies[4].start()
            copies[1].wait_recv()
            sum_x[...] = (part[block(1, False), :].astype(f32) + over_y[...].astype(f32)).astype(bf16)
            copies[5].start()
            for copy in copies[:2]:
                copy.wait_send()
            for copy in copies[2:]:
                copy.wait()

        def step(i, carry):
            at = pl.ds(pl.multiple_of(i * STEP, STEP), STEP)
            total = None
            if has:
                total = part[at, :].astype(f32) + by_x[at, :].astype(f32) + by_y[at, :].astype(f32)
            body(i, at, total, block_refs, own_refs, mine)
            return carry

        lax.fori_loop(0, rows // STEP, step, 0)
        if gathered:
            from_x, from_y = everything.at[block(1, True)], everything.at[block(2, False)]
            copies = [
                to(x_side, mine.at[low], from_x, out_send, out_recv, 0),
                to(y_side, mine.at[high], from_y, out_send, out_recv, 1),
                to(x_side, mine.at[high], everything.at[block(1, False)], out_send, out_recv, 2),
                to(y_side, mine.at[low], everything.at[block(2, True)], out_send, out_recv, 3),
                to(y_side, from_x, everything.at[block(3, True)], out_send, out_recv, 4),
                to(x_side, from_y, everything.at[block(3, False)], out_send, out_recv, 5),
            ]
            keep = pltpu.make_async_copy(mine, everything.at[pl.ds(0, rows)], out_send.at[6])
            for copy in copies[:4]:
                copy.start()
            keep.start()
            copies[0].wait_recv()
            copies[4].start()
            copies[1].wait_recv()
            copies[5].start()
            for copy in copies[:2]:
                copy.wait_send()
            for copy in copies[2:]:
                copy.wait()
            keep.wait()

    vmem = pl.BlockSpec(memory_space=pltpu.VMEM)
    shapes = [jax.ShapeDtypeStruct(s, d) for s, d in own]
    if gathered:
        shapes.append(jax.ShapeDtypeStruct((HEADS * rows, width), bf16))
    whole, part_of = ((rows, width), (half, width)) if has else ((STEP, 128), (STEP, 128))
    return pl.pallas_call(
        kernel,
        out_shape=shapes,
        in_specs=[vmem] * (has + len(blocks)),
        out_specs=[vmem] * len(own) + [ANY] * int(gathered),
        scratch_shapes=[pltpu.VMEM(s, bf16) for s in (whole, whole, part_of, part_of, part_of, part_of)]
        + [pltpu.VMEM((rows, width), bf16)]
        + [pltpu.SemaphoreType.DMA((n,)) for n in (6, 6, 7, 6)],
        compiler_params=pltpu.CompilerParams(
            collective_id=cid, has_side_effects=True, vmem_limit_bytes=40 << 20
        ),
    )(*([partial] if has else []), *blocks)


def factor_of(x):
    return lax.rsqrt(jnp.mean(x * x, axis=-1, keepdims=True) + epsilon)


def norm_body(i, at, total, blocks, own, mine):
    tokens, gain = blocks
    x = tokens[at, :].astype(f32)
    mine[at, :] = (x * factor_of(x) * gain[...]).astype(bf16)


def residual_body(i, at, total, blocks, own, mine):
    tokens, gain = blocks
    x = tokens[at, :].astype(f32) + total
    own[0][at, :] = x
    mine[at, :] = (x * factor_of(x) * gain[...]).astype(bf16)


def accumulate(i, ref, product):
    part = product[:8] + product[8:]

    @pl.when(i == 0)
    def _():
        ref[...] = part

    @pl.when(i > 0)
    def _():
        ref[...] += part


def residual_grad_body(i, at, total, blocks, own, mine):
    residual, cotangent, gain = blocks
    x = residual[at, :]
    factor = factor_of(x)
    normed = x * factor
    accumulate(i, own[1], normed * total)
    scaled = total * gain[...]
    grad = cotangent[at, :].astype(f32) + factor * (
        scaled - normed * jnp.mean(normed * scaled, axis=-1, keepdims=True)
    )
    own[0][at, :] = grad
    mine[at, :] = grad.astype(bf16)


def last_body(planes):
    def body(i, at, total, blocks, own, mine):
        tokens, later, gain, residual, *outs = blocks
        x = tokens[at, :].astype(f32)
        factor = factor_of(x)
        normed = x * factor
        accumulate(i, own[1], normed * total)
        scaled = total * gain[...]
        grad = later[at, :] + factor * (
            scaled - normed * jnp.mean(normed * scaled, axis=-1, keepdims=True)
        )
        own[0][at, :] = reorder(grad, planes, True)
        result = residual[at, :]
        for out in outs:
            result = result + out[at, :].astype(f32)
        own[2][at, :] = reorder(result.astype(bf16), planes, True)

    return body


def carry_states(cid, keys, values, gains, planes, reverse):
    sent = bf16 if reverse else f32
    _, slots, size = keys.shape
    half = slots // 2

    def kernel(k_in, v_in, g_in, k_out, v_out, k_all, v_all, g_all, k_pre, v_pre, g_pre, k_run, v_run, g_run,
               k_far, v_far, g_far, k_base, v_base, k_mine, v_mine, s_send, s_recv, z_send, z_recv, b_send, b_recv):
        me = lax.axis_index("seq")
        h = chip_of(me)
        core = lax.rem(me, 2)
        z = lax.div(me, PLANE)
        sibling = me + 1 - 2 * core
        barrier = pltpu.get_barrier_semaphore()
        others = [me + PLANE * (lax.rem(z + k, planes) - z) for k in range(1, planes)]
        for device in (sibling, *others):
            pl.semaphore_signal(barrier, inc=1, device_id=(device,), device_id_type=MESH)
        pl.semaphore_wait(barrier, planes)

        def remote(src, dst, s, r, device):
            return pltpu.make_async_remote_copy(
                src_ref=src, dst_ref=dst, send_sem=s, recv_sem=r, device_id=(device,), device_id_type=MESH
            )

        k_base[...] = jnp.zeros_like(k_base)
        v_base[...] = jnp.zeros_like(v_base)
        copies = []
        for k in range(HEADS):
            chip = chip_on(me, h, k)[1]
            for j, (src, dst) in enumerate(((g_in, g_all), (k_in, k_all), (v_in, v_all))):
                n = 3 * k + j
                copies.append(remote(src.at[k], dst.at[chip, core], s_send.at[n], s_recv.at[n], sibling))
        for copy in copies:
            copy.start()
        for k in range(HEADS):
            chip = chip_on(me, h, k)[1]
            for src, dst in ((g_in, g_all), (k_in, k_all), (v_in, v_all)):
                dst[chip, core] = src[k]
        for copy in copies:
            copy.wait()
        k_run[...] = jnp.zeros_like(k_run)
        v_run[...] = jnp.zeros_like(v_run)
        g_run[...] = jnp.ones_like(g_run)
        order = [(c, d) for c in range(HEADS) for d in range(2)]
        for c, d in reversed(order) if reverse else order:
            k_pre[c, d] = k_run[...]
            v_pre[c, d] = v_run[...]
            g_pre[c, d] = g_run[...]
            gain = g_all[c, d]
            k_run[...] = gain[:, :1] * k_run[...] + k_all[c, d]
            v_run[...] = gain[:, :1] * v_run[...] + v_all[c, d]
            g_run[...] = gain * g_run[...]
        mine = pl.ds(pl.multiple_of(core * half, half), half)
        k_mine[...] = k_run[mine, :].astype(sent)
        v_mine[...] = v_run[mine, :].astype(sent)

        def along(k, go):
            step = -PLANE * k if reverse else PLANE * k
            device = me + step if go else me - step
            return [
                remote(src, dst.at[k - 1], z_send.at[n], z_recv.at[n], device)
                for n, src, dst in (
                    (3 * k - 3, g_run.at[mine], g_far),
                    (3 * k - 2, k_mine, k_far),
                    (3 * k - 1, v_mine, v_far),
                )
            ]

        def ahead(k):
            return z - k >= 0 if reverse else z + k < planes

        def behind(k):
            return z + k < planes if reverse else z - k >= 0

        for k in range(1, planes):
            @pl.when(ahead(k))
            def _(k=k):
                for copy in along(k, True):
                    copy.start()

        for k in reversed(range(1, planes)):
            @pl.when(behind(k))
            def _(k=k):
                for copy in along(k, False):
                    copy.wait_recv()
                gain = g_far[k - 1][:, :1]
                k_base[mine, :] = gain * k_base[mine, :] + k_far[k - 1].astype(f32)
                v_base[mine, :] = gain * v_base[mine, :] + v_far[k - 1].astype(f32)

        copies = [
            remote(k_base.at[mine], k_base.at[mine], b_send.at[0], b_recv.at[0], sibling),
            remote(v_base.at[mine], v_base.at[mine], b_send.at[1], b_recv.at[1], sibling),
        ]
        for copy in copies:
            copy.start()
        for copy in copies:
            copy.wait()
        for k in range(HEADS):
            chip = chip_on(me, h, k)[1]
            gain = g_pre[chip, core][:, :1]
            k_out[k] = gain * k_base[...] + k_pre[chip, core]
            v_out[k] = gain * v_base[...] + v_pre[chip, core]
        for k in range(1, planes):
            @pl.when(ahead(k))
            def _(k=k):
                for copy in along(k, True):
                    copy.wait_send()

    vmem = pl.BlockSpec(memory_space=pltpu.VMEM)
    wide = [pltpu.VMEM((HEADS, 2, slots, n), f32) for n in (size, size, 128)]
    state = [pltpu.VMEM((slots, n), f32) for n in (size, size, 128)]
    far = [pltpu.VMEM((planes - 1, half, n), d) for n, d in ((size, sent), (size, sent), (128, f32))]
    sends = [pltpu.VMEM((half, size), sent)] * 2
    semaphores = [12, 12, 3 * planes - 3, 3 * planes - 3, 2, 2]
    return pl.pallas_call(
        kernel,
        out_shape=[jax.ShapeDtypeStruct(keys.shape, f32)] * 2,
        in_specs=[vmem] * 3,
        out_specs=[vmem] * 2,
        scratch_shapes=wide + wide + state + far + state[:2] + sends
        + [pltpu.SemaphoreType.DMA((n,)) for n in semaphores],
        compiler_params=pltpu.CompilerParams(
            collective_id=cid, has_side_effects=True, vmem_limit_bytes=32 << 20
        ),
    )(keys, values, gains)


def rms_factor(value_rows):
    return lax.rsqrt(jnp.mean(value_rows * value_rows, axis=-1, keepdims=True) + epsilon)


def precise(form, left, right):
    return jnp.einsum(form, left, right, precision=highest, preferred_element_type=f32)


def plain(form, left, right):
    return jnp.einsum(form, left, right, preferred_element_type=f32)


def local(
    tokens,
    cotangent,
    gate_codes,
    lengths,
    mixer_gain,
    query_weight,
    key_weight,
    value_weight,
    head_gain,
    output_weight,
    feed_gain,
    gate_weight,
    up_weight,
    down_weight,
):
    count = lax.axis_size("seq")
    planes = count // PLANE
    me = lax.axis_index("seq")
    z, h, core = me // PLANE, (me // 2) % HEADS, me % 2
    rows, width = tokens.shape
    strip = query_weight.shape[0]
    head_size = width // HEADS
    lines = [
        [p * PLANE + c * 2 + k for p in range(planes) for k in range(2)] for c in range(HEADS)
    ]

    def gather_line(x):
        return lax.all_gather(x, "seq", axis=0, tiled=True, axis_index_groups=lines)

    def scatter_line(x):
        return lax.psum_scatter(
            x, "seq", scatter_dimension=0, tiled=True, axis_index_groups=lines
        )

    def shuffled(x):
        y = x.reshape(*x.shape[:-1], planes, HEADS, 2, strip)
        return jnp.swapaxes(y, -3, -2).reshape(x.shape)

    def restored(x):
        y = x.reshape(*x.shape[:-1], planes, 2, HEADS, strip)
        return jnp.swapaxes(y, -3, -2).reshape(x.shape)

    turns = [
        [(d, d - 2 * (d // 2 % HEADS) + 2 * (d // 2 % HEADS ^ k)) for d in range(count)]
        for k in range(HEADS)
    ]

    def send_on(x, k):
        return lax.ppermute(x, "seq", turns[k])

    def in_chip_order(parts):
        whole = jnp.stack(parts)
        return jnp.stack(
            [lax.dynamic_index_in_dim(whole, j ^ h, keepdims=False) for j in range(HEADS)]
        )

    gains = jnp.stack([mixer_gain, head_gain, feed_gain]).astype(f32)
    gains = jnp.pad(gains, ((0, 5), (0, 128 - strip)))
    codes = gate_codes.reshape(rows, HEADS, SLOTS).swapaxes(0, 1)
    (output_own,) = reordered([output_weight], planes)
    mixer_rows = first_exchange(0, (query_weight, key_weight, value_weight), output_own)
    mixer_line = gather_line(mixer_rows)
    gains_all, codes_all, feed_rows, down_rows = second_exchange(
        1, gains, codes, gate_weight, up_weight, down_weight, count
    )
    feed_weight = gather_line(feed_rows)
    down_line = gather_line(down_rows)
    gain_of = gains_all[:, :3, :strip].swapaxes(0, 1).reshape(3, width)
    gain_one, gain_two = shuffled(gain_of[0])[None], shuffled(gain_of[2])[None]
    head_gain_f = lax.dynamic_slice(gain_of[1], (h * head_size,), (head_size,))

    tokens_own, cotangent_own = reordered([tokens, cotangent], planes)
    (h1,) = plane_stage(2, None, [tokens_own, gain_one], norm_body, [], True)
    h1, cotangent_sent = lax.optimization_barrier((h1, cotangent_own))
    cotangent_parts = [cotangent_own] + [send_on(cotangent_sent, k) for k in (1, 2, 3)]

    decay = jax.nn.log_sigmoid(codes_all.astype(f32) / 256.0)
    block = z * PLANE + 2 * ((h ^ jnp.arange(HEADS))) + core
    first = (block * rows)[:, None]
    position = first + jnp.arange(rows)[None, :]
    order = jnp.arange(lengths.shape[0])
    first_token = jnp.sum(
        jnp.where(order[:, None] > order[None, :], lengths[None, :], 0), axis=1
    )
    seen = jnp.sum(
        jnp.where(
            (first_token[None, None, :] <= position[:, :, None])
            & (first_token[None, None, :] >= first[:, :, None]),
            1,
            0,
        ),
        axis=2,
    )
    places = jnp.arange(rows)
    before = places[:, None] >= places[None, :]
    same = jnp.where(before[None] & (seen[:, :, None] == seen[:, None, :]), 1.0, 0.0).astype(f32)
    fresh = jnp.where(seen == 0, 1.0, 0.0).astype(f32)[:, :, None]
    logsum = precise("ts,bsm->btm", before.astype(f32), decay)
    grow = jnp.exp(logsum)
    back = jnp.exp(-logsum) * -jnp.expm1(decay)
    tail = jnp.where(seen == seen[:, -1:], 1.0, 0.0).astype(f32)[:, :, None]
    weights = grow[:, -1:] * back * tail
    carried = fresh[:, -1] * grow[:, -1]
    carried = jnp.broadcast_to(carried[:, :, None], (HEADS, SLOTS, 128))

    blocked = (HEADS, rows, head_size)
    mixer_weight = mixer_line[:, : 3 * head_size]
    projected = jnp.dot(h1, mixer_weight, preferred_element_type=f32).astype(bf16)
    query = projected[:, :head_size].reshape(blocked)
    key = projected[:, head_size : 2 * head_size].reshape(blocked)
    value = projected[:, 2 * head_size :].reshape(blocked)
    query_f = query.astype(f32)

    key_state, value_state = carry_states(
        3,
        precise("bsm,bsd->bmd", weights, key.astype(f32)),
        precise("bsm,bsd->bmd", weights, value.astype(f32)),
        carried,
        planes,
        False,
    )

    affinity = plain("btd,bsd->bts", query, key) * same
    score = grow * precise("bts,bsm->btm", affinity, back) + grow * fresh * precise(
        "btd,bmd->btm", query_f, key_state
    )
    probs = jax.nn.softmax(score, axis=-1)
    lifted = probs * grow
    mixing = (precise("btm,bsm->bts", lifted, back) * same).astype(bf16)
    entry = lifted * fresh
    slot_out = plain("bts,bsd->btd", mixing, value) + precise("btm,bmd->btd", entry, value_state)
    head_factor = rms_factor(slot_out)
    unit_heads = slot_out * head_factor
    normed_heads = (unit_heads * head_gain_f).astype(bf16).reshape(HEADS * rows, head_size)

    quarter = planes // HEADS
    output_line = mixer_line[:, 3 * head_size :].reshape(planes, 2, HEADS, strip, head_size)
    pieces = [
        lax.dynamic_slice_in_dim(output_line, (h ^ k) * quarter, quarter)
        for k in range(HEADS)
    ]
    pieces = in_chip_order([pieces[0]] + [send_on(pieces[k], k) for k in (1, 2, 3)])
    out_weight = pieces.transpose(1, 0, 2, 4, 3, 5).reshape(head_size, width)
    mixed = jnp.dot(normed_heads, out_weight, preferred_element_type=f32).astype(bf16)
    residual, h2 = plane_stage(
        4, mixed, [tokens_own, gain_two], residual_body, [((rows, width), f32)], True
    )

    h2, *cotangent_parts = lax.optimization_barrier((h2, *cotangent_parts))
    cotangent_all = jnp.concatenate(cotangent_parts)
    part = down_line.shape[1]
    both = jnp.dot(h2, feed_weight, preferred_element_type=f32)
    sigma = jax.nn.sigmoid(both[:, :part])
    hidden = (both[:, :part] * sigma * both[:, part:]).astype(bf16)
    hidden, both = lax.optimization_barrier((hidden, both))
    down_part = plain("td,tf->df", cotangent_all, hidden).astype(bf16)
    down_part, down_line = lax.optimization_barrier((down_part, down_line))
    down_sums = scatter_line(down_part)
    gate, upward = both[:, :part], both[:, part:]
    sigma = jax.nn.sigmoid(gate)
    hidden_grad = jnp.dot(cotangent_all, down_line, preferred_element_type=f32)
    gate_back = (hidden_grad * upward * sigma * (1.0 + gate * (1.0 - sigma))).astype(bf16)
    up_back = (hidden_grad * (gate * sigma)).astype(bf16)
    both_back = jnp.concatenate([gate_back, up_back], axis=1)
    feed_part = plain("td,tf->df", h2, both_back).astype(bf16)
    feed_part, both_back = lax.optimization_barrier((feed_part, both_back))
    feed_sums = scatter_line(feed_part)
    feed_in = plain("tf,df->td", both_back, feed_weight).astype(bf16)
    residual_grad, feed_gain_part, mixed_grad = plane_stage(
        5,
        feed_in,
        [residual, cotangent_own, gain_two],
        residual_grad_body,
        [((rows, width), f32), ((8, width), f32)],
        True,
    )
    mixed_grad, hidden = lax.optimization_barrier((mixed_grad, hidden))
    feed_out = plain("tf,df->td", hidden, down_line).astype(bf16)
    feed_outs = [feed_out[:rows]]
    feed_outs += [send_on(feed_out[k * rows : (k + 1) * rows], k) for k in (1, 2, 3)]

    mixed_grad, down_sums = lax.optimization_barrier((mixed_grad, down_sums))
    heads_grad = plain("td,fd->tf", mixed_grad, out_weight).reshape(blocked)
    head_gain_part = jnp.sum(unit_heads * heads_grad, axis=(0, 1))
    scaled_heads = heads_grad * head_gain_f
    out_back = (
        head_factor
        * (scaled_heads - unit_heads * jnp.mean(unit_heads * scaled_heads, axis=-1, keepdims=True))
    ).astype(bf16)
    out_back_f = out_back.astype(f32)
    mixing_grad = plain("btd,bsd->bts", out_back, value) * same
    local_value = plain("bts,btd->bsd", mixing, out_back)
    lifted_grad = grow * precise("bts,bsm->btm", mixing_grad, back) + grow * fresh * precise(
        "btd,bmd->btm", out_back_f, value_state
    )
    score_grad = probs * (lifted_grad - jnp.sum(probs * lifted_grad, axis=-1, keepdims=True))
    inner_grad = grow * score_grad
    state_grad = inner_grad * fresh
    affinity_grad = (precise("btm,bsm->bts", inner_grad, back) * same).astype(bf16)
    first_key = precise("btm,btd->bmd", state_grad, query_f)
    first_value = precise("btm,btd->bmd", entry, out_back_f)
    first_key, feed_outs = lax.optimization_barrier((first_key, feed_outs))
    later_key, later_value = carry_states(6, first_key, first_value, carried, planes, True)

    query_back = plain("bts,bsd->btd", affinity_grad, key) + precise(
        "btm,bmd->btd", state_grad, key_state
    )
    key_back = plain("bts,btd->bsd", affinity_grad, query) + precise(
        "bsm,bmd->bsd", weights, later_key
    )
    value_back = local_value + precise("bsm,bmd->bsd", weights, later_value)
    backs = jnp.concatenate(
        [
            x.astype(bf16).reshape(HEADS * rows, head_size)
            for x in (query_back, key_back, value_back)
        ],
        axis=1,
    )
    out_part = plain("tf,td->fd", normed_heads, mixed_grad).astype(bf16)
    out_part = out_part.reshape(quarter, HEADS, 2, strip, HEADS, head_size)
    pieces = [
        lax.dynamic_index_in_dim(out_part, h ^ k, 1, keepdims=False) for k in range(HEADS)
    ]
    pieces = in_chip_order([pieces[0]] + [send_on(pieces[k], k) for k in (1, 2, 3)])
    out_part = pieces.transpose(0, 1, 2, 4, 3, 5).reshape(width, head_size)
    mixer_part = plain("td,tf->df", h1, backs).astype(bf16)
    mixer_part = jnp.concatenate([mixer_part, out_part], axis=1)
    mixer_part, feed_sums = lax.optimization_barrier((mixer_part, feed_sums))
    mixer_sums = scatter_line(mixer_part)
    mixer_in = plain("tf,df->td", backs, mixer_weight).astype(bf16)
    input_grad, mixer_gain_part, block_out = plane_stage(
        7,
        mixer_in,
        [tokens_own, residual_grad, gain_one, residual, *feed_outs],
        last_body(planes),
        [((rows, width), f32), ((8, width), f32), ((rows, width), bf16)],
        False,
    )

    (down_grad,) = return_columns(8, down_sums, 1)
    gate_grad, up_grad = return_columns(9, feed_sums, 2)
    query_grad, key_grad, value_grad = return_columns(10, mixer_sums[:, : 3 * head_size], 3)
    out_sums = mixer_sums[:, 3 * head_size :].reshape(HEADS, strip, head_size)
    out_sums = out_sums.swapaxes(0, 1).reshape(strip, width)

    head_whole = lax.dynamic_update_slice(
        jnp.zeros((width,), f32), head_gain_part, (h * head_size,)
    )
    gain_parts = jnp.stack(
        [
            restored(jnp.sum(mixer_gain_part, axis=0)),
            head_whole,
            restored(jnp.sum(feed_gain_part, axis=0)),
        ]
    )
    gain_parts = gain_parts.reshape(3, count, strip).swapaxes(0, 1)
    gain_parts = jnp.pad(gain_parts, ((0, 0), (0, 5), (0, 128 - strip)))
    gain_sums = jnp.sum(swap_all(11, gain_parts, count), axis=0)[:3, :strip]
    return (
        block_out,
        input_grad,
        gain_sums[0],
        query_grad.astype(f32),
        key_grad.astype(f32),
        value_grad.astype(f32),
        gain_sums[1],
        restored(out_sums).astype(f32),
        gain_sums[2],
        gate_grad.astype(f32),
        up_grad.astype(f32),
        down_grad.astype(f32),
    )


def solution(mesh):
    split, line = P("seq", None), P("seq")
    return jax.shard_map(
        local,
        mesh=mesh,
        in_specs=(split, split, split, P(), line, split, split, split, line, split, line, split, split, split),
        out_specs=(split, split, line, split, split, split, line, split, line, split, split, split),
        check_vma=False,
    )
```

```python
import jax
import jax.numpy as jnp
from jax import lax
from jax.experimental import pallas as pl
from jax.experimental.pallas import tpu as pltpu
from jax.sharding import PartitionSpec as P

HEADS = 4
SLOTS = 64
PLANE = 8

epsilon = 1e-06
highest = lax.Precision.HIGHEST
bf16 = jnp.bfloat16
f32 = jnp.float32
MESH = pl.DeviceIdType.MESH
ANY = pl.BlockSpec(memory_space=pl.ANY)


def lasting(us):
    return pl.CostEstimate(flops=0, bytes_accessed=us * 3_400_000, transcendentals=0)


def exchange(cid, us, arrays, outs, moves, plan):
    def kernel(*refs):
        ins = refs[: len(arrays)]
        dsts = refs[len(arrays) : len(arrays) + len(outs)]
        send, recv = refs[len(arrays) + len(outs) :]
        me = lax.axis_index("seq")
        peers, copies = plan(me, ins, dsts)
        barrier = pltpu.get_barrier_semaphore()
        for peer in peers:
            pl.semaphore_signal(barrier, inc=1, device_id=(peer,), device_id_type=MESH)
        pl.semaphore_wait(barrier, len(peers))
        started = []
        for k, (src, dst, device) in enumerate(copies):
            if device is None:
                copy = pltpu.make_async_copy(src, dst, send.at[k])
            else:
                copy = pltpu.make_async_remote_copy(
                    src_ref=src,
                    dst_ref=dst,
                    send_sem=send.at[k],
                    recv_sem=recv.at[k],
                    device_id=(device,),
                    device_id_type=MESH,
                )
            copy.start()
            started.append(copy)
        for copy in started:
            copy.wait()

    return pl.pallas_call(
        kernel,
        out_shape=[jax.ShapeDtypeStruct(s, d) for s, d in outs],
        in_specs=[ANY] * len(arrays),
        out_specs=[ANY] * len(outs),
        scratch_shapes=[
            pltpu.SemaphoreType.DMA((moves,)),
            pltpu.SemaphoreType.DMA((moves,)),
        ],
        compiler_params=pltpu.CompilerParams(collective_id=cid, has_side_effects=True),
        cost_estimate=lasting(us),
    )(*arrays)


def chip_of(me):
    return lax.rem(lax.div(me, 2), HEADS)


def chip_on(me, h, k):
    turn = (k % 2) * (1 - 2 * lax.rem(h, 2)) + (k // 2) * (2 - 4 * lax.div(h, 2))
    return me + 2 * turn, h + turn


def rows_at(ref, block, size):
    return ref.at[pl.ds(pl.multiple_of(block * size, size), size)]


def columns_at(ref, block, size):
    return ref.at[:, pl.ds(pl.multiple_of(block * size, 128), size)]


def first_exchange(cid, weights, output_rows):
    rows, width = weights[0].shape
    part = width // HEADS

    def plan(me, ins, outs):
        h = chip_of(me)
        targets = [chip_on(me, h, k) for k in (2, 1, 3)] + [(None, h)]
        at = pl.ds(pl.multiple_of(h * rows, rows), rows)
        moves = []
        for device, other in targets:
            for j in range(3):
                dst = outs[0].at[at, pl.ds(j * part, part)]
                moves.append((columns_at(ins[j], other, part), dst, device))
        for k in range(HEADS):
            dst = outs[0].at[pl.ds(k * rows, rows), pl.ds(3 * part, part)]
            moves.append((ins[3].at[:, pl.ds(k * part, part)], dst, None))
        return [p for p, _ in targets[:3]], moves

    shape = (HEADS * rows, 4 * part)
    return exchange(cid, 18, [*weights, output_rows], [(shape, bf16)], 16, plan)[0]


def second_exchange(cid, gains, codes, gate, up, down, count):
    rows, width = gate.shape
    part = width // HEADS

    def plan(me, ins, outs):
        h = chip_of(me)
        g_in, c_in = ins[:2]
        everyone = [lax.rem(me + k, count) for k in range(1, count)]
        targets = [chip_on(me, h, k) for k in (1, 2, 3)] + [(None, h)]
        at = pl.ds(pl.multiple_of(h * rows, rows), rows)
        moves = [(g_in, outs[0].at[me], p) for p in everyone] + [(g_in, outs[0].at[me], None)]
        for k, (device, other) in zip((1, 2, 3, 0), targets):
            moves.append((c_in.at[other], outs[1].at[k], device))
        for w, out, column in ((2, 2, 0), (3, 2, part), (4, 3, 0)):
            for device, other in targets:
                dst = outs[out].at[at, pl.ds(column, part)]
                moves.append((columns_at(ins[w], other, part), dst, device))
        return everyone, moves

    return exchange(
        cid,
        36,
        [gains, codes, gate, up, down],
        [
            ((count, *gains.shape), gains.dtype),
            (codes.shape, codes.dtype),
            ((HEADS * rows, 2 * part), bf16),
            ((HEADS * rows, part), bf16),
        ],
        count + 16,
        plan,
    )


def return_columns(cid, x, pieces, part, planes, gains):
    rows = x.shape[0] // HEADS
    last = planes > 0
    count = planes * PLANE

    def kernel(*refs):
        src, refs = refs[0], refs[1:]
        shares, refs = (refs[0], refs[1:]) if last else (None, refs)
        outs, rest = refs[:pieces], refs[pieces:]
        extra, gain_out, rest = (rest[0], rest[1], rest[2:]) if last else (None, None, rest)
        landed, send, recv, gain_in, gain_send, gain_recv = rest
        me = lax.axis_index("seq")
        h = chip_of(me)
        targets = [chip_on(me, h, k) for k in (3, 1, 2)]
        everyone = [lax.rem(me + k, count) for k in range(1, count)]
        peers = everyone if last else [device for device, _ in targets]
        barrier = pltpu.get_barrier_semaphore()
        for device in peers:
            pl.semaphore_signal(barrier, inc=1, device_id=(device,), device_id_type=MESH)
        pl.semaphore_wait(barrier, len(peers))

        def to(device, source, dst, sends, recvs, n):
            return pltpu.make_async_remote_copy(
                src_ref=source, dst_ref=dst, send_sem=sends.at[n], recv_sem=recvs.at[n],
                device_id=(device,), device_id_type=MESH,
            )

        copies = []
        for k, (device, other) in enumerate(targets):
            for j in range(pieces):
                source = src.at[
                    pl.ds(pl.multiple_of(other * rows, rows), rows), pl.ds(j * part, part)
                ]
                copies.append(to(device, source, landed.at[j, h], send, recv, k * pieces + j))
        if last:
            for n, device in enumerate(everyone):
                copies.append(to(device, shares.at[device], gain_in.at[me], gain_send, gain_recv, n))
        for copy in copies:
            copy.start()
        own = pl.ds(pl.multiple_of(h * rows, rows), rows)
        for j in range(pieces):
            landed[j, h] = src[own, pl.ds(j * part, part)]
        if last:
            gain_in[me] = shares[me]
            blocks = [src[pl.ds(k * rows, rows), pl.ds(pieces * part, part)] for k in range(HEADS)]
            extra[...] = reorder(jnp.concatenate(blocks, axis=1).astype(f32), planes, True)
        for copy in copies:
            copy.wait()
        for j in range(pieces):
            for k in range(HEADS):
                outs[j][:, pl.ds(k * part, part)] = landed[j, k].astype(f32)
        if last:
            total = gain_in[0]
            for k in range(1, count):
                total = total + gain_in[k]
            gain_out[...] = total

    vmem = pl.BlockSpec(memory_space=pltpu.VMEM)
    shapes = [(rows, HEADS * part)] * (pieces + int(last)) + [(8, 128)] * int(last)
    return pl.pallas_call(
        kernel,
        out_shape=[jax.ShapeDtypeStruct(shape, f32) for shape in shapes],
        in_specs=[vmem] * (1 + int(last)),
        out_specs=[vmem] * len(shapes),
        scratch_shapes=[
            pltpu.VMEM((pieces, HEADS, rows, part), x.dtype),
            pltpu.SemaphoreType.DMA((3 * pieces,)),
            pltpu.SemaphoreType.DMA((3 * pieces,)),
            pltpu.VMEM((max(count, 1), 8, 128), f32),
            pltpu.SemaphoreType.DMA((max(count, 2),)),
            pltpu.SemaphoreType.DMA((max(count, 2),)),
        ],
        compiler_params=pltpu.CompilerParams(
            collective_id=cid, has_side_effects=True, vmem_limit_bytes=40 << 20
        ),
        cost_estimate=lasting(14),
    )(*([x, gains] if last else [x]))


STEP = 16


def reorder(x, planes, back):
    chips = planes * HEADS
    strip = x.shape[1] // (2 * chips)
    pieces = []
    for i in range(2 * chips):
        n = (i % 2) * chips + i // 2 if back else (i % chips) * 2 + i // chips
        pieces.append(x[:, n * strip : (n + 1) * strip])
    return jnp.concatenate(pieces, axis=1)


def reordered(arrays, planes):
    def kernel(*refs):
        for src, dst in zip(refs[: len(arrays)], refs[len(arrays) :]):

            def step(i, carry, src=src, dst=dst):
                at = pl.ds(pl.multiple_of(i * STEP, STEP), STEP)
                dst[at, :] = reorder(src[at, :], planes, False)
                return carry

            lax.fori_loop(0, src.shape[0] // STEP, step, 0)

    vmem = pl.BlockSpec(memory_space=pltpu.VMEM)
    return pl.pallas_call(
        kernel,
        out_shape=[jax.ShapeDtypeStruct(x.shape, x.dtype) for x in arrays],
        in_specs=[vmem] * len(arrays),
        out_specs=[vmem] * len(arrays),
        compiler_params=pltpu.CompilerParams(vmem_limit_bytes=32 << 20),
    )(*arrays)


def plane_stage(cid, partial, blocks, body, own, gathered, product=None):
    rows, width = blocks[0].shape
    half = rows // 2
    has = int(partial is not None)
    low, high = pl.ds(0, half), pl.ds(half, half)

    def kernel(*refs):
        part = refs[0] if has else None
        block_refs = refs[has : has + len(blocks)]
        rest = refs[has + len(blocks) :]
        factors, rest = (rest[:2], rest[2:]) if product else (None, rest)
        own_refs, rest = rest[: len(own)], rest[len(own) :]
        everything, rest = (rest[0], rest[1:]) if gathered else (None, rest)
        results, rest = (rest[:HEADS], rest[HEADS:]) if product else (None, rest)
        (left, right, load), rest = (rest[:3], rest[3:]) if product else ((None,) * 3, rest)
        by_x, by_y, over_x, over_y, sum_x, sum_y, mine, send, recv, out_send, out_recv = rest
        me = lax.axis_index("seq")
        h = chip_of(me)
        x_side, y_side = chip_on(me, h, 1)[0], chip_on(me, h, 2)[0]
        barrier = pltpu.get_barrier_semaphore()
        for device in (x_side, y_side):
            pl.semaphore_signal(barrier, inc=1, device_id=(device,), device_id_type=MESH)
        pl.semaphore_wait(barrier, 2)

        def to(device, src, dst, sends, recvs, n):
            return pltpu.make_async_remote_copy(
                src_ref=src, dst_ref=dst, send_sem=sends.at[n], recv_sem=recvs.at[n],
                device_id=(device,), device_id_type=MESH,
            )

        def block(k, first):
            return pl.ds(k * rows + (0 if first else half), half)

        loads = []
        if product:
            loads = [
                pltpu.make_async_copy(src, dst, load.at[n])
                for n, (src, dst) in enumerate(zip(factors, (left, right)))
            ]

        def multiply(k):
            if product:
                results[k][...] = lax.dot_general(
                    left[pl.ds(k * rows, rows), :], right[...], (((1,), (1,)), ((), ())),
                    preferred_element_type=f32,
                ).astype(bf16)

        if has:
            copies = [
                to(x_side, part.at[block(3, True)], over_x, send, recv, 0),
                to(y_side, part.at[block(3, False)], over_y, send, recv, 1),
                to(x_side, part.at[block(1, True)], by_x.at[low], send, recv, 2),
                to(y_side, part.at[block(2, False)], by_y.at[high], send, recv, 3),
                to(y_side, sum_y, by_y.at[low], send, recv, 4),
                to(x_side, sum_x, by_x.at[high], send, recv, 5),
            ]
            for copy in copies[:4]:
                copy.start()
            for copy in loads:
                copy.start()
            for copy in loads:
                copy.wait()
            multiply(0)
            copies[0].wait_recv()
            sum_y[...] = (part[block(2, True), :].astype(f32) + over_x[...].astype(f32)).astype(bf16)
            copies[4].start()
            copies[1].wait_recv()
            sum_x[...] = (part[block(1, False), :].astype(f32) + over_y[...].astype(f32)).astype(bf16)
            copies[5].start()
            multiply(1)
            for copy in copies[:2]:
                copy.wait_send()
            for copy in copies[2:]:
                copy.wait()

        def step(i, carry):
            at = pl.ds(pl.multiple_of(i * STEP, STEP), STEP)
            total = None
            if has:
                total = part[at, :].astype(f32) + by_x[at, :].astype(f32) + by_y[at, :].astype(f32)
            body(i, at, total, block_refs, own_refs, mine)
            return carry

        lax.fori_loop(0, rows // STEP, step, 0)
        if gathered:
            from_x, from_y = everything.at[block(1, True)], everything.at[block(2, False)]
            copies = [
                to(x_side, mine.at[low], from_x, out_send, out_recv, 0),
                to(y_side, mine.at[high], from_y, out_send, out_recv, 1),
                to(x_side, mine.at[high], everything.at[block(1, False)], out_send, out_recv, 2),
                to(y_side, mine.at[low], everything.at[block(2, True)], out_send, out_recv, 3),
                to(y_side, from_x, everything.at[block(3, True)], out_send, out_recv, 4),
                to(x_side, from_y, everything.at[block(3, False)], out_send, out_recv, 5),
            ]
            keep = pltpu.make_async_copy(mine, everything.at[pl.ds(0, rows)], out_send.at[6])
            for copy in copies[:4]:
                copy.start()
            keep.start()
            multiply(2)
            copies[0].wait_recv()
            copies[4].start()
            copies[1].wait_recv()
            copies[5].start()
            multiply(3)
            for copy in copies[:2]:
                copy.wait_send()
            for copy in copies[2:]:
                copy.wait()
            keep.wait()

    vmem = pl.BlockSpec(memory_space=pltpu.VMEM)
    shapes = [jax.ShapeDtypeStruct(s, d) for s, d in own]
    if gathered:
        shapes.append(jax.ShapeDtypeStruct((HEADS * rows, width), bf16))
    factors_in, loaded = [], []
    if product:
        shapes += [jax.ShapeDtypeStruct((rows, width), bf16)] * HEADS
        factors_in = list(product)
        loaded = [pltpu.VMEM(x.shape, x.dtype) for x in product] + [pltpu.SemaphoreType.DMA((2,))]
    whole, part_of = ((rows, width), (half, width)) if has else ((STEP, 128), (STEP, 128))
    return pl.pallas_call(
        kernel,
        out_shape=shapes,
        in_specs=[vmem] * (has + len(blocks)) + [ANY] * len(factors_in),
        out_specs=[vmem] * len(own) + [ANY] * int(gathered) + [vmem] * (HEADS if product else 0),
        scratch_shapes=loaded + [pltpu.VMEM(s, bf16) for s in (whole, whole, part_of, part_of, part_of, part_of)]
        + [pltpu.VMEM((rows, width), bf16)]
        + [pltpu.SemaphoreType.DMA((n,)) for n in (6, 6, 7, 6)],
        compiler_params=pltpu.CompilerParams(
            collective_id=cid, has_side_effects=True, vmem_limit_bytes=40 << 20
        ),
        cost_estimate=lasting(25 * has + 25 * int(gathered)),
    )(*([partial] if has else []), *blocks, *factors_in)


def chip_sum(core, left, right, other_left, other_right, extra=None):
    tokens, columns = right.shape
    half = left.shape[1] // 2
    block = min(half, 256)
    steps = half // block
    more = 0 if extra is None else extra.shape[1]
    contract = (((0,), (0,)), ((), ()))
    pieces = 2 if columns % 256 == 0 and columns > 2048 else 1
    size = columns // pieces

    def kernel(which, a, b, c, d, *rest):
        out = rest[-1]
        for n in range(pieces):
            at = pl.ds(n * size, size)
            total = lax.dot_general(a[...], b[:, at], contract, preferred_element_type=f32)
            total += lax.dot_general(c[...], d[:, at], contract, preferred_element_type=f32)
            out[:, at] = total.astype(bf16)
        if more:
            out[:, pl.ds(columns, more)] = rest[0][...]

    whole = pl.BlockSpec((tokens, columns), lambda i, w: (0, 0), pipeline_mode=pl.Buffered(1))
    specs = [
        pl.BlockSpec((tokens, block), lambda i, w: (0, w[0] * steps + i)),
        whole,
        pl.BlockSpec((tokens, block), lambda i, w: (0, i)),
        whole,
    ]
    if more:
        specs.append(pl.BlockSpec((block, more), lambda i, w: (i, 0)))
    return pl.pallas_call(
        kernel,
        out_shape=jax.ShapeDtypeStruct((half, columns + more), bf16),
        grid_spec=pltpu.PrefetchScalarGridSpec(
            num_scalar_prefetch=1,
            grid=(steps,),
            in_specs=specs,
            out_specs=pl.BlockSpec((block, columns + more), lambda i, w: (i, 0)),
        ),
        compiler_params=pltpu.CompilerParams(vmem_limit_bytes=40 << 20),
        cost_estimate=pl.CostEstimate(
            flops=4 * tokens * half * columns,
            bytes_accessed=4 * tokens * (half + columns) + 2 * half * columns,
            transcendentals=0,
        ),
    )(core.reshape(1), left, right, other_left, other_right, *(() if extra is None else (extra,)))


def factor_of(x):
    return lax.rsqrt(jnp.mean(x * x, axis=-1, keepdims=True) + epsilon)


def norm_body(i, at, total, blocks, own, mine):
    tokens, gain = blocks
    x = tokens[at, :].astype(f32)
    mine[at, :] = (x * factor_of(x) * gain[...]).astype(bf16)


def residual_body(i, at, total, blocks, own, mine):
    tokens, gain = blocks
    x = tokens[at, :].astype(f32) + total
    own[0][at, :] = x
    mine[at, :] = (x * factor_of(x) * gain[...]).astype(bf16)


def accumulate(i, ref, product):
    part = product[:8] + product[8:]

    @pl.when(i == 0)
    def _():
        ref[...] = part

    @pl.when(i > 0)
    def _():
        ref[...] += part


def residual_grad_body(i, at, total, blocks, own, mine):
    residual, cotangent, gain = blocks
    x = residual[at, :]
    factor = factor_of(x)
    normed = x * factor
    accumulate(i, own[1], normed * total)
    scaled = total * gain[...]
    grad = cotangent[at, :].astype(f32) + factor * (
        scaled - normed * jnp.mean(normed * scaled, axis=-1, keepdims=True)
    )
    own[0][at, :] = grad
    mine[at, :] = grad.astype(bf16)


def last_body(planes):
    def body(i, at, total, blocks, own, mine):
        tokens, later, gain, residual, *outs = blocks
        x = tokens[at, :].astype(f32)
        factor = factor_of(x)
        normed = x * factor
        accumulate(i, own[1], normed * total)
        scaled = total * gain[...]
        grad = later[at, :] + factor * (
            scaled - normed * jnp.mean(normed * scaled, axis=-1, keepdims=True)
        )
        own[0][at, :] = reorder(grad, planes, True)
        result = residual[at, :]
        for out in outs:
            result = result + out[at, :].astype(f32)
        own[2][at, :] = reorder(result.astype(bf16), planes, True)

    return body


def carry_states(cid, keys, values, gains, planes, reverse, rows_out=None):
    more = int(rows_out is not None)
    sent = bf16 if reverse else f32
    _, slots, size = keys.shape
    half = slots // 2
    quarter, _, strip, _ = rows_out.shape if more else (1, 0, 0, 0)

    def kernel(k_in, v_in, g_in, *refs):
        r_in, refs = (refs[0], refs[1:]) if more else (None, refs)
        k_out, v_out, refs = refs[0], refs[1], refs[2:]
        r_out, refs = (refs[0], refs[1:]) if more else (None, refs)
        r_all, r_send, r_recv, refs = (*refs[:3], refs[3:]) if more else (None, None, None, refs)
        main(k_in, v_in, g_in, k_out, v_out, *refs, r_in=r_in, r_out=r_out, r_all=r_all, r_send=r_send, r_recv=r_recv)

    def main(k_in, v_in, g_in, k_out, v_out, k_all, v_all, g_all, k_pre, v_pre, g_pre, k_run, v_run, g_run,
               k_far, v_far, g_far, k_base, v_base, k_mine, v_mine, s_send, s_recv, z_send, z_recv, b_send, b_recv,
             *, r_in, r_out, r_all, r_send, r_recv):
        me = lax.axis_index("seq")
        h = chip_of(me)
        core = lax.rem(me, 2)
        z = lax.div(me, PLANE)
        sibling = me + 1 - 2 * core
        barrier = pltpu.get_barrier_semaphore()
        others = [me + PLANE * (lax.rem(z + k, planes) - z) for k in range(1, planes)]
        chips = [chip_on(me, h, k) for k in (1, 2, 3)]
        greeted = [sibling, *others] + ([device for device, _ in chips] if more else [])
        for device in greeted:
            pl.semaphore_signal(barrier, inc=1, device_id=(device,), device_id_type=MESH)
        pl.semaphore_wait(barrier, len(greeted))

        def remote(src, dst, s, r, device):
            return pltpu.make_async_remote_copy(
                src_ref=src, dst_ref=dst, send_sem=s, recv_sem=r, device_id=(device,), device_id_type=MESH
            )

        k_base[...] = jnp.zeros_like(k_base)
        v_base[...] = jnp.zeros_like(v_base)
        copies = []
        for k in range(HEADS):
            chip = chip_on(me, h, k)[1]
            for j, (src, dst) in enumerate(((g_in, g_all), (k_in, k_all), (v_in, v_all))):
                n = 3 * k + j
                copies.append(remote(src.at[k], dst.at[chip, core], s_send.at[n], s_recv.at[n], sibling))
        for copy in copies:
            copy.start()
        swaps = []
        if more:
            for n, (device, chip) in enumerate(chips):
                for q in range(quarter):
                    at = quarter * n + q
                    swaps.append(
                        remote(r_in.at[q, chip], r_all.at[h, q], r_send.at[at], r_recv.at[at], device)
                    )
            for swap in swaps:
                swap.start()
            for q in range(quarter):
                r_all[h, q] = r_in[q, h]
        for k in range(HEADS):
            chip = chip_on(me, h, k)[1]
            for src, dst in ((g_in, g_all), (k_in, k_all), (v_in, v_all)):
                dst[chip, core] = src[k]
        for copy in copies:
            copy.wait()
        k_run[...] = jnp.zeros_like(k_run)
        v_run[...] = jnp.zeros_like(v_run)
        g_run[...] = jnp.ones_like(g_run)
        order = [(c, d) for c in range(HEADS) for d in range(2)]
        for c, d in reversed(order) if reverse else order:
            k_pre[c, d] = k_run[...]
            v_pre[c, d] = v_run[...]
            g_pre[c, d] = g_run[...]
            gain = g_all[c, d]
            k_run[...] = gain[:, :1] * k_run[...] + k_all[c, d]
            v_run[...] = gain[:, :1] * v_run[...] + v_all[c, d]
            g_run[...] = gain * g_run[...]
        mine = pl.ds(pl.multiple_of(core * half, half), half)
        k_mine[...] = k_run[mine, :].astype(sent)
        v_mine[...] = v_run[mine, :].astype(sent)

        def along(k, go):
            step = -PLANE * k if reverse else PLANE * k
            device = me + step if go else me - step
            return [
                remote(src, dst.at[k - 1], z_send.at[n], z_recv.at[n], device)
                for n, src, dst in (
                    (3 * k - 3, g_run.at[mine], g_far),
                    (3 * k - 2, k_mine, k_far),
                    (3 * k - 1, v_mine, v_far),
                )
            ]

        def ahead(k):
            return z - k >= 0 if reverse else z + k < planes

        def behind(k):
            return z + k < planes if reverse else z - k >= 0

        for k in range(1, planes):
            @pl.when(ahead(k))
            def _(k=k):
                for copy in along(k, True):
                    copy.start()

        for k in reversed(range(1, planes)):
            @pl.when(behind(k))
            def _(k=k):
                for copy in along(k, False):
                    copy.wait_recv()
                gain = g_far[k - 1][:, :1]
                k_base[mine, :] = gain * k_base[mine, :] + k_far[k - 1].astype(f32)
                v_base[mine, :] = gain * v_base[mine, :] + v_far[k - 1].astype(f32)

        copies = [
            remote(k_base.at[mine], k_base.at[mine], b_send.at[0], b_recv.at[0], sibling),
            remote(v_base.at[mine], v_base.at[mine], b_send.at[1], b_recv.at[1], sibling),
        ]
        for copy in copies:
            copy.start()
        for copy in copies:
            copy.wait()
        for k in range(HEADS):
            chip = chip_on(me, h, k)[1]
            gain = g_pre[chip, core][:, :1]
            k_out[k] = gain * k_base[...] + k_pre[chip, core]
            v_out[k] = gain * v_base[...] + v_pre[chip, core]
        for swap in swaps:
            swap.wait()
        if more:
            for c in range(HEADS):
                for q in range(quarter):
                    for b in range(HEADS):
                        at = ((c * quarter + q) * HEADS + b) * strip
                        r_out[pl.ds(at, strip), :] = r_all[c, q, :, pl.ds(b * size, size)]
        for k in range(1, planes):
            @pl.when(ahead(k))
            def _(k=k):
                for copy in along(k, True):
                    copy.wait_send()

    vmem = pl.BlockSpec(memory_space=pltpu.VMEM)
    wide = [pltpu.VMEM((HEADS, 2, slots, n), f32) for n in (size, size, 128)]
    state = [pltpu.VMEM((slots, n), f32) for n in (size, size, 128)]
    far = [pltpu.VMEM((planes - 1, half, n), d) for n, d in ((size, sent), (size, sent), (128, f32))]
    sends = [pltpu.VMEM((half, size), sent)] * 2
    side = []
    if more:
        side = [pltpu.VMEM((HEADS, quarter, strip, HEADS * size), bf16)]
        side += [pltpu.SemaphoreType.DMA((3 * quarter,))] * 2
    semaphores = [12, 12, 3 * planes - 3, 3 * planes - 3, 2, 2]
    return pl.pallas_call(
        kernel,
        out_shape=[jax.ShapeDtypeStruct(keys.shape, f32)] * 2
        + [jax.ShapeDtypeStruct((HEADS * quarter * HEADS * strip, size), bf16)] * more,
        in_specs=[vmem] * (3 + more),
        out_specs=[vmem] * (2 + more),
        scratch_shapes=side + wide + wide + state + far + state[:2] + sends
        + [pltpu.SemaphoreType.DMA((n,)) for n in semaphores],
        compiler_params=pltpu.CompilerParams(
            collective_id=cid, has_side_effects=True, vmem_limit_bytes=32 << 20
        ),
        cost_estimate=lasting(22),
    )(keys, values, gains, *([rows_out] if more else []))


def rms_factor(value_rows):
    return lax.rsqrt(jnp.mean(value_rows * value_rows, axis=-1, keepdims=True) + epsilon)


def precise(form, left, right):
    return jnp.einsum(form, left, right, precision=highest, preferred_element_type=f32)


def plain(form, left, right):
    return jnp.einsum(form, left, right, preferred_element_type=f32)


def local(
    tokens,
    cotangent,
    gate_codes,
    lengths,
    mixer_gain,
    query_weight,
    key_weight,
    value_weight,
    head_gain,
    output_weight,
    feed_gain,
    gate_weight,
    up_weight,
    down_weight,
):
    count = lax.axis_size("seq")
    planes = count // PLANE
    me = lax.axis_index("seq")
    z, h, core = me // PLANE, (me // 2) % HEADS, me % 2
    rows, width = tokens.shape
    strip = query_weight.shape[0]
    head_size = width // HEADS
    lines = [
        [p * PLANE + c * 2 + k for k in range(2) for p in range(planes)] for c in range(HEADS)
    ]

    def gather_line(x):
        return lax.all_gather(x, "seq", axis=0, tiled=True, axis_index_groups=lines)

    columns = [[p * PLANE + k for p in range(planes)] for k in range(PLANE)]

    def scatter_column(x):
        return lax.psum_scatter(
            x, "seq", scatter_dimension=0, tiled=True, axis_index_groups=columns
        )

    def to_sibling(x):
        return lax.ppermute(x, "seq", [(d, d ^ 1) for d in range(count)])

    def cut(x, side):
        part_width = x.shape[1] // 2
        return lax.dynamic_slice_in_dim(x, (core ^ side) * part_width, part_width, axis=1)


    def shuffled(x):
        y = x.reshape(*x.shape[:-1], planes * HEADS, 2, strip)
        return jnp.swapaxes(y, -3, -2).reshape(x.shape)

    def restored(x):
        y = x.reshape(*x.shape[:-1], 2, planes * HEADS, strip)
        return jnp.swapaxes(y, -3, -2).reshape(x.shape)

    turns = [
        [(d, d - 2 * (d // 2 % HEADS) + 2 * (d // 2 % HEADS ^ k)) for d in range(count)]
        for k in range(HEADS)
    ]

    def send_on(x, k):
        return lax.ppermute(x, "seq", turns[k])

    def in_chip_order(parts):
        whole = jnp.stack(parts)
        return jnp.stack(
            [lax.dynamic_index_in_dim(whole, j ^ h, keepdims=False) for j in range(HEADS)]
        )

    gains = jnp.stack([mixer_gain, head_gain, feed_gain]).astype(f32)
    gains = jnp.pad(gains, ((0, 5), (0, 128 - strip)))
    codes = gate_codes.reshape(rows, HEADS, SLOTS).swapaxes(0, 1)
    (output_own,) = reordered([output_weight], planes)
    mixer_rows = first_exchange(0, (query_weight, key_weight, value_weight), output_own)
    mixer_line = gather_line(mixer_rows)
    gains_all, codes_all, feed_rows, down_rows = second_exchange(
        1, gains, codes, gate_weight, up_weight, down_weight, count
    )
    feed_weight = gather_line(feed_rows)
    down_line = gather_line(down_rows)
    gain_of = gains_all[:, :3, :strip].swapaxes(0, 1).reshape(3, width)
    gain_one, gain_two = shuffled(gain_of[0])[None], shuffled(gain_of[2])[None]
    head_gain_f = lax.dynamic_slice(gain_of[1], (h * head_size,), (head_size,))

    tokens_own, cotangent_own = reordered([tokens, cotangent], planes)
    (h1,) = plane_stage(2, None, [tokens_own, gain_one], norm_body, [], True)
    h1, cotangent_sent = lax.optimization_barrier((h1, cotangent_own))
    h1_other = to_sibling(cut(h1, 1))
    cotangent_parts = [cotangent_own] + [send_on(cotangent_sent, k) for k in (1, 2, 3)]

    decay = jax.nn.log_sigmoid(codes_all.astype(f32) / 256.0)
    block = z * PLANE + 2 * ((h ^ jnp.arange(HEADS))) + core
    first = (block * rows)[:, None]
    position = first + jnp.arange(rows)[None, :]
    order = jnp.arange(lengths.shape[0])
    first_token = jnp.sum(
        jnp.where(order[:, None] > order[None, :], lengths[None, :], 0), axis=1
    )
    seen = jnp.sum(
        jnp.where(
            (first_token[None, None, :] <= position[:, :, None])
            & (first_token[None, None, :] >= first[:, :, None]),
            1,
            0,
        ),
        axis=2,
    )
    places = jnp.arange(rows)
    before = places[:, None] >= places[None, :]
    same = jnp.where(before[None] & (seen[:, :, None] == seen[:, None, :]), 1.0, 0.0).astype(f32)
    fresh = jnp.where(seen == 0, 1.0, 0.0).astype(f32)[:, :, None]
    logsum = precise("ts,bsm->btm", before.astype(f32), decay)
    grow = jnp.exp(logsum)
    back = jnp.exp(-logsum) * -jnp.expm1(decay)
    tail = jnp.where(seen == seen[:, -1:], 1.0, 0.0).astype(f32)[:, :, None]
    weights = grow[:, -1:] * back * tail
    carried = fresh[:, -1] * grow[:, -1]
    carried = jnp.broadcast_to(carried[:, :, None], (HEADS, SLOTS, 128))

    blocked = (HEADS, rows, head_size)
    mixer_weight = mixer_line[:, : 3 * head_size]
    projected = jnp.dot(h1, mixer_weight, preferred_element_type=f32).astype(bf16)
    query = projected[:, :head_size].reshape(blocked)
    key = projected[:, head_size : 2 * head_size].reshape(blocked)
    value = projected[:, 2 * head_size :].reshape(blocked)
    query_f = query.astype(f32)

    key_state, value_state = carry_states(
        3,
        precise("bsm,bsd->bmd", weights, key.astype(f32)),
        precise("bsm,bsd->bmd", weights, value.astype(f32)),
        carried,
        planes,
        False,
    )

    affinity = plain("btd,bsd->bts", query, key) * same
    score = grow * precise("bts,bsm->btm", affinity, back) + grow * fresh * precise(
        "btd,bmd->btm", query_f, key_state
    )
    probs = jax.nn.softmax(score, axis=-1)
    lifted = probs * grow
    mixing = (precise("btm,bsm->bts", lifted, back) * same).astype(bf16)
    entry = lifted * fresh
    slot_out = plain("bts,bsd->btd", mixing, value) + precise("btm,bmd->btd", entry, value_state)
    head_factor = rms_factor(slot_out)
    unit_heads = slot_out * head_factor
    normed_heads = (unit_heads * head_gain_f).astype(bf16).reshape(HEADS * rows, head_size)

    quarter = planes // HEADS
    output_line = mixer_line[:, 3 * head_size :].reshape(2, planes, HEADS, strip, head_size)
    pieces = [
        lax.dynamic_slice_in_dim(output_line, (h ^ k) * quarter, quarter, axis=1)
        for k in range(HEADS)
    ]
    pieces = in_chip_order([pieces[0]] + [send_on(pieces[k], k) for k in (1, 2, 3)])
    out_weight = pieces.transpose(2, 0, 1, 4, 3, 5).reshape(head_size, width)
    mixed = jnp.dot(normed_heads, out_weight, preferred_element_type=f32).astype(bf16)
    residual, h2 = plane_stage(
        4, mixed, [tokens_own, gain_two], residual_body, [((rows, width), f32)], True
    )

    h2, *cotangent_parts = lax.optimization_barrier((h2, *cotangent_parts))
    cotangent_all = jnp.concatenate(cotangent_parts)
    part = down_line.shape[1]
    both = jnp.dot(h2, feed_weight, preferred_element_type=f32)
    sigma = jax.nn.sigmoid(both[:, :part])
    hidden = (both[:, :part] * sigma * both[:, part:]).astype(bf16)
    hidden, both = lax.optimization_barrier((hidden, both))
    down_part = chip_sum(
        core, cotangent_all, hidden, to_sibling(cut(cotangent_all, 1)), to_sibling(hidden)
    )
    down_sums = scatter_column(down_part)
    h2_other = to_sibling(cut(h2, 1))
    (heads_cut,) = reordered([normed_heads], quarter)
    heads_other = to_sibling(cut(heads_cut, 1))
    _, down_line, out_weight, h2_other, heads_other = lax.optimization_barrier(
        (down_part, down_line, out_weight, h2_other, heads_other)
    )
    gate, upward = both[:, :part], both[:, part:]
    sigma = jax.nn.sigmoid(gate)
    hidden_grad = jnp.dot(cotangent_all, down_line, preferred_element_type=f32)
    gate_back = (hidden_grad * upward * sigma * (1.0 + gate * (1.0 - sigma))).astype(bf16)
    up_back = (hidden_grad * (gate * sigma)).astype(bf16)
    both_back = jnp.concatenate([gate_back, up_back], axis=1)
    both_other = to_sibling(both_back)
    feed_in = plain("tf,df->td", both_back, feed_weight).astype(bf16)
    both_other, feed_in = lax.optimization_barrier((both_other, feed_in))
    feed_part = chip_sum(core, h2, both_back, h2_other, both_other)
    feed_part, feed_in = lax.optimization_barrier((feed_part, feed_in))
    feed_sums = scatter_column(feed_part)
    residual_grad, feed_gain_part, mixed_grad, *feed_out = plane_stage(
        5,
        feed_in,
        [residual, cotangent_own, gain_two],
        residual_grad_body,
        [((rows, width), f32), ((8, width), f32)],
        True,
        (hidden, down_line),
    )
    mixed_other = to_sibling(mixed_grad)
    feed_outs = [feed_out[0]] + [send_on(feed_out[k], k) for k in (1, 2, 3)]

    mixed_grad, down_sums = lax.optimization_barrier((mixed_grad, down_sums))
    heads_grad = plain("td,fd->tf", mixed_grad, out_weight).reshape(blocked)
    head_gain_part = jnp.sum(unit_heads * heads_grad, axis=(0, 1))
    scaled_heads = heads_grad * head_gain_f
    out_back = (
        head_factor
        * (scaled_heads - unit_heads * jnp.mean(unit_heads * scaled_heads, axis=-1, keepdims=True))
    ).astype(bf16)
    out_back_f = out_back.astype(f32)
    mixing_grad = plain("btd,bsd->bts", out_back, value) * same
    local_value = plain("bts,btd->bsd", mixing, out_back)
    lifted_grad = grow * precise("bts,bsm->btm", mixing_grad, back) + grow * fresh * precise(
        "btd,bmd->btm", out_back_f, value_state
    )
    score_grad = probs * (lifted_grad - jnp.sum(probs * lifted_grad, axis=-1, keepdims=True))
    inner_grad = grow * score_grad
    state_grad = inner_grad * fresh
    affinity_grad = (precise("btm,bsm->bts", inner_grad, back) * same).astype(bf16)
    first_key = precise("btm,btd->bmd", state_grad, query_f)
    first_value = precise("btm,btd->bmd", entry, out_back_f)
    out_part = chip_sum(core, heads_cut, mixed_grad, heads_other, mixed_other)
    out_part = out_part.reshape(quarter, HEADS, strip, width)
    later_key, later_value, out_part = carry_states(
        6, first_key, first_value, carried, planes, True, out_part
    )
    later_key, feed_outs = lax.optimization_barrier((later_key, feed_outs))

    query_back = plain("bts,bsd->btd", affinity_grad, key) + precise(
        "btm,bmd->btd", state_grad, key_state
    )
    key_back = plain("bts,btd->bsd", affinity_grad, query) + precise(
        "bsm,bmd->bsd", weights, later_key
    )
    value_back = local_value + precise("bsm,bmd->bsd", weights, later_value)
    backs = jnp.concatenate(
        [
            x.astype(bf16).reshape(HEADS * rows, head_size)
            for x in (query_back, key_back, value_back)
        ],
        axis=1,
    )
    backs_other = to_sibling(backs)
    mixer_part = chip_sum(core, h1, backs, h1_other, backs_other, out_part)
    mixer_part, feed_sums, backs = lax.optimization_barrier((mixer_part, feed_sums, backs))
    mixer_sums = scatter_column(mixer_part)
    mixer_in = plain("tf,df->td", backs, mixer_weight).astype(bf16)
    input_grad, mixer_gain_part, block_out = plane_stage(
        7,
        mixer_in,
        [tokens_own, residual_grad, gain_one, residual, *feed_outs],
        last_body(planes),
        [((rows, width), f32), ((8, width), f32), ((rows, width), bf16)],
        False,
    )

    head_whole = lax.dynamic_update_slice(
        jnp.zeros((width,), f32), head_gain_part, (h * head_size,)
    )
    gain_parts = jnp.stack(
        [
            restored(jnp.sum(mixer_gain_part, axis=0)),
            head_whole,
            restored(jnp.sum(feed_gain_part, axis=0)),
        ]
    )
    gain_parts = gain_parts.reshape(3, count, strip).swapaxes(0, 1)
    gain_parts = jnp.pad(gain_parts, ((0, 0), (0, 5), (0, 128 - strip)))
    (down_grad,) = return_columns(8, down_sums, 1, part, 0, None)
    gate_grad, up_grad = return_columns(9, feed_sums, 2, part, 0, None)
    query_grad, key_grad, value_grad, output_grad, gain_sums = return_columns(
        10, mixer_sums, 3, head_size, planes, gain_parts
    )
    gain_sums = gain_sums[:3, :strip]
    return (
        block_out,
        input_grad,
        gain_sums[0],
        query_grad,
        key_grad,
        value_grad,
        gain_sums[1],
        output_grad,
        gain_sums[2],
        gate_grad,
        up_grad,
        down_grad,
    )


def solution(mesh):
    split, line = P("seq", None), P("seq")
    return jax.shard_map(
        local,
        mesh=mesh,
        in_specs=(split, split, split, P(), line, split, split, split, line, split, line, split, split, split),
        out_specs=(split, split, line, split, split, split, line, split, line, split, split, split),
        check_vma=False,
    )
```

```python
import jax
import jax.numpy as jnp
from jax import lax
from jax.experimental import pallas as pl
from jax.experimental.pallas import tpu as pltpu
from jax.sharding import PartitionSpec as P

HEADS = 4
SLOTS = 64
PLANE = 8

epsilon = 1e-06
highest = lax.Precision.HIGHEST
bf16 = jnp.bfloat16
f32 = jnp.float32
MESH = pl.DeviceIdType.MESH
ANY = pl.BlockSpec(memory_space=pl.ANY)


def lasting(us):
    return pl.CostEstimate(flops=0, bytes_accessed=us * 3_400_000, transcendentals=0)


def chip_of(me):
    return lax.rem(lax.div(me, 2), HEADS)


def chip_on(me, h, k):
    turn = (k % 2) * (1 - 2 * lax.rem(h, 2)) + (k // 2) * (2 - 4 * lax.div(h, 2))
    return me + 2 * turn, h + turn


def rows_at(ref, block, size):
    return ref.at[pl.ds(pl.multiple_of(block * size, size), size)]


def columns_at(ref, block, size):
    return ref.at[:, pl.ds(pl.multiple_of(block * size, 128), size)]


def opening(cid, gains, codes, weights, output_rows, feed, tokens, planes):
    strip, width = weights[0].shape
    part = width // HEADS
    feed_part = feed[0].shape[1] // HEADS
    count = planes * PLANE
    hops = planes - 1

    tokens_rows = tokens.shape[0]

    def kernel(g0_in, g1_in, g2_in, codes_in, q_far, k_far, v_far, o_in, gate_far, up_far, down_far, t_in,
               g_out, c_out, line, feed_out, down_out, t_out, gain, t_mine, g_in, c_in, q_in, k_in, v_in,
               gate_in, up_in, down_in, load, t_send, t_recv, own_sem, q_send, q_recv, side_send, side_recv, u_send, u_recv, d_send, d_recv, s_send, s_recv):
        me = lax.axis_index("seq")
        h = chip_of(me)
        core = lax.rem(me, 2)
        z = lax.div(me, PLANE)
        sibling = me + 1 - 2 * core
        chips = [(None, h)] + [chip_on(me, h, k) for k in (1, 2, 3)]
        everyone = [lax.rem(me + k, count) for k in range(1, count)]
        far = (q_far, k_far, v_far, gate_far, up_far, down_far)
        near = (q_in, k_in, v_in, gate_in, up_in, down_in)
        loads = [pltpu.make_async_copy(a, b, load.at[n]) for n, (a, b) in enumerate(zip(far, near))]
        for copy in loads:
            copy.start()
        barrier = pltpu.get_barrier_semaphore()
        for device in everyone:
            pl.semaphore_signal(barrier, inc=1, device_id=(device,), device_id_type=MESH)
        g_in[...] = jnp.zeros_like(g_in)
        for n, ref in enumerate((g0_in, g1_in, g2_in)):
            g_in[n : n + 1, 0:strip] = ref[...].astype(f32)
        for k in range(HEADS):
            c_in[k] = codes_in[:, pl.ds(k * SLOTS, SLOTS)]
        for copy in loads[:3]:
            copy.wait()
        pl.semaphore_wait(barrier, count - 1)

        def remote(src, dst, s, r, device):
            return pltpu.make_async_remote_copy(
                src_ref=src, dst_ref=dst, send_sem=s, recv_sem=r, device_id=(device,), device_id_type=MESH
            )

        def row(plane, chip):
            return pl.ds(pl.multiple_of(((core * planes + plane) * HEADS + chip) * strip, strip), strip)

        def unit(plane, k):
            return line.at[row(plane, chips[k][1])]

        def up(d, k):
            n = (d - 1) * HEADS + k
            return remote(unit(z - d + 1, k), unit(z - d + 1, k), u_send.at[n], u_recv.at[n], me + PLANE)

        def down(d, k):
            n = (d - 1) * HEADS + k
            return remote(unit(z + d - 1, k), unit(z + d - 1, k), d_send.at[n], d_recv.at[n], me - PLANE)

        def across(plane, k):
            n = plane * HEADS + k
            return remote(unit(plane, k), unit(plane, k), s_send.at[n], s_recv.at[n], sibling)

        def pass_on(k):
            @pl.when(z + 1 < planes)
            def _():
                up(1, k).start()

            @pl.when(z >= 1)
            def _():
                down(1, k).start()

            across(z, k).start()

        projections = []
        for k in (3, 1, 2):
            device, chip = chips[k]
            for j, w in enumerate((q_in, k_in, v_in)):
                n = 3 * (k - 1) + j
                dst = line.at[row(z, h), pl.ds(j * part, part)]
                projections.append((k, remote(columns_at(w, chip, part), dst, q_send.at[n], q_recv.at[n], device)))
        own = [
            pltpu.make_async_copy(
                columns_at(w, h, part), line.at[row(z, h), pl.ds(j * part, part)], own_sem.at[j]
            )
            for j, w in enumerate((q_in, k_in, v_in))
        ]
        for _, copy in projections:
            copy.start()
        for copy in own:
            copy.start()
        turned = reorder(o_in[...], planes, False)
        for k in range(HEADS):
            line[row(z, k), pl.ds(3 * part, part)] = turned[:, k * part : (k + 1) * part]
        for copy in own:
            copy.wait()
        pass_on(0)

        shared = [(g_in, g_out.at[me], device) for device in everyone]
        sides = [(c_in.at[chip], c_out.at[k], device) for k, (device, chip) in list(enumerate(chips))[1:]]
        at = pl.ds(pl.multiple_of(h * strip, strip), strip)
        for src, out, column in ((gate_in, feed_out, 0), (up_in, feed_out, feed_part), (down_in, down_out, 0)):
            for device, chip in chips[1:] + chips[:1]:
                dst = out.at[at, pl.ds(column, feed_part)]
                sides.append((columns_at(src, chip, feed_part), dst, device))
        sides.append((c_in.at[h], c_out.at[0], None))
        begun = []

        def begin(listed):
            for src, dst, device in listed:
                n = len(begun)
                if device is None:
                    copy = pltpu.make_async_copy(src, dst, side_send.at[n])
                else:
                    copy = remote(src, dst, side_send.at[n], side_recv.at[n], device)
                copy.start()
                begun.append(copy)

        begin(shared)
        g_out[me] = g_in[...]
        for k in (1, 2, 3):
            for other, copy in projections:
                if other == k:
                    copy.wait_recv()
            pass_on(k)
        for copy in begun:
            copy.wait()
        shares = begun[:]
        gain[...] = jnp.concatenate(
            [
                g_out[(p * PLANE + c * 2 + k), 0:1, 0:strip]
                for k in range(2)
                for p in range(planes)
                for c in range(HEADS)
            ],
            axis=1,
        )

        def step(i, carry):
            at = pl.ds(pl.multiple_of(i * STEP, STEP), STEP)
            x = t_in[at, :].astype(f32)
            t_mine[at, :] = (reorder(x * factor_of(x), planes, False) * gain[...]).astype(bf16)
            return carry

        half = tokens_rows // 2
        low, high = pl.ds(0, half), pl.ds(half, half)
        x_side, y_side = chips[1][0], chips[2][0]

        def spread_out(mine, everything, sends, recvs):
            def block(k, first):
                return everything.at[pl.ds(k * tokens_rows + (0 if first else half), half)]

            copies = [
                remote(mine.at[low], block(1, True), sends.at[0], recvs.at[0], x_side),
                remote(mine.at[high], block(2, False), sends.at[1], recvs.at[1], y_side),
                remote(mine.at[high], block(1, False), sends.at[2], recvs.at[2], x_side),
                remote(mine.at[low], block(2, True), sends.at[3], recvs.at[3], y_side),
                remote(block(1, True), block(3, True), sends.at[4], recvs.at[4], y_side),
                remote(block(2, False), block(3, False), sends.at[5], recvs.at[5], x_side),
            ]
            keep = pltpu.make_async_copy(mine, everything.at[pl.ds(0, tokens_rows)], sends.at[6])
            for copy in copies[:4]:
                copy.start()
            keep.start()
            return copies, keep

        def relay(copies):
            copies[0].wait_recv()
            copies[4].start()
            copies[1].wait_recv()
            copies[5].start()

        def finish(copies, keep):
            for copy in copies[:2]:
                copy.wait_send()
            for copy in copies[2:]:
                copy.wait()
            keep.wait()

        lax.fori_loop(0, tokens_rows // STEP, step, 0)
        spread_t = spread_out(t_mine, t_out, t_send, t_recv)
        for copy in loads[3:]:
            copy.wait()
        begin(sides)
        for d in range(1, planes):
            for k in range(HEADS):

                @pl.when(z - d >= 0)
                def _(d=d, k=k):
                    up(d, k).wait_recv()

                    @pl.when(z + 1 < planes)
                    def _():
                        up(d + 1, k).start()

                    across(z - d, k).start()

                @pl.when(z + d < planes)
                def _(d=d, k=k):
                    down(d, k).wait_recv()

                    @pl.when(z >= 1)
                    def _():
                        down(d + 1, k).start()

                    across(z + d, k).start()

            if d == 1:
                relay(spread_t[0])
        for _, copy in projections:
            copy.wait_send()
        finish(*spread_t)
        for copy in begun[len(shares) :]:
            copy.wait()
        for d in range(1, planes):
            for k in range(HEADS):

                @pl.when((z - d + 1 >= 0) & (z + 1 < planes))
                def _(d=d, k=k):
                    up(d, k).wait_send()

                @pl.when((z + d - 1 < planes) & (z >= 1))
                def _(d=d, k=k):
                    down(d, k).wait_send()

        for plane in range(planes):
            for k in range(HEADS):
                across(plane, k).wait()

    sides = count + 4 + 12
    vmem = pl.BlockSpec(memory_space=pltpu.VMEM)
    sizes = (6, 7, 6, 3, 9, 9, sides, sides) + (hops * HEADS,) * 4 + (planes * HEADS,) * 2
    shares = jax.ShapeDtypeStruct((count, 8, 128), f32)
    logits = jax.ShapeDtypeStruct((HEADS, tokens_rows, SLOTS), codes.dtype)
    return pl.pallas_call(
        kernel,
        out_shape=[
            shares,
            logits,
            jax.ShapeDtypeStruct((count * strip, 4 * part), bf16),
            jax.ShapeDtypeStruct((HEADS * strip, 2 * feed_part), bf16),
            jax.ShapeDtypeStruct((HEADS * strip, feed_part), bf16),
            jax.ShapeDtypeStruct((HEADS * tokens_rows, width), bf16),
        ],
        in_specs=[vmem] * 4 + [ANY] * 3 + [vmem] + [ANY] * 3 + [vmem],
        out_specs=[vmem] * 5 + [ANY],
        scratch_shapes=[
            pltpu.VMEM((1, width), f32),
            pltpu.VMEM(tokens.shape, bf16),
            pltpu.VMEM((8, 128), f32),
            pltpu.VMEM((HEADS, tokens_rows, SLOTS), codes.dtype),
        ]
        + [pltpu.VMEM(x.shape, bf16) for x in (*weights, *feed)]
        + [pltpu.SemaphoreType.DMA((n,)) for n in sizes],
        compiler_params=pltpu.CompilerParams(
            collective_id=cid, has_side_effects=True, vmem_limit_bytes=58 << 20
        ),
        cost_estimate=lasting(85),
    )(*(g[None] for g in gains), codes, *weights, output_rows, *feed, tokens)


def return_columns(cid, x, pieces, part, planes, gains=None, own_rows=False):
    rows = x.shape[0] // HEADS
    shared = gains is not None
    count = planes * PLANE

    def kernel(*refs):
        src, refs = refs[0], refs[1:]
        shares, refs = (refs[0], refs[1:]) if shared else (None, refs)
        outs, refs = refs[:pieces], refs[pieces:]
        extra, refs = (refs[0], refs[1:]) if own_rows else (None, refs)
        gain_out, refs = (refs[0], refs[1:]) if shared else (None, refs)
        landed, send, recv, gain_in, gain_send, gain_recv = refs
        me = lax.axis_index("seq")
        h = chip_of(me)
        targets = [chip_on(me, h, k) for k in (3, 1, 2)]
        everyone = [lax.rem(me + k, count) for k in range(1, count)]
        peers = everyone if shared else [device for device, _ in targets]
        barrier = pltpu.get_barrier_semaphore()
        for device in peers:
            pl.semaphore_signal(barrier, inc=1, device_id=(device,), device_id_type=MESH)
        pl.semaphore_wait(barrier, len(peers))

        def to(device, source, dst, sends, recvs, n):
            return pltpu.make_async_remote_copy(
                src_ref=source, dst_ref=dst, send_sem=sends.at[n], recv_sem=recvs.at[n],
                device_id=(device,), device_id_type=MESH,
            )

        def place(j):
            return landed.at[j, h] if own_rows else columns_at(outs[j], h, part)

        copies = []
        for k, (device, other) in enumerate(targets):
            for j in range(pieces):
                source = src.at[
                    pl.ds(pl.multiple_of(other * rows, rows), rows), pl.ds(j * part, part)
                ]
                copies.append(to(device, source, place(j), send, recv, k * pieces + j))
        if shared:
            for n, device in enumerate(everyone):
                copies.append(to(device, shares.at[device], gain_in.at[me], gain_send, gain_recv, n))
        own = pl.ds(pl.multiple_of(h * rows, rows), rows)
        for j in range(pieces):
            copies.append(
                pltpu.make_async_copy(src.at[own, pl.ds(j * part, part)], place(j), send.at[3 * pieces + j])
            )
        for copy in copies:
            copy.start()
        if shared:
            gain_in[me] = shares[me]
        if own_rows:
            blocks = [src[pl.ds(k * rows, rows), pl.ds(pieces * part, part)] for k in range(HEADS)]
            extra[...] = reorder(jnp.concatenate(blocks, axis=1).astype(f32), planes, True)
        for copy in copies:
            copy.wait()
        if own_rows:
            for j in range(pieces):
                for k in range(HEADS):
                    outs[j][:, pl.ds(k * part, part)] = landed[j, k].astype(f32)
        if shared:
            total = gain_in[0]
            for k in range(1, count):
                total = total + gain_in[k]
            gain_out[...] = total

    vmem = pl.BlockSpec(memory_space=pltpu.VMEM)
    kind = f32 if own_rows else bf16
    shapes = [jax.ShapeDtypeStruct((rows, HEADS * part), kind)] * (pieces + int(own_rows))
    shapes += [jax.ShapeDtypeStruct((8, 128), f32)] * int(shared)
    return pl.pallas_call(
        kernel,
        out_shape=shapes,
        in_specs=[vmem] * (1 + int(shared)),
        out_specs=[vmem] * len(shapes),
        scratch_shapes=[
            pltpu.VMEM((pieces, HEADS, rows, part) if own_rows else (1, 1, 16, 128), x.dtype),
            pltpu.SemaphoreType.DMA((4 * pieces,)),
            pltpu.SemaphoreType.DMA((3 * pieces,)),
            pltpu.VMEM((count if shared else 1, 8, 128), f32),
            pltpu.SemaphoreType.DMA((count if shared else 1,)),
            pltpu.SemaphoreType.DMA((count if shared else 1,)),
        ],
        compiler_params=pltpu.CompilerParams(
            collective_id=cid, has_side_effects=True, vmem_limit_bytes=40 << 20
        ),
        cost_estimate=lasting(14),
    )(*([x, gains] if shared else [x]))


def finished(narrow, others):
    arrays = [*narrow, *others]
    kinds = [f32] * len(narrow) + [x.dtype for x in others]

    def kernel(*refs):
        for src, dst in zip(refs[: len(arrays)], refs[len(arrays) :]):
            dst[...] = src[...].astype(dst.dtype)

    specs = [pl.BlockSpec((x.shape[0] // 2, x.shape[1]), lambda i: (i, 0)) for x in arrays]
    if any(x.shape[0] % 32 for x in arrays):
        specs = [pl.BlockSpec(x.shape, lambda i: (0, 0)) for x in arrays]
    return pl.pallas_call(
        kernel,
        out_shape=[jax.ShapeDtypeStruct(x.shape, kind) for x, kind in zip(arrays, kinds)],
        grid=(2 if specs[0].block_shape[0] < arrays[0].shape[0] else 1,),
        in_specs=specs,
        out_specs=specs,
        compiler_params=pltpu.CompilerParams(vmem_limit_bytes=40 << 20),
        cost_estimate=lasting(3),
    )(*arrays)


STEP = 16


def reorder(x, planes, back):
    chips = planes * HEADS
    strip = x.shape[1] // (2 * chips)
    pieces = []
    for i in range(2 * chips):
        n = (i % 2) * chips + i // 2 if back else (i % chips) * 2 + i // chips
        pieces.append(x[:, n * strip : (n + 1) * strip])
    return jnp.concatenate(pieces, axis=1)


def reordered(arrays, planes):
    def kernel(*refs):
        for src, dst in zip(refs[: len(arrays)], refs[len(arrays) :]):

            def step(i, carry, src=src, dst=dst):
                at = pl.ds(pl.multiple_of(i * STEP, STEP), STEP)
                dst[at, :] = reorder(src[at, :], planes, False)
                return carry

            lax.fori_loop(0, src.shape[0] // STEP, step, 0)

    vmem = pl.BlockSpec(memory_space=pltpu.VMEM)
    return pl.pallas_call(
        kernel,
        out_shape=[jax.ShapeDtypeStruct(x.shape, x.dtype) for x in arrays],
        in_specs=[vmem] * len(arrays),
        out_specs=[vmem] * len(arrays),
        compiler_params=pltpu.CompilerParams(vmem_limit_bytes=32 << 20),
    )(*arrays)


def plane_stage(cid, partial, blocks, body, own, gathered, product=None):
    rows, width = blocks[0].shape
    half = rows // 2
    has = int(partial is not None)
    low, high = pl.ds(0, half), pl.ds(half, half)

    def kernel(*refs):
        part = refs[0] if has else None
        block_refs = refs[has : has + len(blocks)]
        rest = refs[has + len(blocks) :]
        factors, rest = (rest[:2], rest[2:]) if product else (None, rest)
        own_refs, rest = rest[: len(own)], rest[len(own) :]
        everything, rest = (rest[0], rest[1:]) if gathered else (None, rest)
        results, rest = (rest[:HEADS], rest[HEADS:]) if product else (None, rest)
        (left, right, load), rest = (rest[:3], rest[3:]) if product else ((None,) * 3, rest)
        by_x, by_y, over_x, over_y, sum_x, sum_y, mine, send, recv, out_send, out_recv = rest
        me = lax.axis_index("seq")
        h = chip_of(me)
        x_side, y_side = chip_on(me, h, 1)[0], chip_on(me, h, 2)[0]
        barrier = pltpu.get_barrier_semaphore()
        for device in (x_side, y_side):
            pl.semaphore_signal(barrier, inc=1, device_id=(device,), device_id_type=MESH)
        pl.semaphore_wait(barrier, 2)

        def to(device, src, dst, sends, recvs, n):
            return pltpu.make_async_remote_copy(
                src_ref=src, dst_ref=dst, send_sem=sends.at[n], recv_sem=recvs.at[n],
                device_id=(device,), device_id_type=MESH,
            )

        def block(k, first):
            return pl.ds(k * rows + (0 if first else half), half)

        loads = []
        if product:
            loads = [
                pltpu.make_async_copy(src, dst, load.at[n])
                for n, (src, dst) in enumerate(zip(factors, (left, right)))
            ]

        def multiply(k):
            if product:
                results[k][...] = lax.dot_general(
                    left[pl.ds(k * rows, rows), :], right[...], (((1,), (1,)), ((), ())),
                    preferred_element_type=f32,
                ).astype(bf16)

        if has:
            copies = [
                to(x_side, part.at[block(3, True)], over_x, send, recv, 0),
                to(y_side, part.at[block(3, False)], over_y, send, recv, 1),
                to(x_side, part.at[block(1, True)], by_x.at[low], send, recv, 2),
                to(y_side, part.at[block(2, False)], by_y.at[high], send, recv, 3),
                to(y_side, sum_y, by_y.at[low], send, recv, 4),
                to(x_side, sum_x, by_x.at[high], send, recv, 5),
            ]
            for copy in copies[:4]:
                copy.start()
            for copy in loads:
                copy.start()
            for copy in loads:
                copy.wait()
            multiply(0)
            copies[0].wait_recv()
            sum_y[...] = (part[block(2, True), :].astype(f32) + over_x[...].astype(f32)).astype(bf16)
            copies[4].start()
            copies[1].wait_recv()
            sum_x[...] = (part[block(1, False), :].astype(f32) + over_y[...].astype(f32)).astype(bf16)
            copies[5].start()
            multiply(1)
            for copy in copies[:2]:
                copy.wait_send()
            for copy in copies[2:]:
                copy.wait()

        def step(i, carry):
            at = pl.ds(pl.multiple_of(i * STEP, STEP), STEP)
            total = None
            if has:
                total = part[at, :].astype(f32) + by_x[at, :].astype(f32) + by_y[at, :].astype(f32)
            body(i, at, total, block_refs, own_refs, mine)
            return carry

        lax.fori_loop(0, rows // STEP, step, 0)
        if gathered:
            from_x, from_y = everything.at[block(1, True)], everything.at[block(2, False)]
            copies = [
                to(x_side, mine.at[low], from_x, out_send, out_recv, 0),
                to(y_side, mine.at[high], from_y, out_send, out_recv, 1),
                to(x_side, mine.at[high], everything.at[block(1, False)], out_send, out_recv, 2),
                to(y_side, mine.at[low], everything.at[block(2, True)], out_send, out_recv, 3),
                to(y_side, from_x, everything.at[block(3, True)], out_send, out_recv, 4),
                to(x_side, from_y, everything.at[block(3, False)], out_send, out_recv, 5),
            ]
            keep = pltpu.make_async_copy(mine, everything.at[pl.ds(0, rows)], out_send.at[6])
            for copy in copies[:4]:
                copy.start()
            keep.start()
            multiply(2)
            copies[0].wait_recv()
            copies[4].start()
            copies[1].wait_recv()
            copies[5].start()
            multiply(3)
            for copy in copies[:2]:
                copy.wait_send()
            for copy in copies[2:]:
                copy.wait()
            keep.wait()

    vmem = pl.BlockSpec(memory_space=pltpu.VMEM)
    shapes = [jax.ShapeDtypeStruct(s, d) for s, d in own]
    if gathered:
        shapes.append(jax.ShapeDtypeStruct((HEADS * rows, width), bf16))
    factors_in, loaded = [], []
    if product:
        shapes += [jax.ShapeDtypeStruct((rows, width), bf16)] * HEADS
        factors_in = list(product)
        loaded = [pltpu.VMEM(x.shape, x.dtype) for x in product] + [pltpu.SemaphoreType.DMA((2,))]
    whole, part_of = ((rows, width), (half, width)) if has else ((STEP, 128), (STEP, 128))
    return pl.pallas_call(
        kernel,
        out_shape=shapes,
        in_specs=[vmem] * (has + len(blocks)) + [ANY] * len(factors_in),
        out_specs=[vmem] * len(own) + [ANY] * int(gathered) + [vmem] * (HEADS if product else 0),
        scratch_shapes=loaded + [pltpu.VMEM(s, bf16) for s in (whole, whole, part_of, part_of, part_of, part_of)]
        + [pltpu.VMEM((rows, width), bf16)]
        + [pltpu.SemaphoreType.DMA((n,)) for n in (6, 6, 7, 6)],
        compiler_params=pltpu.CompilerParams(
            collective_id=cid, has_side_effects=True, vmem_limit_bytes=40 << 20
        ),
        cost_estimate=lasting(25 * has + 25 * int(gathered)),
    )(*([partial] if has else []), *blocks, *factors_in)


def chip_sum(core, left, right, other_left, other_right, extra=None):
    tokens, columns = right.shape
    half = left.shape[1] // 2
    block = min(half, 256)
    steps = half // block
    more = 0 if extra is None else extra.shape[1]
    contract = (((0,), (0,)), ((), ()))
    pieces = 2 if columns % 256 == 0 and columns > 2048 else 1
    size = columns // pieces

    def kernel(which, a, b, c, d, *rest):
        out = rest[-1]
        for n in range(pieces):
            at = pl.ds(n * size, size)
            total = lax.dot_general(a[...], b[:, at], contract, preferred_element_type=f32)
            total += lax.dot_general(c[...], d[:, at], contract, preferred_element_type=f32)
            out[:, at] = total.astype(bf16)
        if more:
            out[:, pl.ds(columns, more)] = rest[0][...]

    whole = pl.BlockSpec((tokens, columns), lambda i, w: (0, 0), pipeline_mode=pl.Buffered(1))
    specs = [
        pl.BlockSpec((tokens, block), lambda i, w: (0, w[0] * steps + i)),
        whole,
        pl.BlockSpec((tokens, block), lambda i, w: (0, i)),
        whole,
    ]
    if more:
        specs.append(pl.BlockSpec((block, more), lambda i, w: (i, 0)))
    return pl.pallas_call(
        kernel,
        out_shape=jax.ShapeDtypeStruct((half, columns + more), bf16),
        grid_spec=pltpu.PrefetchScalarGridSpec(
            num_scalar_prefetch=1,
            grid=(steps,),
            in_specs=specs,
            out_specs=pl.BlockSpec((block, columns + more), lambda i, w: (i, 0)),
        ),
        compiler_params=pltpu.CompilerParams(vmem_limit_bytes=40 << 20),
        cost_estimate=pl.CostEstimate(
            flops=4 * tokens * half * columns,
            bytes_accessed=4 * tokens * (half + columns) + 2 * half * columns,
            transcendentals=0,
        ),
    )(core.reshape(1), left, right, other_left, other_right, *(() if extra is None else (extra,)))


def factor_of(x):
    return lax.rsqrt(jnp.mean(x * x, axis=-1, keepdims=True) + epsilon)


def residual_body(i, at, total, blocks, own, mine):
    tokens, gain = blocks
    x = tokens[at, :].astype(f32) + total
    own[0][at, :] = x
    mine[at, :] = (x * factor_of(x) * gain[...]).astype(bf16)


def accumulate(i, ref, product):
    part = product[:8] + product[8:]

    @pl.when(i == 0)
    def _():
        ref[...] = part

    @pl.when(i > 0)
    def _():
        ref[...] += part


def residual_grad_body(i, at, total, blocks, own, mine):
    residual, cotangent, gain = blocks
    x = residual[at, :]
    factor = factor_of(x)
    normed = x * factor
    accumulate(i, own[1], normed * total)
    scaled = total * gain[...]
    grad = cotangent[at, :].astype(f32) + factor * (
        scaled - normed * jnp.mean(normed * scaled, axis=-1, keepdims=True)
    )
    own[0][at, :] = grad
    mine[at, :] = grad.astype(bf16)


def last_body(planes):
    def body(i, at, total, blocks, own, mine):
        tokens, later, gain, residual, *outs = blocks
        x = tokens[at, :].astype(f32)
        factor = factor_of(x)
        normed = x * factor
        accumulate(i, own[1], normed * total)
        scaled = total * gain[...]
        grad = later[at, :] + factor * (
            scaled - normed * jnp.mean(normed * scaled, axis=-1, keepdims=True)
        )
        own[0][at, :] = reorder(grad, planes, True)
        result = residual[at, :]
        for out in outs:
            result = result + out[at, :].astype(f32)
        own[2][at, :] = reorder(result.astype(bf16), planes, True)

    return body


def carry_states(cid, keys, values, gains, planes, reverse, rows_out=None, line=None):
    lined = line is not None
    more = int(rows_out is not None or lined)
    sent = bf16 if reverse else f32
    _, slots, size = keys.shape
    half = slots // 2
    if lined:
        quarter, strip = planes // HEADS, line.shape[0] // (planes * PLANE)
        landing, result = (HEADS, 2 * quarter, HEADS * strip, size), (size, HEADS * size)
        links = 2 * quarter
    elif more:
        quarter, _, strip, _ = rows_out.shape
        landing, result = (HEADS, quarter, strip, HEADS * size), (HEADS * quarter * HEADS * strip, size)
        links = quarter

    def kernel(k_in, v_in, g_in, *refs):
        r_in, refs = (refs[0], refs[1:]) if more else (None, refs)
        k_out, v_out, refs = refs[0], refs[1], refs[2:]
        r_out, refs = (refs[0], refs[1:]) if more else (None, refs)
        r_all, r_send, r_recv, refs = (*refs[:3], refs[3:]) if more else (None, None, None, refs)
        main(k_in, v_in, g_in, k_out, v_out, *refs, r_in=r_in, r_out=r_out, r_all=r_all, r_send=r_send, r_recv=r_recv)

    def main(k_in, v_in, g_in, k_out, v_out, k_all, v_all, g_all, k_pre, v_pre, g_pre, k_run, v_run, g_run,
               k_far, v_far, g_far, k_base, v_base, k_mine, v_mine, s_send, s_recv, z_send, z_recv, b_send, b_recv,
             *, r_in, r_out, r_all, r_send, r_recv):
        me = lax.axis_index("seq")
        h = chip_of(me)
        core = lax.rem(me, 2)
        z = lax.div(me, PLANE)
        sibling = me + 1 - 2 * core
        barrier = pltpu.get_barrier_semaphore()
        others = [me + PLANE * (lax.rem(z + k, planes) - z) for k in range(1, planes)]
        chips = [chip_on(me, h, k) for k in (1, 2, 3)]
        greeted = [sibling, *others] + ([device for device, _ in chips] if more else [])
        for device in greeted:
            pl.semaphore_signal(barrier, inc=1, device_id=(device,), device_id_type=MESH)
        pl.semaphore_wait(barrier, len(greeted))

        def remote(src, dst, s, r, device):
            return pltpu.make_async_remote_copy(
                src_ref=src, dst_ref=dst, send_sem=s, recv_sem=r, device_id=(device,), device_id_type=MESH
            )

        k_base[...] = jnp.zeros_like(k_base)
        v_base[...] = jnp.zeros_like(v_base)
        copies = []
        for k in range(HEADS):
            chip = chip_on(me, h, k)[1]
            for j, (src, dst) in enumerate(((g_in, g_all), (k_in, k_all), (v_in, v_all))):
                n = 3 * k + j
                copies.append(remote(src.at[k], dst.at[chip, core], s_send.at[n], s_recv.at[n], sibling))
        for copy in copies:
            copy.start()
        swaps = []

        def sent_rows(chip, n):
            if not lined:
                return r_in.at[n, chip]
            at = ((n // quarter * planes) + chip * quarter + n % quarter) * HEADS * strip
            return r_in.at[pl.ds(pl.multiple_of(at, HEADS * strip), HEADS * strip), pl.ds(3 * size, size)]

        if more:
            for n, (device, chip) in enumerate(chips):
                for q in range(links):
                    at = links * n + q
                    swaps.append(
                        remote(sent_rows(chip, q), r_all.at[h, q], r_send.at[at], r_recv.at[at], device)
                    )
            for q in range(links):
                swaps.append(
                    pltpu.make_async_copy(sent_rows(h, q), r_all.at[h, q], r_send.at[3 * links + q])
                )
            for swap in swaps:
                swap.start()
        for k in range(HEADS):
            chip = chip_on(me, h, k)[1]
            for src, dst in ((g_in, g_all), (k_in, k_all), (v_in, v_all)):
                dst[chip, core] = src[k]
        for copy in copies:
            copy.wait()
        k_run[...] = jnp.zeros_like(k_run)
        v_run[...] = jnp.zeros_like(v_run)
        g_run[...] = jnp.ones_like(g_run)
        order = [(c, d) for c in range(HEADS) for d in range(2)]
        for c, d in reversed(order) if reverse else order:
            k_pre[c, d] = k_run[...]
            v_pre[c, d] = v_run[...]
            g_pre[c, d] = g_run[...]
            gain = g_all[c, d]
            k_run[...] = gain[:, :1] * k_run[...] + k_all[c, d]
            v_run[...] = gain[:, :1] * v_run[...] + v_all[c, d]
            g_run[...] = gain * g_run[...]
        mine = pl.ds(pl.multiple_of(core * half, half), half)
        k_mine[...] = k_run[mine, :].astype(sent)
        v_mine[...] = v_run[mine, :].astype(sent)

        def along(k, go):
            step = -PLANE * k if reverse else PLANE * k
            device = me + step if go else me - step
            return [
                remote(src, dst.at[k - 1], z_send.at[n], z_recv.at[n], device)
                for n, src, dst in (
                    (3 * k - 3, g_run.at[mine], g_far),
                    (3 * k - 2, k_mine, k_far),
                    (3 * k - 1, v_mine, v_far),
                )
            ]

        def ahead(k):
            return z - k >= 0 if reverse else z + k < planes

        def behind(k):
            return z + k < planes if reverse else z - k >= 0

        for k in range(1, planes):
            @pl.when(ahead(k))
            def _(k=k):
                for copy in along(k, True):
                    copy.start()

        for k in reversed(range(1, planes)):
            @pl.when(behind(k))
            def _(k=k):
                for copy in along(k, False):
                    copy.wait_recv()
                gain = g_far[k - 1][:, :1]
                k_base[mine, :] = gain * k_base[mine, :] + k_far[k - 1].astype(f32)
                v_base[mine, :] = gain * v_base[mine, :] + v_far[k - 1].astype(f32)

        copies = [
            remote(k_base.at[mine], k_base.at[mine], b_send.at[0], b_recv.at[0], sibling),
            remote(v_base.at[mine], v_base.at[mine], b_send.at[1], b_recv.at[1], sibling),
        ]
        for copy in copies:
            copy.start()
        for copy in copies:
            copy.wait()
        for k in range(HEADS):
            chip = chip_on(me, h, k)[1]
            gain = g_pre[chip, core][:, :1]
            k_out[k] = gain * k_base[...] + k_pre[chip, core]
            v_out[k] = gain * v_base[...] + v_pre[chip, core]
        for swap in swaps:
            swap.wait()
        if lined:
            for c in range(HEADS):
                for n in range(links):
                    for b in range(HEADS):
                        at = ((n % quarter * HEADS + c) * 2 + n // quarter) * strip
                        r_out[pl.ds(at, strip), pl.ds(b * size, size)] = r_all[c, n, pl.ds(b * strip, strip), :]
        elif more:
            for c in range(HEADS):
                for q in range(quarter):
                    for b in range(HEADS):
                        at = ((c * quarter + q) * HEADS + b) * strip
                        r_out[pl.ds(at, strip), :] = r_all[c, q, :, pl.ds(b * size, size)]
        for k in range(1, planes):
            @pl.when(ahead(k))
            def _(k=k):
                for copy in along(k, True):
                    copy.wait_send()

    vmem = pl.BlockSpec(memory_space=pltpu.VMEM)
    wide = [pltpu.VMEM((HEADS, 2, slots, n), f32) for n in (size, size, 128)]
    state = [pltpu.VMEM((slots, n), f32) for n in (size, size, 128)]
    far = [pltpu.VMEM((planes - 1, half, n), d) for n, d in ((size, sent), (size, sent), (128, f32))]
    sends = [pltpu.VMEM((half, size), sent)] * 2
    side = []
    if more:
        side = [pltpu.VMEM(landing, bf16)] + [pltpu.SemaphoreType.DMA((4 * links,))] * 2
    semaphores = [12, 12, 3 * planes - 3, 3 * planes - 3, 2, 2]
    return pl.pallas_call(
        kernel,
        out_shape=[jax.ShapeDtypeStruct(keys.shape, f32)] * 2
        + ([jax.ShapeDtypeStruct(result, bf16)] if more else []),
        in_specs=[vmem] * 3 + [ANY] * more,
        out_specs=[vmem] * (2 + more),
        scratch_shapes=side + wide + wide + state + far + state[:2] + sends
        + [pltpu.SemaphoreType.DMA((n,)) for n in semaphores],
        compiler_params=pltpu.CompilerParams(
            collective_id=cid, has_side_effects=True, vmem_limit_bytes=32 << 20
        ),
        cost_estimate=lasting(22),
    )(keys, values, gains, *([line if lined else rows_out] if more else []))


def rms_factor(value_rows):
    return lax.rsqrt(jnp.mean(value_rows * value_rows, axis=-1, keepdims=True) + epsilon)


def precise(form, left, right):
    return jnp.einsum(form, left, right, precision=highest, preferred_element_type=f32)


def plain(form, left, right):
    return jnp.einsum(form, left, right, preferred_element_type=f32)


def local(
    tokens,
    cotangent,
    gate_codes,
    lengths,
    mixer_gain,
    query_weight,
    key_weight,
    value_weight,
    head_gain,
    output_weight,
    feed_gain,
    gate_weight,
    up_weight,
    down_weight,
):
    count = lax.axis_size("seq")
    planes = count // PLANE
    me = lax.axis_index("seq")
    z, h, core = me // PLANE, (me // 2) % HEADS, me % 2
    rows, width = tokens.shape
    strip = query_weight.shape[0]
    head_size = width // HEADS
    lines = [
        [p * PLANE + c * 2 + k for k in range(2) for p in range(planes)] for c in range(HEADS)
    ]

    def gather_line(x):
        return lax.all_gather(x, "seq", axis=0, tiled=True, axis_index_groups=lines)

    columns = [[p * PLANE + k for p in range(planes)] for k in range(PLANE)]

    def scatter_column(x):
        return lax.psum_scatter(
            x, "seq", scatter_dimension=0, tiled=True, axis_index_groups=columns
        )

    def to_sibling(x):
        return lax.ppermute(x, "seq", [(d, d ^ 1) for d in range(count)])

    def cut(x, side):
        part_width = x.shape[1] // 2
        return lax.dynamic_slice_in_dim(x, (core ^ side) * part_width, part_width, axis=1)


    def shuffled(x):
        y = x.reshape(*x.shape[:-1], planes * HEADS, 2, strip)
        return jnp.swapaxes(y, -3, -2).reshape(x.shape)

    def restored(x):
        y = x.reshape(*x.shape[:-1], 2, planes * HEADS, strip)
        return jnp.swapaxes(y, -3, -2).reshape(x.shape)

    turns = [
        [(d, d - 2 * (d // 2 % HEADS) + 2 * (d // 2 % HEADS ^ k)) for d in range(count)]
        for k in range(HEADS)
    ]

    def send_on(x, k):
        return lax.ppermute(x, "seq", turns[k])

    gains_all, codes_all, mixer_line, feed_rows, down_rows, h1 = opening(
        0,
        (mixer_gain, head_gain, feed_gain),
        gate_codes,
        (query_weight, key_weight, value_weight),
        output_weight,
        (gate_weight, up_weight, down_weight),
        tokens,
        planes,
    )
    feed_weight = gather_line(feed_rows)
    down_line = gather_line(down_rows)
    gain_of = gains_all[:, :3, :strip].swapaxes(0, 1).reshape(3, width)
    gain_one, gain_two = shuffled(gain_of[0])[None], shuffled(gain_of[2])[None]
    head_gain_f = lax.dynamic_slice(gain_of[1], (h * head_size,), (head_size,))

    tokens_own, cotangent_own = reordered([tokens, cotangent], planes)
    h1_other = to_sibling(cut(h1, 1))
    cotangent_parts = [cotangent_own] + [send_on(cotangent_own, k) for k in (1, 2, 3)]

    decay = jax.nn.log_sigmoid(codes_all.astype(f32) / 256.0)
    block = z * PLANE + 2 * ((h ^ jnp.arange(HEADS))) + core
    first = (block * rows)[:, None]
    position = first + jnp.arange(rows)[None, :]
    order = jnp.arange(lengths.shape[0])
    first_token = jnp.sum(
        jnp.where(order[:, None] > order[None, :], lengths[None, :], 0), axis=1
    )
    seen = jnp.sum(
        jnp.where(
            (first_token[None, None, :] <= position[:, :, None])
            & (first_token[None, None, :] >= first[:, :, None]),
            1,
            0,
        ),
        axis=2,
    )
    places = jnp.arange(rows)
    before = places[:, None] >= places[None, :]
    same = jnp.where(before[None] & (seen[:, :, None] == seen[:, None, :]), 1.0, 0.0).astype(f32)
    fresh = jnp.where(seen == 0, 1.0, 0.0).astype(f32)[:, :, None]
    logsum = precise("ts,bsm->btm", before.astype(f32), decay)
    grow = jnp.exp(logsum)
    back = jnp.exp(-logsum) * -jnp.expm1(decay)
    tail = jnp.where(seen == seen[:, -1:], 1.0, 0.0).astype(f32)[:, :, None]
    weights = grow[:, -1:] * back * tail
    carried = fresh[:, -1] * grow[:, -1]
    carried = jnp.broadcast_to(carried[:, :, None], (HEADS, SLOTS, 128))

    blocked = (HEADS, rows, head_size)
    mixer_weight = mixer_line[:, : 3 * head_size]
    projected = jnp.dot(h1, mixer_weight, preferred_element_type=f32).astype(bf16)
    query = projected[:, :head_size].reshape(blocked)
    key = projected[:, head_size : 2 * head_size].reshape(blocked)
    value = projected[:, 2 * head_size :].reshape(blocked)
    query_f = query.astype(f32)

    key_state, value_state, out_weight = carry_states(
        3,
        precise("bsm,bsd->bmd", weights, key.astype(f32)),
        precise("bsm,bsd->bmd", weights, value.astype(f32)),
        carried,
        planes,
        False,
        None,
        mixer_line,
    )

    affinity = plain("btd,bsd->bts", query, key) * same
    score = grow * precise("bts,bsm->btm", affinity, back) + grow * fresh * precise(
        "btd,bmd->btm", query_f, key_state
    )
    probs = jax.nn.softmax(score, axis=-1)
    lifted = probs * grow
    mixing = (precise("btm,bsm->bts", lifted, back) * same).astype(bf16)
    entry = lifted * fresh
    slot_out = plain("bts,bsd->btd", mixing, value) + precise("btm,bmd->btd", entry, value_state)
    head_factor = rms_factor(slot_out)
    unit_heads = slot_out * head_factor
    normed_heads = (unit_heads * head_gain_f).astype(bf16).reshape(HEADS * rows, head_size)

    quarter = planes // HEADS
    mixed = jnp.dot(normed_heads, out_weight, preferred_element_type=f32).astype(bf16)
    residual, h2 = plane_stage(
        4, mixed, [tokens_own, gain_two], residual_body, [((rows, width), f32)], True
    )

    h2, *cotangent_parts = lax.optimization_barrier((h2, *cotangent_parts))
    cotangent_all = jnp.concatenate(cotangent_parts)
    cotangent_other = to_sibling(cut(cotangent_all, 1))
    part = down_line.shape[1]
    both = jnp.dot(h2, feed_weight, preferred_element_type=f32)
    sigma = jax.nn.sigmoid(both[:, :part])
    hidden = (both[:, :part] * sigma * both[:, part:]).astype(bf16)
    hidden, both = lax.optimization_barrier((hidden, both))
    down_part = chip_sum(
        core, cotangent_all, hidden, cotangent_other, to_sibling(hidden)
    )
    down_sums = scatter_column(down_part)
    h2_other = to_sibling(cut(h2, 1))
    (heads_cut,) = reordered([normed_heads], quarter)
    heads_other = to_sibling(cut(heads_cut, 1))
    _, down_line, out_weight, h2_other, heads_other = lax.optimization_barrier(
        (down_part, down_line, out_weight, h2_other, heads_other)
    )
    gate, upward = both[:, :part], both[:, part:]
    sigma = jax.nn.sigmoid(gate)
    hidden_grad = jnp.dot(cotangent_all, down_line, preferred_element_type=f32)
    gate_back = (hidden_grad * upward * sigma * (1.0 + gate * (1.0 - sigma))).astype(bf16)
    up_back = (hidden_grad * (gate * sigma)).astype(bf16)
    both_back = jnp.concatenate([gate_back, up_back], axis=1)
    both_other = to_sibling(both_back)
    feed_in = plain("tf,df->td", both_back, feed_weight).astype(bf16)
    both_other, feed_in = lax.optimization_barrier((both_other, feed_in))
    feed_part = chip_sum(core, h2, both_back, h2_other, both_other)
    feed_part, feed_in = lax.optimization_barrier((feed_part, feed_in))
    feed_sums = scatter_column(feed_part)
    residual_grad, feed_gain_part, mixed_grad, *feed_out = plane_stage(
        5,
        feed_in,
        [residual, cotangent_own, gain_two],
        residual_grad_body,
        [((rows, width), f32), ((8, width), f32)],
        True,
        (hidden, down_line),
    )
    mixed_other = to_sibling(mixed_grad)
    feed_outs = [feed_out[0]] + [send_on(feed_out[k], k) for k in (1, 2, 3)]

    mixed_grad, down_sums = lax.optimization_barrier((mixed_grad, down_sums))
    heads_grad = plain("td,fd->tf", mixed_grad, out_weight).reshape(blocked)
    head_gain_part = jnp.sum(unit_heads * heads_grad, axis=(0, 1))
    scaled_heads = heads_grad * head_gain_f
    out_back = (
        head_factor
        * (scaled_heads - unit_heads * jnp.mean(unit_heads * scaled_heads, axis=-1, keepdims=True))
    ).astype(bf16)
    out_back_f = out_back.astype(f32)
    mixing_grad = plain("btd,bsd->bts", out_back, value) * same
    local_value = plain("bts,btd->bsd", mixing, out_back)
    lifted_grad = grow * precise("bts,bsm->btm", mixing_grad, back) + grow * fresh * precise(
        "btd,bmd->btm", out_back_f, value_state
    )
    score_grad = probs * (lifted_grad - jnp.sum(probs * lifted_grad, axis=-1, keepdims=True))
    inner_grad = grow * score_grad
    state_grad = inner_grad * fresh
    affinity_grad = (precise("btm,bsm->bts", inner_grad, back) * same).astype(bf16)
    first_key = precise("btm,btd->bmd", state_grad, query_f)
    first_value = precise("btm,btd->bmd", entry, out_back_f)
    out_part = chip_sum(core, heads_cut, mixed_grad, heads_other, mixed_other)
    out_part = out_part.reshape(quarter, HEADS, strip, width)
    later_key, later_value, out_part = carry_states(
        6, first_key, first_value, carried, planes, True, out_part
    )
    later_key, feed_outs = lax.optimization_barrier((later_key, feed_outs))

    query_back = plain("bts,bsd->btd", affinity_grad, key) + precise(
        "btm,bmd->btd", state_grad, key_state
    )
    key_back = plain("bts,btd->bsd", affinity_grad, query) + precise(
        "bsm,bmd->bsd", weights, later_key
    )
    value_back = local_value + precise("bsm,bmd->bsd", weights, later_value)
    backs = jnp.concatenate(
        [
            x.astype(bf16).reshape(HEADS * rows, head_size)
            for x in (query_back, key_back, value_back)
        ],
        axis=1,
    )
    backs_other = to_sibling(backs)
    mixer_part = chip_sum(core, h1, backs, h1_other, backs_other, out_part)
    (down_grad,) = return_columns(8, down_sums, 1, part, planes)
    mixer_part, feed_sums, backs, down_grad = lax.optimization_barrier(
        (mixer_part, feed_sums, backs, down_grad)
    )
    mixer_sums = scatter_column(mixer_part)
    mixer_in = plain("tf,df->td", backs, mixer_weight).astype(bf16)
    input_grad, mixer_gain_part, block_out = plane_stage(
        7,
        mixer_in,
        [tokens_own, residual_grad, gain_one, residual, *feed_outs],
        last_body(planes),
        [((rows, width), f32), ((8, width), f32), ((rows, width), bf16)],
        False,
    )

    head_whole = lax.dynamic_update_slice(
        jnp.zeros((width,), f32), head_gain_part, (h * head_size,)
    )
    gain_parts = jnp.stack(
        [
            restored(jnp.sum(mixer_gain_part, axis=0)),
            head_whole,
            restored(jnp.sum(feed_gain_part, axis=0)),
        ]
    )
    gain_parts = gain_parts.reshape(3, count, strip).swapaxes(0, 1)
    gain_parts = jnp.pad(gain_parts, ((0, 0), (0, 5), (0, 128 - strip)))
    gate_grad, up_grad, gain_sums = return_columns(9, feed_sums, 2, part, planes, gain_parts)
    down_grad, gate_grad, up_grad, input_grad, block_out = finished(
        [down_grad, gate_grad, up_grad], [input_grad, block_out]
    )
    mixer_sums, _ = lax.optimization_barrier((mixer_sums, block_out))
    query_grad, key_grad, value_grad, output_grad = return_columns(
        10, mixer_sums, 3, head_size, planes, None, True
    )
    gain_sums = gain_sums[:3, :strip]
    return (
        block_out,
        input_grad,
        gain_sums[0],
        query_grad,
        key_grad,
        value_grad,
        gain_sums[1],
        output_grad,
        gain_sums[2],
        gate_grad,
        up_grad,
        down_grad,
    )


def solution(mesh):
    split, line = P("seq", None), P("seq")
    return jax.shard_map(
        local,
        mesh=mesh,
        in_specs=(split, split, split, P(), line, split, split, split, line, split, line, split, split, split),
        out_specs=(split, split, line, split, split, split, line, split, line, split, split, split),
        check_vma=False,
    )
```

```python
import jax
import jax.numpy as jnp
from jax import lax
from jax.experimental import pallas as pl
from jax.experimental.pallas import tpu as pltpu
from jax.sharding import PartitionSpec as P

HEADS = 4
SLOTS = 64
PLANE = 8

epsilon = 1e-06
highest = lax.Precision.HIGHEST
bf16 = jnp.bfloat16
f32 = jnp.float32
MESH = pl.DeviceIdType.MESH
ANY = pl.BlockSpec(memory_space=pl.ANY)


def lasting(us):
    return pl.CostEstimate(flops=0, bytes_accessed=us * 3_400_000, transcendentals=0)


def chip_of(me):
    return lax.rem(lax.div(me, 2), HEADS)


def chip_on(me, h, k):
    turn = (k % 2) * (1 - 2 * lax.rem(h, 2)) + (k // 2) * (2 - 4 * lax.div(h, 2))
    return me + 2 * turn, h + turn


def rows_at(ref, block, size):
    return ref.at[pl.ds(pl.multiple_of(block * size, size), size)]


def columns_at(ref, block, size):
    return ref.at[:, pl.ds(pl.multiple_of(block * size, 128), size)]


def opening(cid, gains, codes, weights, output_rows, feed, tokens, planes):
    strip, width = weights[0].shape
    part = width // HEADS
    feed_part = feed[0].shape[1] // HEADS
    count = planes * PLANE
    hops = planes - 1

    tokens_rows = tokens.shape[0]

    def kernel(g0_in, g1_in, g2_in, codes_in, q_far, k_far, v_far, o_in, gate_far, up_far, down_far, t_in,
               g_out, c_out, line, feed_out, down_out, t_out, gain, t_mine, g_in, c_in, q_in, k_in, v_in,
               gate_in, up_in, down_in, load, t_send, t_recv, own_sem, q_send, q_recv, side_send, side_recv, u_send, u_recv, d_send, d_recv, s_send, s_recv):
        me = lax.axis_index("seq")
        h = chip_of(me)
        core = lax.rem(me, 2)
        z = lax.div(me, PLANE)
        sibling = me + 1 - 2 * core
        chips = [(None, h)] + [chip_on(me, h, k) for k in (1, 2, 3)]
        everyone = [lax.rem(me + k, count) for k in range(1, count)]
        far = (q_far, k_far, v_far, gate_far, up_far, down_far)
        near = (q_in, k_in, v_in, gate_in, up_in, down_in)
        loads = [pltpu.make_async_copy(a, b, load.at[n]) for n, (a, b) in enumerate(zip(far, near))]
        for copy in loads:
            copy.start()
        barrier = pltpu.get_barrier_semaphore()
        for device in everyone:
            pl.semaphore_signal(barrier, inc=1, device_id=(device,), device_id_type=MESH)
        g_in[...] = jnp.zeros_like(g_in)
        for n, ref in enumerate((g0_in, g1_in, g2_in)):
            g_in[n : n + 1, 0:strip] = ref[...].astype(f32)
        for k in range(HEADS):
            c_in[k] = codes_in[:, pl.ds(k * SLOTS, SLOTS)]
        for copy in loads[:3]:
            copy.wait()
        pl.semaphore_wait(barrier, count - 1)

        def remote(src, dst, s, r, device):
            return pltpu.make_async_remote_copy(
                src_ref=src, dst_ref=dst, send_sem=s, recv_sem=r, device_id=(device,), device_id_type=MESH
            )

        def row(plane, chip):
            return pl.ds(pl.multiple_of(((core * planes + plane) * HEADS + chip) * strip, strip), strip)

        def unit(plane, k):
            return line.at[row(plane, chips[k][1]), pl.ds(0, 3 * part)]

        def stack(plane):
            at = pl.multiple_of((core * planes + plane) * HEADS * strip, strip)
            return line.at[pl.ds(at, HEADS * strip), pl.ds(3 * part, part)]

        def stack_up(d):
            n = hops * HEADS + d - 1
            return remote(stack(z - d + 1), stack(z - d + 1), u_send.at[n], u_recv.at[n], me + PLANE)

        def stack_down(d):
            n = hops * HEADS + d - 1
            return remote(stack(z + d - 1), stack(z + d - 1), d_send.at[n], d_recv.at[n], me - PLANE)

        def stack_across(plane):
            n = planes * HEADS + plane
            return remote(stack(plane), stack(plane), s_send.at[n], s_recv.at[n], sibling)

        def up(d, k):
            n = (d - 1) * HEADS + k
            return remote(unit(z - d + 1, k), unit(z - d + 1, k), u_send.at[n], u_recv.at[n], me + PLANE)

        def down(d, k):
            n = (d - 1) * HEADS + k
            return remote(unit(z + d - 1, k), unit(z + d - 1, k), d_send.at[n], d_recv.at[n], me - PLANE)

        def across(plane, k):
            n = plane * HEADS + k
            return remote(unit(plane, k), unit(plane, k), s_send.at[n], s_recv.at[n], sibling)

        def pass_on(k):
            @pl.when(z + 1 < planes)
            def _():
                up(1, k).start()

            @pl.when(z >= 1)
            def _():
                down(1, k).start()

            across(z, k).start()

        projections = []
        for k in (3, 1, 2):
            device, chip = chips[k]
            for j, w in enumerate((q_in, k_in, v_in)):
                n = 3 * (k - 1) + j
                dst = line.at[row(z, h), pl.ds(j * part, part)]
                projections.append((k, remote(columns_at(w, chip, part), dst, q_send.at[n], q_recv.at[n], device)))
        own = [
            pltpu.make_async_copy(
                columns_at(w, h, part), line.at[row(z, h), pl.ds(j * part, part)], own_sem.at[j]
            )
            for j, w in enumerate((q_in, k_in, v_in))
        ]
        for _, copy in projections:
            copy.start()
        for copy in own:
            copy.start()
        turned = reorder(o_in[...], planes, False)
        for k in range(HEADS):
            line[row(z, k), pl.ds(3 * part, part)] = turned[:, k * part : (k + 1) * part]

        @pl.when(z + 1 < planes)
        def _():
            stack_up(1).start()

        @pl.when(z >= 1)
        def _():
            stack_down(1).start()

        stack_across(z).start()
        for copy in own:
            copy.wait()
        pass_on(0)

        shared = [(g_in, g_out.at[me], device) for device in everyone]
        sides = [(c_in.at[chip], c_out.at[k], device) for k, (device, chip) in list(enumerate(chips))[1:]]
        at = pl.ds(pl.multiple_of(h * strip, strip), strip)
        for src, out, column in ((gate_in, feed_out, 0), (up_in, feed_out, feed_part), (down_in, down_out, 0)):
            for device, chip in chips[1:] + chips[:1]:
                dst = out.at[at, pl.ds(column, feed_part)]
                sides.append((columns_at(src, chip, feed_part), dst, device))
        sides.append((c_in.at[h], c_out.at[0], None))
        begun = []

        def begin(listed):
            for src, dst, device in listed:
                n = len(begun)
                if device is None:
                    copy = pltpu.make_async_copy(src, dst, side_send.at[n])
                else:
                    copy = remote(src, dst, side_send.at[n], side_recv.at[n], device)
                copy.start()
                begun.append(copy)

        begin(shared)
        g_out[me] = g_in[...]
        for k in (1, 2, 3):
            for other, copy in projections:
                if other == k:
                    copy.wait_recv()
            pass_on(k)
        for copy in begun:
            copy.wait()
        shares = begun[:]
        gain[...] = jnp.concatenate(
            [
                g_out[(p * PLANE + c * 2 + k), 0:1, 0:strip]
                for k in range(2)
                for p in range(planes)
                for c in range(HEADS)
            ],
            axis=1,
        )

        def step(i, carry):
            at = pl.ds(pl.multiple_of(i * STEP, STEP), STEP)
            x = t_in[at, :].astype(f32)
            t_mine[at, :] = (reorder(x * factor_of(x), planes, False) * gain[...]).astype(bf16)
            return carry

        half = tokens_rows // 2
        low, high = pl.ds(0, half), pl.ds(half, half)
        x_side, y_side = chips[1][0], chips[2][0]

        def spread_out(mine, everything, sends, recvs):
            def block(k, first):
                return everything.at[pl.ds(k * tokens_rows + (0 if first else half), half)]

            copies = [
                remote(mine.at[low], block(1, True), sends.at[0], recvs.at[0], x_side),
                remote(mine.at[high], block(2, False), sends.at[1], recvs.at[1], y_side),
                remote(mine.at[high], block(1, False), sends.at[2], recvs.at[2], x_side),
                remote(mine.at[low], block(2, True), sends.at[3], recvs.at[3], y_side),
                remote(block(1, True), block(3, True), sends.at[4], recvs.at[4], y_side),
                remote(block(2, False), block(3, False), sends.at[5], recvs.at[5], x_side),
            ]
            keep = pltpu.make_async_copy(mine, everything.at[pl.ds(0, tokens_rows)], sends.at[6])
            for copy in copies[:4]:
                copy.start()
            keep.start()
            return copies, keep

        def relay(copies):
            copies[0].wait_recv()
            copies[4].start()
            copies[1].wait_recv()
            copies[5].start()

        def finish(copies, keep):
            for copy in copies[:2]:
                copy.wait_send()
            for copy in copies[2:]:
                copy.wait()
            keep.wait()

        lax.fori_loop(0, tokens_rows // STEP, step, 0)
        spread_t = spread_out(t_mine, t_out, t_send, t_recv)
        for copy in loads[3:]:
            copy.wait()
        begin(sides)
        for d in range(1, planes):

            @pl.when(z - d >= 0)
            def _(d=d):
                stack_up(d).wait_recv()

                @pl.when(z + 1 < planes)
                def _():
                    stack_up(d + 1).start()

                stack_across(z - d).start()

            @pl.when(z + d < planes)
            def _(d=d):
                stack_down(d).wait_recv()

                @pl.when(z >= 1)
                def _():
                    stack_down(d + 1).start()

                stack_across(z + d).start()

            for k in range(HEADS):

                @pl.when(z - d >= 0)
                def _(d=d, k=k):
                    up(d, k).wait_recv()

                    @pl.when(z + 1 < planes)
                    def _():
                        up(d + 1, k).start()

                    across(z - d, k).start()

                @pl.when(z + d < planes)
                def _(d=d, k=k):
                    down(d, k).wait_recv()

                    @pl.when(z >= 1)
                    def _():
                        down(d + 1, k).start()

                    across(z + d, k).start()

            if d == 1:
                relay(spread_t[0])
        for _, copy in projections:
            copy.wait_send()
        finish(*spread_t)
        for copy in begun[len(shares) :]:
            copy.wait()
        for d in range(1, planes):

            @pl.when((z - d + 1 >= 0) & (z + 1 < planes))
            def _(d=d):
                stack_up(d).wait_send()
                for k in range(HEADS):
                    up(d, k).wait_send()

            @pl.when((z + d - 1 < planes) & (z >= 1))
            def _(d=d):
                stack_down(d).wait_send()
                for k in range(HEADS):
                    down(d, k).wait_send()

        for plane in range(planes):
            stack_across(plane).wait()
            for k in range(HEADS):
                across(plane, k).wait()

    sides = count + 4 + 12
    vmem = pl.BlockSpec(memory_space=pltpu.VMEM)
    sizes = (6, 7, 6, 3, 9, 9, sides, sides) + (hops * (HEADS + 1),) * 4 + (planes * (HEADS + 1),) * 2
    shares = jax.ShapeDtypeStruct((count, 8, 128), f32)
    logits = jax.ShapeDtypeStruct((HEADS, tokens_rows, SLOTS), codes.dtype)
    return pl.pallas_call(
        kernel,
        out_shape=[
            shares,
            logits,
            jax.ShapeDtypeStruct((count * strip, 4 * part), bf16),
            jax.ShapeDtypeStruct((HEADS * strip, 2 * feed_part), bf16),
            jax.ShapeDtypeStruct((HEADS * strip, feed_part), bf16),
            jax.ShapeDtypeStruct((HEADS * tokens_rows, width), bf16),
        ],
        in_specs=[vmem] * 4 + [ANY] * 3 + [vmem] + [ANY] * 3 + [vmem],
        out_specs=[vmem] * 5 + [ANY],
        scratch_shapes=[
            pltpu.VMEM((1, width), f32),
            pltpu.VMEM(tokens.shape, bf16),
            pltpu.VMEM((8, 128), f32),
            pltpu.VMEM((HEADS, tokens_rows, SLOTS), codes.dtype),
        ]
        + [pltpu.VMEM(x.shape, bf16) for x in (*weights, *feed)]
        + [pltpu.SemaphoreType.DMA((n,)) for n in sizes],
        compiler_params=pltpu.CompilerParams(
            collective_id=cid, has_side_effects=True, vmem_limit_bytes=58 << 20
        ),
        cost_estimate=lasting(85),
    )(*(g[None] for g in gains), codes, *weights, output_rows, *feed, tokens)


def return_columns(cid, x, pieces, part, planes, gains=None, own_rows=False):
    rows = x.shape[0] // HEADS
    shared = gains is not None
    count = planes * PLANE

    def kernel(*refs):
        src, refs = refs[0], refs[1:]
        shares, refs = (refs[0], refs[1:]) if shared else (None, refs)
        outs, refs = refs[:pieces], refs[pieces:]
        extra, refs = (refs[0], refs[1:]) if own_rows else (None, refs)
        gain_out, refs = (refs[0], refs[1:]) if shared else (None, refs)
        send, recv, gain_in, gain_send, gain_recv = refs
        me = lax.axis_index("seq")
        h = chip_of(me)
        targets = [chip_on(me, h, k) for k in (3, 1, 2)]
        everyone = [lax.rem(me + k, count) for k in range(1, count)]
        peers = everyone if shared else [device for device, _ in targets]
        barrier = pltpu.get_barrier_semaphore()
        for device in peers:
            pl.semaphore_signal(barrier, inc=1, device_id=(device,), device_id_type=MESH)
        pl.semaphore_wait(barrier, len(peers))

        def to(device, source, dst, sends, recvs, n):
            return pltpu.make_async_remote_copy(
                src_ref=source, dst_ref=dst, send_sem=sends.at[n], recv_sem=recvs.at[n],
                device_id=(device,), device_id_type=MESH,
            )

        def place(j):
            return columns_at(outs[j], h, part)

        copies = []
        for k, (device, other) in enumerate(targets):
            for j in range(pieces):
                source = src.at[
                    pl.ds(pl.multiple_of(other * rows, rows), rows), pl.ds(j * part, part)
                ]
                copies.append(to(device, source, place(j), send, recv, k * pieces + j))
        if shared:
            for n, device in enumerate(everyone):
                copies.append(to(device, shares.at[device], gain_in.at[me], gain_send, gain_recv, n))
        own = pl.ds(pl.multiple_of(h * rows, rows), rows)
        for j in range(pieces):
            copies.append(
                pltpu.make_async_copy(src.at[own, pl.ds(j * part, part)], place(j), send.at[3 * pieces + j])
            )
        for copy in copies:
            copy.start()
        if shared:
            gain_in[me] = shares[me]
        if own_rows:
            blocks = [src[pl.ds(k * rows, rows), pl.ds(pieces * part, part)] for k in range(HEADS)]
            extra[...] = reorder(jnp.concatenate(blocks, axis=1), planes, True)
        for copy in copies:
            copy.wait()
        if shared:
            total = gain_in[0]
            for k in range(1, count):
                total = total + gain_in[k]
            gain_out[...] = total

    vmem = pl.BlockSpec(memory_space=pltpu.VMEM)
    shapes = [jax.ShapeDtypeStruct((rows, HEADS * part), bf16)] * (pieces + int(own_rows))
    shapes += [jax.ShapeDtypeStruct((8, 128), f32)] * int(shared)
    return pl.pallas_call(
        kernel,
        out_shape=shapes,
        in_specs=[vmem] * (1 + int(shared)),
        out_specs=[vmem] * len(shapes),
        scratch_shapes=[
            pltpu.SemaphoreType.DMA((4 * pieces,)),
            pltpu.SemaphoreType.DMA((3 * pieces,)),
            pltpu.VMEM((count if shared else 1, 8, 128), f32),
            pltpu.SemaphoreType.DMA((count if shared else 1,)),
            pltpu.SemaphoreType.DMA((count if shared else 1,)),
        ],
        compiler_params=pltpu.CompilerParams(
            collective_id=cid, has_side_effects=True, vmem_limit_bytes=40 << 20
        ),
        cost_estimate=lasting(14),
    )(*([x, gains] if shared else [x]))


def finished(narrow, others):
    arrays = [*narrow, *others]
    kinds = [f32] * len(narrow) + [x.dtype for x in others]

    def kernel(*refs):
        for src, dst in zip(refs[: len(arrays)], refs[len(arrays) :]):
            dst[...] = src[...].astype(dst.dtype)

    specs = [pl.BlockSpec((x.shape[0] // 2, x.shape[1]), lambda i: (i, 0)) for x in arrays]
    if any(x.shape[0] % 32 for x in arrays):
        specs = [pl.BlockSpec(x.shape, lambda i: (0, 0)) for x in arrays]
    return pl.pallas_call(
        kernel,
        out_shape=[jax.ShapeDtypeStruct(x.shape, kind) for x, kind in zip(arrays, kinds)],
        grid=(2 if specs[0].block_shape[0] < arrays[0].shape[0] else 1,),
        in_specs=specs,
        out_specs=specs,
        compiler_params=pltpu.CompilerParams(vmem_limit_bytes=40 << 20),
        cost_estimate=lasting(3),
    )(*arrays)


STEP = 16


def reorder(x, planes, back):
    chips = planes * HEADS
    strip = x.shape[1] // (2 * chips)
    pieces = []
    for i in range(2 * chips):
        n = (i % 2) * chips + i // 2 if back else (i % chips) * 2 + i // chips
        pieces.append(x[:, n * strip : (n + 1) * strip])
    return jnp.concatenate(pieces, axis=1)


def reordered(arrays, planes):
    def kernel(*refs):
        for src, dst in zip(refs[: len(arrays)], refs[len(arrays) :]):

            def step(i, carry, src=src, dst=dst):
                at = pl.ds(pl.multiple_of(i * STEP, STEP), STEP)
                dst[at, :] = reorder(src[at, :], planes, False)
                return carry

            lax.fori_loop(0, src.shape[0] // STEP, step, 0)

    vmem = pl.BlockSpec(memory_space=pltpu.VMEM)
    return pl.pallas_call(
        kernel,
        out_shape=[jax.ShapeDtypeStruct(x.shape, x.dtype) for x in arrays],
        in_specs=[vmem] * len(arrays),
        out_specs=[vmem] * len(arrays),
        compiler_params=pltpu.CompilerParams(vmem_limit_bytes=32 << 20),
    )(*arrays)


def plane_stage(cid, partial, blocks, body, own, gathered, product=None):
    rows, width = blocks[0].shape
    half = rows // 2
    has = int(partial is not None)
    low, high = pl.ds(0, half), pl.ds(half, half)

    def kernel(*refs):
        part = refs[0] if has else None
        block_refs = refs[has : has + len(blocks)]
        rest = refs[has + len(blocks) :]
        factors, rest = (rest[:2], rest[2:]) if product else (None, rest)
        own_refs, rest = rest[: len(own)], rest[len(own) :]
        everything, rest = (rest[0], rest[1:]) if gathered else (None, rest)
        results, rest = (rest[:HEADS], rest[HEADS:]) if product else (None, rest)
        (left, right, load), rest = (rest[:3], rest[3:]) if product else ((None,) * 3, rest)
        by_x, by_y, over_x, over_y, sum_x, sum_y, mine, send, recv, out_send, out_recv = rest
        me = lax.axis_index("seq")
        h = chip_of(me)
        x_side, y_side = chip_on(me, h, 1)[0], chip_on(me, h, 2)[0]
        barrier = pltpu.get_barrier_semaphore()
        for device in (x_side, y_side):
            pl.semaphore_signal(barrier, inc=1, device_id=(device,), device_id_type=MESH)
        pl.semaphore_wait(barrier, 2)

        def to(device, src, dst, sends, recvs, n):
            return pltpu.make_async_remote_copy(
                src_ref=src, dst_ref=dst, send_sem=sends.at[n], recv_sem=recvs.at[n],
                device_id=(device,), device_id_type=MESH,
            )

        def block(k, first):
            return pl.ds(k * rows + (0 if first else half), half)

        loads = []
        if product:
            loads = [
                pltpu.make_async_copy(src, dst, load.at[n])
                for n, (src, dst) in enumerate(zip(factors, (left, right)))
            ]

        def multiply(k):
            if product:
                results[k][...] = lax.dot_general(
                    left[pl.ds(k * rows, rows), :], right[...], (((1,), (1,)), ((), ())),
                    preferred_element_type=f32,
                ).astype(bf16)

        if has:
            copies = [
                to(x_side, part.at[block(3, True)], over_x, send, recv, 0),
                to(y_side, part.at[block(3, False)], over_y, send, recv, 1),
                to(x_side, part.at[block(1, True)], by_x.at[low], send, recv, 2),
                to(y_side, part.at[block(2, False)], by_y.at[high], send, recv, 3),
                to(y_side, sum_y, by_y.at[low], send, recv, 4),
                to(x_side, sum_x, by_x.at[high], send, recv, 5),
            ]
            for copy in copies[:4]:
                copy.start()
            for copy in loads:
                copy.start()
            for copy in loads:
                copy.wait()
            multiply(0)
            copies[0].wait_recv()
            sum_y[...] = (part[block(2, True), :].astype(f32) + over_x[...].astype(f32)).astype(bf16)
            copies[4].start()
            copies[1].wait_recv()
            sum_x[...] = (part[block(1, False), :].astype(f32) + over_y[...].astype(f32)).astype(bf16)
            copies[5].start()
            multiply(1)
            for copy in copies[:2]:
                copy.wait_send()
            for copy in copies[2:]:
                copy.wait()

        def step(i, carry):
            at = pl.ds(pl.multiple_of(i * STEP, STEP), STEP)
            total = None
            if has:
                total = part[at, :].astype(f32) + by_x[at, :].astype(f32) + by_y[at, :].astype(f32)
            body(i, at, total, block_refs, own_refs, mine)
            return carry

        lax.fori_loop(0, rows // STEP, step, 0)
        if gathered:
            from_x, from_y = everything.at[block(1, True)], everything.at[block(2, False)]
            copies = [
                to(x_side, mine.at[low], from_x, out_send, out_recv, 0),
                to(y_side, mine.at[high], from_y, out_send, out_recv, 1),
                to(x_side, mine.at[high], everything.at[block(1, False)], out_send, out_recv, 2),
                to(y_side, mine.at[low], everything.at[block(2, True)], out_send, out_recv, 3),
                to(y_side, from_x, everything.at[block(3, True)], out_send, out_recv, 4),
                to(x_side, from_y, everything.at[block(3, False)], out_send, out_recv, 5),
            ]
            keep = pltpu.make_async_copy(mine, everything.at[pl.ds(0, rows)], out_send.at[6])
            for copy in copies[:4]:
                copy.start()
            keep.start()
            multiply(2)
            copies[0].wait_recv()
            copies[4].start()
            copies[1].wait_recv()
            copies[5].start()
            multiply(3)
            for copy in copies[:2]:
                copy.wait_send()
            for copy in copies[2:]:
                copy.wait()
            keep.wait()

    vmem = pl.BlockSpec(memory_space=pltpu.VMEM)
    shapes = [jax.ShapeDtypeStruct(s, d) for s, d in own]
    if gathered:
        shapes.append(jax.ShapeDtypeStruct((HEADS * rows, width), bf16))
    factors_in, loaded = [], []
    if product:
        shapes += [jax.ShapeDtypeStruct((rows, width), bf16)] * HEADS
        factors_in = list(product)
        loaded = [pltpu.VMEM(x.shape, x.dtype) for x in product] + [pltpu.SemaphoreType.DMA((2,))]
    whole, part_of = ((rows, width), (half, width)) if has else ((STEP, 128), (STEP, 128))
    return pl.pallas_call(
        kernel,
        out_shape=shapes,
        in_specs=[vmem] * (has + len(blocks)) + [ANY] * len(factors_in),
        out_specs=[vmem] * len(own) + [ANY] * int(gathered) + [vmem] * (HEADS if product else 0),
        scratch_shapes=loaded + [pltpu.VMEM(s, bf16) for s in (whole, whole, part_of, part_of, part_of, part_of)]
        + [pltpu.VMEM((rows, width), bf16)]
        + [pltpu.SemaphoreType.DMA((n,)) for n in (6, 6, 7, 6)],
        compiler_params=pltpu.CompilerParams(
            collective_id=cid, has_side_effects=True, vmem_limit_bytes=40 << 20
        ),
        cost_estimate=lasting(25 * has + 25 * int(gathered)),
    )(*([partial] if has else []), *blocks, *factors_in)


def chip_sum(core, left, right, other_left, other_right, extra=None):
    tokens, columns = right.shape
    half = left.shape[1] // 2
    block = min(half, 256)
    steps = half // block
    more = 0 if extra is None else extra.shape[1]
    contract = (((0,), (0,)), ((), ()))
    pieces = 2 if columns % 256 == 0 and columns > 2048 else 1
    size = columns // pieces

    def kernel(which, a, b, c, d, *rest):
        out = rest[-1]
        for n in range(pieces):
            at = pl.ds(n * size, size)
            total = lax.dot_general(a[...], b[:, at], contract, preferred_element_type=f32)
            total += lax.dot_general(c[...], d[:, at], contract, preferred_element_type=f32)
            out[:, at] = total.astype(bf16)
        if more:
            out[:, pl.ds(columns, more)] = rest[0][...]

    whole = pl.BlockSpec((tokens, columns), lambda i, w: (0, 0), pipeline_mode=pl.Buffered(1))
    specs = [
        pl.BlockSpec((tokens, block), lambda i, w: (0, w[0] * steps + i)),
        whole,
        pl.BlockSpec((tokens, block), lambda i, w: (0, i)),
        whole,
    ]
    if more:
        specs.append(pl.BlockSpec((block, more), lambda i, w: (i, 0)))
    return pl.pallas_call(
        kernel,
        out_shape=jax.ShapeDtypeStruct((half, columns + more), bf16),
        grid_spec=pltpu.PrefetchScalarGridSpec(
            num_scalar_prefetch=1,
            grid=(steps,),
            in_specs=specs,
            out_specs=pl.BlockSpec((block, columns + more), lambda i, w: (i, 0)),
        ),
        compiler_params=pltpu.CompilerParams(vmem_limit_bytes=40 << 20),
        cost_estimate=pl.CostEstimate(
            flops=4 * tokens * half * columns,
            bytes_accessed=4 * tokens * (half + columns) + 2 * half * columns,
            transcendentals=0,
        ),
    )(core.reshape(1), left, right, other_left, other_right, *(() if extra is None else (extra,)))


def factor_of(x):
    return lax.rsqrt(jnp.mean(x * x, axis=-1, keepdims=True) + epsilon)


def residual_body(i, at, total, blocks, own, mine):
    tokens, gain = blocks
    x = tokens[at, :].astype(f32) + total
    own[0][at, :] = x
    mine[at, :] = (x * factor_of(x) * gain[...]).astype(bf16)


def accumulate(i, ref, product):
    part = product[:8] + product[8:]

    @pl.when(i == 0)
    def _():
        ref[...] = part

    @pl.when(i > 0)
    def _():
        ref[...] += part


def residual_grad_body(i, at, total, blocks, own, mine):
    residual, cotangent, gain = blocks
    x = residual[at, :]
    factor = factor_of(x)
    normed = x * factor
    accumulate(i, own[1], normed * total)
    scaled = total * gain[...]
    grad = cotangent[at, :].astype(f32) + factor * (
        scaled - normed * jnp.mean(normed * scaled, axis=-1, keepdims=True)
    )
    own[0][at, :] = grad
    mine[at, :] = grad.astype(bf16)


def last_body(planes):
    def body(i, at, total, blocks, own, mine):
        tokens, later, gain, residual, *outs = blocks
        x = tokens[at, :].astype(f32)
        factor = factor_of(x)
        normed = x * factor
        accumulate(i, own[1], normed * total)
        scaled = total * gain[...]
        grad = later[at, :] + factor * (
            scaled - normed * jnp.mean(normed * scaled, axis=-1, keepdims=True)
        )
        own[0][at, :] = reorder(grad, planes, True)
        result = residual[at, :]
        for out in outs:
            result = result + out[at, :].astype(f32)
        own[2][at, :] = reorder(result.astype(bf16), planes, True)

    return body


def carry_states(cid, keys, values, gains, planes, reverse, rows_out=None, line=None):
    lined = line is not None
    more = int(rows_out is not None or lined)
    sent = bf16 if reverse else f32
    _, slots, size = keys.shape
    half = slots // 2
    if lined:
        quarter, strip = planes // HEADS, line.shape[0] // (planes * PLANE)
        landing, result = (HEADS, 2 * quarter, HEADS * strip, size), (size, HEADS * size)
        links = 2 * quarter
    elif more:
        quarter, _, strip, _ = rows_out.shape
        landing, result = (HEADS, quarter, strip, HEADS * size), (HEADS * quarter * HEADS * strip, size)
        links = quarter

    def kernel(k_in, v_in, g_in, *refs):
        r_in, refs = (refs[0], refs[1:]) if more else (None, refs)
        k_out, v_out, refs = refs[0], refs[1], refs[2:]
        r_out, refs = (refs[0], refs[1:]) if more else (None, refs)
        r_all, r_send, r_recv, refs = (*refs[:3], refs[3:]) if more else (None, None, None, refs)
        main(k_in, v_in, g_in, k_out, v_out, *refs, r_in=r_in, r_out=r_out, r_all=r_all, r_send=r_send, r_recv=r_recv)

    def main(k_in, v_in, g_in, k_out, v_out, k_all, v_all, g_all, k_pre, v_pre, g_pre, k_run, v_run, g_run,
               k_far, v_far, g_far, k_base, v_base, k_mine, v_mine, s_send, s_recv, z_send, z_recv, b_send, b_recv,
             *, r_in, r_out, r_all, r_send, r_recv):
        me = lax.axis_index("seq")
        h = chip_of(me)
        core = lax.rem(me, 2)
        z = lax.div(me, PLANE)
        sibling = me + 1 - 2 * core
        barrier = pltpu.get_barrier_semaphore()
        others = [me + PLANE * (lax.rem(z + k, planes) - z) for k in range(1, planes)]
        chips = [chip_on(me, h, k) for k in (1, 2, 3)]
        greeted = [sibling, *others] + ([device for device, _ in chips] if more else [])
        for device in greeted:
            pl.semaphore_signal(barrier, inc=1, device_id=(device,), device_id_type=MESH)
        pl.semaphore_wait(barrier, len(greeted))

        def remote(src, dst, s, r, device):
            return pltpu.make_async_remote_copy(
                src_ref=src, dst_ref=dst, send_sem=s, recv_sem=r, device_id=(device,), device_id_type=MESH
            )

        k_base[...] = jnp.zeros_like(k_base)
        v_base[...] = jnp.zeros_like(v_base)
        copies = []
        for k in range(HEADS):
            chip = chip_on(me, h, k)[1]
            for j, (src, dst) in enumerate(((g_in, g_all), (k_in, k_all), (v_in, v_all))):
                n = 3 * k + j
                copies.append(remote(src.at[k], dst.at[chip, core], s_send.at[n], s_recv.at[n], sibling))
        for copy in copies:
            copy.start()
        swaps = []

        def sent_rows(chip, n):
            if not lined:
                return r_in.at[n, chip]
            at = ((n // quarter * planes) + chip * quarter + n % quarter) * HEADS * strip
            return r_in.at[pl.ds(pl.multiple_of(at, HEADS * strip), HEADS * strip), pl.ds(3 * size, size)]

        if more:
            for n, (device, chip) in enumerate(chips):
                for q in range(links):
                    at = links * n + q
                    swaps.append(
                        remote(sent_rows(chip, q), r_all.at[h, q], r_send.at[at], r_recv.at[at], device)
                    )
            for q in range(links):
                swaps.append(
                    pltpu.make_async_copy(sent_rows(h, q), r_all.at[h, q], r_send.at[3 * links + q])
                )
            for swap in swaps:
                swap.start()
        for k in range(HEADS):
            chip = chip_on(me, h, k)[1]
            for src, dst in ((g_in, g_all), (k_in, k_all), (v_in, v_all)):
                dst[chip, core] = src[k]
        for copy in copies:
            copy.wait()
        k_run[...] = jnp.zeros_like(k_run)
        v_run[...] = jnp.zeros_like(v_run)
        g_run[...] = jnp.ones_like(g_run)
        order = [(c, d) for c in range(HEADS) for d in range(2)]
        for c, d in reversed(order) if reverse else order:
            k_pre[c, d] = k_run[...]
            v_pre[c, d] = v_run[...]
            g_pre[c, d] = g_run[...]
            gain = g_all[c, d]
            k_run[...] = gain[:, :1] * k_run[...] + k_all[c, d]
            v_run[...] = gain[:, :1] * v_run[...] + v_all[c, d]
            g_run[...] = gain * g_run[...]
        mine = pl.ds(pl.multiple_of(core * half, half), half)
        k_mine[...] = k_run[mine, :].astype(sent)
        v_mine[...] = v_run[mine, :].astype(sent)

        def along(k, go):
            step = -PLANE * k if reverse else PLANE * k
            device = me + step if go else me - step
            return [
                remote(src, dst.at[k - 1], z_send.at[n], z_recv.at[n], device)
                for n, src, dst in (
                    (3 * k - 3, g_run.at[mine], g_far),
                    (3 * k - 2, k_mine, k_far),
                    (3 * k - 1, v_mine, v_far),
                )
            ]

        def ahead(k):
            return z - k >= 0 if reverse else z + k < planes

        def behind(k):
            return z + k < planes if reverse else z - k >= 0

        for k in range(1, planes):
            @pl.when(ahead(k))
            def _(k=k):
                for copy in along(k, True):
                    copy.start()

        for k in reversed(range(1, planes)):
            @pl.when(behind(k))
            def _(k=k):
                for copy in along(k, False):
                    copy.wait_recv()
                gain = g_far[k - 1][:, :1]
                k_base[mine, :] = gain * k_base[mine, :] + k_far[k - 1].astype(f32)
                v_base[mine, :] = gain * v_base[mine, :] + v_far[k - 1].astype(f32)

        copies = [
            remote(k_base.at[mine], k_base.at[mine], b_send.at[0], b_recv.at[0], sibling),
            remote(v_base.at[mine], v_base.at[mine], b_send.at[1], b_recv.at[1], sibling),
        ]
        for copy in copies:
            copy.start()
        for copy in copies:
            copy.wait()
        for k in range(HEADS):
            chip = chip_on(me, h, k)[1]
            gain = g_pre[chip, core][:, :1]
            k_out[k] = gain * k_base[...] + k_pre[chip, core]
            v_out[k] = gain * v_base[...] + v_pre[chip, core]
        for swap in swaps:
            swap.wait()
        if lined:
            for c in range(HEADS):
                for n in range(links):
                    for b in range(HEADS):
                        at = ((n % quarter * HEADS + c) * 2 + n // quarter) * strip
                        r_out[pl.ds(at, strip), pl.ds(b * size, size)] = r_all[c, n, pl.ds(b * strip, strip), :]
        elif more:
            for c in range(HEADS):
                for q in range(quarter):
                    for b in range(HEADS):
                        at = ((c * quarter + q) * HEADS + b) * strip
                        r_out[pl.ds(at, strip), :] = r_all[c, q, :, pl.ds(b * size, size)]
        for k in range(1, planes):
            @pl.when(ahead(k))
            def _(k=k):
                for copy in along(k, True):
                    copy.wait_send()

    vmem = pl.BlockSpec(memory_space=pltpu.VMEM)
    wide = [pltpu.VMEM((HEADS, 2, slots, n), f32) for n in (size, size, 128)]
    state = [pltpu.VMEM((slots, n), f32) for n in (size, size, 128)]
    far = [pltpu.VMEM((planes - 1, half, n), d) for n, d in ((size, sent), (size, sent), (128, f32))]
    sends = [pltpu.VMEM((half, size), sent)] * 2
    side = []
    if more:
        side = [pltpu.VMEM(landing, bf16)] + [pltpu.SemaphoreType.DMA((4 * links,))] * 2
    semaphores = [12, 12, 3 * planes - 3, 3 * planes - 3, 2, 2]
    return pl.pallas_call(
        kernel,
        out_shape=[jax.ShapeDtypeStruct(keys.shape, f32)] * 2
        + ([jax.ShapeDtypeStruct(result, bf16)] if more else []),
        in_specs=[vmem] * 3 + [ANY] * more,
        out_specs=[vmem] * (2 + more),
        scratch_shapes=side + wide + wide + state + far + state[:2] + sends
        + [pltpu.SemaphoreType.DMA((n,)) for n in semaphores],
        compiler_params=pltpu.CompilerParams(
            collective_id=cid, has_side_effects=True, vmem_limit_bytes=32 << 20
        ),
        cost_estimate=lasting(22),
    )(keys, values, gains, *([line if lined else rows_out] if more else []))


def rms_factor(value_rows):
    return lax.rsqrt(jnp.mean(value_rows * value_rows, axis=-1, keepdims=True) + epsilon)


def precise(form, left, right):
    return jnp.einsum(form, left, right, precision=highest, preferred_element_type=f32)


def plain(form, left, right):
    return jnp.einsum(form, left, right, preferred_element_type=f32)


def local(
    tokens,
    cotangent,
    gate_codes,
    lengths,
    mixer_gain,
    query_weight,
    key_weight,
    value_weight,
    head_gain,
    output_weight,
    feed_gain,
    gate_weight,
    up_weight,
    down_weight,
):
    count = lax.axis_size("seq")
    planes = count // PLANE
    me = lax.axis_index("seq")
    z, h, core = me // PLANE, (me // 2) % HEADS, me % 2
    rows, width = tokens.shape
    strip = query_weight.shape[0]
    head_size = width // HEADS
    lines = [
        [p * PLANE + c * 2 + k for k in range(2) for p in range(planes)] for c in range(HEADS)
    ]

    def gather_line(x):
        return lax.all_gather(x, "seq", axis=0, tiled=True, axis_index_groups=lines)

    columns = [[p * PLANE + k for p in range(planes)] for k in range(PLANE)]

    def scatter_column(x):
        return lax.psum_scatter(
            x, "seq", scatter_dimension=0, tiled=True, axis_index_groups=columns
        )

    def to_sibling(x):
        return lax.ppermute(x, "seq", [(d, d ^ 1) for d in range(count)])

    def cut(x, side):
        part_width = x.shape[1] // 2
        return lax.dynamic_slice_in_dim(x, (core ^ side) * part_width, part_width, axis=1)


    def shuffled(x):
        y = x.reshape(*x.shape[:-1], planes * HEADS, 2, strip)
        return jnp.swapaxes(y, -3, -2).reshape(x.shape)

    def restored(x):
        y = x.reshape(*x.shape[:-1], 2, planes * HEADS, strip)
        return jnp.swapaxes(y, -3, -2).reshape(x.shape)

    turns = [
        [(d, d - 2 * (d // 2 % HEADS) + 2 * (d // 2 % HEADS ^ k)) for d in range(count)]
        for k in range(HEADS)
    ]

    def send_on(x, k):
        return lax.ppermute(x, "seq", turns[k])

    gains_all, codes_all, mixer_line, feed_rows, down_rows, h1 = opening(
        0,
        (mixer_gain, head_gain, feed_gain),
        gate_codes,
        (query_weight, key_weight, value_weight),
        output_weight,
        (gate_weight, up_weight, down_weight),
        tokens,
        planes,
    )
    feed_weight = gather_line(feed_rows)
    down_line = gather_line(down_rows)
    gain_of = gains_all[:, :3, :strip].swapaxes(0, 1).reshape(3, width)
    gain_one, gain_two = shuffled(gain_of[0])[None], shuffled(gain_of[2])[None]
    head_gain_f = lax.dynamic_slice(gain_of[1], (h * head_size,), (head_size,))

    tokens_own, cotangent_own = reordered([tokens, cotangent], planes)
    h1_other = to_sibling(cut(h1, 1))
    cotangent_parts = [cotangent_own] + [send_on(cotangent_own, k) for k in (1, 2, 3)]

    decay = jax.nn.log_sigmoid(codes_all.astype(f32) / 256.0)
    block = z * PLANE + 2 * ((h ^ jnp.arange(HEADS))) + core
    first = (block * rows)[:, None]
    position = first + jnp.arange(rows)[None, :]
    order = jnp.arange(lengths.shape[0])
    first_token = jnp.sum(
        jnp.where(order[:, None] > order[None, :], lengths[None, :], 0), axis=1
    )
    seen = jnp.sum(
        jnp.where(
            (first_token[None, None, :] <= position[:, :, None])
            & (first_token[None, None, :] >= first[:, :, None]),
            1,
            0,
        ),
        axis=2,
    )
    places = jnp.arange(rows)
    before = places[:, None] >= places[None, :]
    same = jnp.where(before[None] & (seen[:, :, None] == seen[:, None, :]), 1.0, 0.0).astype(f32)
    fresh = jnp.where(seen == 0, 1.0, 0.0).astype(f32)[:, :, None]
    logsum = precise("ts,bsm->btm", before.astype(f32), decay)
    grow = jnp.exp(logsum)
    back = jnp.exp(-logsum) * -jnp.expm1(decay)
    tail = jnp.where(seen == seen[:, -1:], 1.0, 0.0).astype(f32)[:, :, None]
    weights = grow[:, -1:] * back * tail
    carried = fresh[:, -1] * grow[:, -1]
    carried = jnp.broadcast_to(carried[:, :, None], (HEADS, SLOTS, 128))

    blocked = (HEADS, rows, head_size)
    mixer_weight = mixer_line[:, : 3 * head_size]
    projected = jnp.dot(h1, mixer_weight, preferred_element_type=f32).astype(bf16)
    query = projected[:, :head_size].reshape(blocked)
    key = projected[:, head_size : 2 * head_size].reshape(blocked)
    value = projected[:, 2 * head_size :].reshape(blocked)
    query_f = query.astype(f32)

    key_state, value_state, out_weight = carry_states(
        3,
        precise("bsm,bsd->bmd", weights, key.astype(f32)),
        precise("bsm,bsd->bmd", weights, value.astype(f32)),
        carried,
        planes,
        False,
        None,
        mixer_line,
    )

    affinity = plain("btd,bsd->bts", query, key) * same
    score = grow * precise("bts,bsm->btm", affinity, back) + grow * fresh * precise(
        "btd,bmd->btm", query_f, key_state
    )
    probs = jax.nn.softmax(score, axis=-1)
    lifted = probs * grow
    mixing = (precise("btm,bsm->bts", lifted, back) * same).astype(bf16)
    entry = lifted * fresh
    slot_out = plain("bts,bsd->btd", mixing, value) + precise("btm,bmd->btd", entry, value_state)
    head_factor = rms_factor(slot_out)
    unit_heads = slot_out * head_factor
    normed_heads = (unit_heads * head_gain_f).astype(bf16).reshape(HEADS * rows, head_size)

    quarter = planes // HEADS
    mixed = jnp.dot(normed_heads, out_weight, preferred_element_type=f32).astype(bf16)
    residual, h2 = plane_stage(
        4, mixed, [tokens_own, gain_two], residual_body, [((rows, width), f32)], True
    )

    h2, *cotangent_parts = lax.optimization_barrier((h2, *cotangent_parts))
    cotangent_all = jnp.concatenate(cotangent_parts)
    cotangent_other = to_sibling(cut(cotangent_all, 1))
    part = down_line.shape[1]
    both = jnp.dot(h2, feed_weight, preferred_element_type=f32)
    sigma = jax.nn.sigmoid(both[:, :part])
    hidden = (both[:, :part] * sigma * both[:, part:]).astype(bf16)
    hidden, both = lax.optimization_barrier((hidden, both))
    down_part = chip_sum(
        core, cotangent_all, hidden, cotangent_other, to_sibling(hidden)
    )
    down_sums = scatter_column(down_part)
    h2_other = to_sibling(cut(h2, 1))
    (heads_cut,) = reordered([normed_heads], quarter)
    heads_other = to_sibling(cut(heads_cut, 1))
    _, down_line, out_weight, h2_other, heads_other = lax.optimization_barrier(
        (down_part, down_line, out_weight, h2_other, heads_other)
    )
    gate, upward = both[:, :part], both[:, part:]
    sigma = jax.nn.sigmoid(gate)
    hidden_grad = jnp.dot(cotangent_all, down_line, preferred_element_type=f32)
    gate_back = (hidden_grad * upward * sigma * (1.0 + gate * (1.0 - sigma))).astype(bf16)
    up_back = (hidden_grad * (gate * sigma)).astype(bf16)
    both_back = jnp.concatenate([gate_back, up_back], axis=1)
    both_other = to_sibling(both_back)
    feed_in = plain("tf,df->td", both_back, feed_weight).astype(bf16)
    both_other, feed_in = lax.optimization_barrier((both_other, feed_in))
    feed_part = chip_sum(core, h2, both_back, h2_other, both_other)
    feed_part, feed_in = lax.optimization_barrier((feed_part, feed_in))
    feed_sums = scatter_column(feed_part)
    residual_grad, feed_gain_part, mixed_grad, *feed_out = plane_stage(
        5,
        feed_in,
        [residual, cotangent_own, gain_two],
        residual_grad_body,
        [((rows, width), f32), ((8, width), f32)],
        True,
        (hidden, down_line),
    )
    mixed_other = to_sibling(mixed_grad)
    feed_outs = [feed_out[0]] + [send_on(feed_out[k], k) for k in (1, 2, 3)]

    mixed_grad, down_sums = lax.optimization_barrier((mixed_grad, down_sums))
    heads_grad = plain("td,fd->tf", mixed_grad, out_weight).reshape(blocked)
    head_gain_part = jnp.sum(unit_heads * heads_grad, axis=(0, 1))
    scaled_heads = heads_grad * head_gain_f
    out_back = (
        head_factor
        * (scaled_heads - unit_heads * jnp.mean(unit_heads * scaled_heads, axis=-1, keepdims=True))
    ).astype(bf16)
    out_back_f = out_back.astype(f32)
    mixing_grad = plain("btd,bsd->bts", out_back, value) * same
    local_value = plain("bts,btd->bsd", mixing, out_back)
    lifted_grad = grow * precise("bts,bsm->btm", mixing_grad, back) + grow * fresh * precise(
        "btd,bmd->btm", out_back_f, value_state
    )
    score_grad = probs * (lifted_grad - jnp.sum(probs * lifted_grad, axis=-1, keepdims=True))
    inner_grad = grow * score_grad
    state_grad = inner_grad * fresh
    affinity_grad = (precise("btm,bsm->bts", inner_grad, back) * same).astype(bf16)
    first_key = precise("btm,btd->bmd", state_grad, query_f)
    first_value = precise("btm,btd->bmd", entry, out_back_f)
    out_part = chip_sum(core, heads_cut, mixed_grad, heads_other, mixed_other)
    out_part = out_part.reshape(quarter, HEADS, strip, width)
    later_key, later_value, out_part = carry_states(
        6, first_key, first_value, carried, planes, True, out_part
    )
    later_key, feed_outs = lax.optimization_barrier((later_key, feed_outs))

    query_back = plain("bts,bsd->btd", affinity_grad, key) + precise(
        "btm,bmd->btd", state_grad, key_state
    )
    key_back = plain("bts,btd->bsd", affinity_grad, query) + precise(
        "bsm,bmd->bsd", weights, later_key
    )
    value_back = local_value + precise("bsm,bmd->bsd", weights, later_value)
    backs = jnp.concatenate(
        [
            x.astype(bf16).reshape(HEADS * rows, head_size)
            for x in (query_back, key_back, value_back)
        ],
        axis=1,
    )
    backs_other = to_sibling(backs)
    mixer_part = chip_sum(core, h1, backs, h1_other, backs_other, out_part)
    (down_grad,) = return_columns(8, down_sums, 1, part, planes)
    mixer_part, feed_sums, backs, down_grad = lax.optimization_barrier(
        (mixer_part, feed_sums, backs, down_grad)
    )
    mixer_sums = scatter_column(mixer_part)
    mixer_in = plain("tf,df->td", backs, mixer_weight).astype(bf16)
    input_grad, mixer_gain_part, block_out = plane_stage(
        7,
        mixer_in,
        [tokens_own, residual_grad, gain_one, residual, *feed_outs],
        last_body(planes),
        [((rows, width), f32), ((8, width), f32), ((rows, width), bf16)],
        False,
    )

    head_whole = lax.dynamic_update_slice(
        jnp.zeros((width,), f32), head_gain_part, (h * head_size,)
    )
    gain_parts = jnp.stack(
        [
            restored(jnp.sum(mixer_gain_part, axis=0)),
            head_whole,
            restored(jnp.sum(feed_gain_part, axis=0)),
        ]
    )
    gain_parts = gain_parts.reshape(3, count, strip).swapaxes(0, 1)
    gain_parts = jnp.pad(gain_parts, ((0, 0), (0, 5), (0, 128 - strip)))
    gate_grad, up_grad, gain_sums = return_columns(9, feed_sums, 2, part, planes, gain_parts)
    down_grad, gate_grad, up_grad, input_grad, block_out = finished(
        [down_grad, gate_grad, up_grad], [input_grad, block_out]
    )
    mixer_sums, _ = lax.optimization_barrier((mixer_sums, block_out))
    query_grad, key_grad, value_grad, output_grad = return_columns(
        10, mixer_sums, 3, head_size, planes, None, True
    )
    query_grad, key_grad, value_grad, output_grad = finished(
        [query_grad, key_grad, value_grad, output_grad], []
    )
    gain_sums = gain_sums[:3, :strip]
    return (
        block_out,
        input_grad,
        gain_sums[0],
        query_grad,
        key_grad,
        value_grad,
        gain_sums[1],
        output_grad,
        gain_sums[2],
        gate_grad,
        up_grad,
        down_grad,
    )


def solution(mesh):
    split, line = P("seq", None), P("seq")
    return jax.shard_map(
        local,
        mesh=mesh,
        in_specs=(split, split, split, P(), line, split, split, split, line, split, line, split, split, split),
        out_specs=(split, split, line, split, split, split, line, split, line, split, split, split),
        check_vma=False,
    )
```

```python
import jax
import jax.numpy as jnp
from jax import lax
from jax.experimental import pallas as pl
from jax.experimental.pallas import tpu as pltpu
from jax.sharding import PartitionSpec as P

HEADS = 4
SLOTS = 64
PLANE = 8

epsilon = 1e-06
highest = lax.Precision.HIGHEST
bf16 = jnp.bfloat16
f32 = jnp.float32
MESH = pl.DeviceIdType.MESH
ANY = pl.BlockSpec(memory_space=pl.ANY)


def lasting(us):
    return pl.CostEstimate(flops=0, bytes_accessed=us * 3_400_000, transcendentals=0)


def chip_of(me):
    return lax.rem(lax.div(me, 2), HEADS)


def chip_on(me, h, k):
    turn = (k % 2) * (1 - 2 * lax.rem(h, 2)) + (k // 2) * (2 - 4 * lax.div(h, 2))
    return me + 2 * turn, h + turn


def rows_at(ref, block, size):
    return ref.at[pl.ds(pl.multiple_of(block * size, size), size)]


def columns_at(ref, block, size):
    return ref.at[:, pl.ds(pl.multiple_of(block * size, 128), size)]


def opening(cid, gains, codes, weights, output_rows, feed, tokens, planes):
    strip, width = weights[0].shape
    part = width // HEADS
    feed_part = feed[0].shape[1] // HEADS
    count = planes * PLANE
    hops = planes - 1

    tokens_rows = tokens.shape[0]

    def kernel(g0_in, g1_in, g2_in, codes_in, q_far, k_far, v_far, o_in, gate_far, up_far, down_far, t_in,
               g_out, c_out, line_out, feed_far_out, down_far_out, t_out, gain, t_mine, g_in, c_in, q_in, k_in, v_in,
               gate_in, up_in, down_in, line, feed_out, down_out, w_sem, load, t_send, t_recv, own_sem, q_send, q_recv, side_send, side_recv, u_send, u_recv, d_send, d_recv, s_send, s_recv):
        me = lax.axis_index("seq")
        h = chip_of(me)
        core = lax.rem(me, 2)
        z = lax.div(me, PLANE)
        sibling = me + 1 - 2 * core
        chips = [(None, h)] + [chip_on(me, h, k) for k in (1, 2, 3)]
        everyone = [lax.rem(me + k, count) for k in range(1, count)]
        far = (q_far, k_far, v_far, gate_far, up_far, down_far)
        near = (q_in, k_in, v_in, gate_in, up_in, down_in)
        loads = [pltpu.make_async_copy(a, b, load.at[n]) for n, (a, b) in enumerate(zip(far, near))]
        for copy in loads:
            copy.start()
        barrier = pltpu.get_barrier_semaphore()
        for device in everyone:
            pl.semaphore_signal(barrier, inc=1, device_id=(device,), device_id_type=MESH)
        g_in[...] = jnp.zeros_like(g_in)
        for n, ref in enumerate((g0_in, g1_in, g2_in)):
            g_in[n : n + 1, 0:strip] = ref[...].astype(f32)
        for k in range(HEADS):
            c_in[k] = codes_in[:, pl.ds(k * SLOTS, SLOTS)]
        for copy in loads[:3]:
            copy.wait()
        pl.semaphore_wait(barrier, count - 1)

        def remote(src, dst, s, r, device):
            return pltpu.make_async_remote_copy(
                src_ref=src, dst_ref=dst, send_sem=s, recv_sem=r, device_id=(device,), device_id_type=MESH
            )

        def row(plane, chip):
            return pl.ds(pl.multiple_of(((core * planes + plane) * HEADS + chip) * strip, strip), strip)

        def unit(plane, k):
            return line.at[row(plane, chips[k][1]), pl.ds(0, 3 * part)]

        def stack(plane):
            at = pl.multiple_of((core * planes + plane) * HEADS * strip, strip)
            return line.at[pl.ds(at, HEADS * strip), pl.ds(3 * part, part)]

        def stack_up(d):
            n = hops * HEADS + d - 1
            return remote(stack(z - d + 1), stack(z - d + 1), u_send.at[n], u_recv.at[n], me + PLANE)

        def stack_down(d):
            n = hops * HEADS + d - 1
            return remote(stack(z + d - 1), stack(z + d - 1), d_send.at[n], d_recv.at[n], me - PLANE)

        def stack_across(plane):
            n = planes * HEADS + plane
            return remote(stack(plane), stack(plane), s_send.at[n], s_recv.at[n], sibling)

        def up(d, k):
            n = (d - 1) * HEADS + k
            return remote(unit(z - d + 1, k), unit(z - d + 1, k), u_send.at[n], u_recv.at[n], me + PLANE)

        def down(d, k):
            n = (d - 1) * HEADS + k
            return remote(unit(z + d - 1, k), unit(z + d - 1, k), d_send.at[n], d_recv.at[n], me - PLANE)

        def across(plane, k):
            n = plane * HEADS + k
            return remote(unit(plane, k), unit(plane, k), s_send.at[n], s_recv.at[n], sibling)

        def pass_on(k):
            @pl.when(z + 1 < planes)
            def _():
                up(1, k).start()

            @pl.when(z >= 1)
            def _():
                down(1, k).start()

            across(z, k).start()

        projections = []
        for k in (3, 1, 2):
            device, chip = chips[k]
            for j, w in enumerate((q_in, k_in, v_in)):
                n = 3 * (k - 1) + j
                dst = line.at[row(z, h), pl.ds(j * part, part)]
                projections.append((k, remote(columns_at(w, chip, part), dst, q_send.at[n], q_recv.at[n], device)))
        own = [
            pltpu.make_async_copy(
                columns_at(w, h, part), line.at[row(z, h), pl.ds(j * part, part)], own_sem.at[j]
            )
            for j, w in enumerate((q_in, k_in, v_in))
        ]
        for _, copy in projections:
            copy.start()
        for copy in own:
            copy.start()
        turned = reorder(o_in[...], planes, False)
        for k in range(HEADS):
            line[row(z, k), pl.ds(3 * part, part)] = turned[:, k * part : (k + 1) * part]

        @pl.when(z + 1 < planes)
        def _():
            stack_up(1).start()

        @pl.when(z >= 1)
        def _():
            stack_down(1).start()

        stack_across(z).start()
        for copy in own:
            copy.wait()
        pass_on(0)

        shared = [(g_in, g_out.at[me], device) for device in everyone]
        sides = [(c_in.at[chip], c_out.at[k], device) for k, (device, chip) in list(enumerate(chips))[1:]]
        at = pl.ds(pl.multiple_of(h * strip, strip), strip)
        for src, out, column in ((gate_in, feed_out, 0), (up_in, feed_out, feed_part), (down_in, down_out, 0)):
            for device, chip in chips[1:] + chips[:1]:
                dst = out.at[at, pl.ds(column, feed_part)]
                sides.append((columns_at(src, chip, feed_part), dst, device))
        sides.append((c_in.at[h], c_out.at[0], None))
        begun = []

        def begin(listed):
            for src, dst, device in listed:
                n = len(begun)
                if device is None:
                    copy = pltpu.make_async_copy(src, dst, side_send.at[n])
                else:
                    copy = remote(src, dst, side_send.at[n], side_recv.at[n], device)
                copy.start()
                begun.append(copy)

        begin(shared)
        g_out[me] = g_in[...]
        for k in (1, 2, 3):
            for other, copy in projections:
                if other == k:
                    copy.wait_recv()
            pass_on(k)
        for copy in begun:
            copy.wait()
        shares = begun[:]
        gain[...] = jnp.concatenate(
            [
                g_out[(p * PLANE + c * 2 + k), 0:1, 0:strip]
                for k in range(2)
                for p in range(planes)
                for c in range(HEADS)
            ],
            axis=1,
        )

        def step(i, carry):
            at = pl.ds(pl.multiple_of(i * STEP, STEP), STEP)
            x = t_in[at, :].astype(f32)
            t_mine[at, :] = (reorder(x * factor_of(x), planes, False) * gain[...]).astype(bf16)
            return carry

        half = tokens_rows // 2
        low, high = pl.ds(0, half), pl.ds(half, half)
        x_side, y_side = chips[1][0], chips[2][0]

        def spread_out(mine, everything, sends, recvs):
            def block(k, first):
                return everything.at[pl.ds(k * tokens_rows + (0 if first else half), half)]

            copies = [
                remote(mine.at[low], block(1, True), sends.at[0], recvs.at[0], x_side),
                remote(mine.at[high], block(2, False), sends.at[1], recvs.at[1], y_side),
                remote(mine.at[high], block(1, False), sends.at[2], recvs.at[2], x_side),
                remote(mine.at[low], block(2, True), sends.at[3], recvs.at[3], y_side),
                remote(block(1, True), block(3, True), sends.at[4], recvs.at[4], y_side),
                remote(block(2, False), block(3, False), sends.at[5], recvs.at[5], x_side),
            ]
            keep = pltpu.make_async_copy(mine, everything.at[pl.ds(0, tokens_rows)], sends.at[6])
            for copy in copies[:4]:
                copy.start()
            keep.start()
            return copies, keep

        def relay(copies):
            copies[0].wait_recv()
            copies[4].start()
            copies[1].wait_recv()
            copies[5].start()

        def finish(copies, keep):
            for copy in copies[:2]:
                copy.wait_send()
            for copy in copies[2:]:
                copy.wait()
            keep.wait()

        lax.fori_loop(0, tokens_rows // STEP, step, 0)
        spread_t = spread_out(t_mine, t_out, t_send, t_recv)
        for copy in loads[3:]:
            copy.wait()
        begin(sides)
        for d in range(1, planes):

            @pl.when(z - d >= 0)
            def _(d=d):
                stack_up(d).wait_recv()

                @pl.when(z + 1 < planes)
                def _():
                    stack_up(d + 1).start()

                stack_across(z - d).start()

            @pl.when(z + d < planes)
            def _(d=d):
                stack_down(d).wait_recv()

                @pl.when(z >= 1)
                def _():
                    stack_down(d + 1).start()

                stack_across(z + d).start()

            for k in range(HEADS):

                @pl.when(z - d >= 0)
                def _(d=d, k=k):
                    up(d, k).wait_recv()

                    @pl.when(z + 1 < planes)
                    def _():
                        up(d + 1, k).start()

                    across(z - d, k).start()

                @pl.when(z + d < planes)
                def _(d=d, k=k):
                    down(d, k).wait_recv()

                    @pl.when(z >= 1)
                    def _():
                        down(d + 1, k).start()

                    across(z + d, k).start()

            if d == 1:
                relay(spread_t[0])
        def written(side, n):
            at = pl.ds(pl.multiple_of(side * (planes * HEADS * strip), strip), planes * HEADS * strip)
            return pltpu.make_async_copy(line.at[at], line_out.at[at], w_sem.at[n])

        writes = [written(core, 0)]
        writes[0].start()
        for _, copy in projections:
            copy.wait_send()
        finish(*spread_t)
        for copy in begun[len(shares) :]:
            copy.wait()
        writes += [
            pltpu.make_async_copy(feed_out, feed_far_out, w_sem.at[1]),
            pltpu.make_async_copy(down_out, down_far_out, w_sem.at[2]),
        ]
        for copy in writes[1:]:
            copy.start()
        for d in range(1, planes):

            @pl.when((z - d + 1 >= 0) & (z + 1 < planes))
            def _(d=d):
                stack_up(d).wait_send()
                for k in range(HEADS):
                    up(d, k).wait_send()

            @pl.when((z + d - 1 < planes) & (z >= 1))
            def _(d=d):
                stack_down(d).wait_send()
                for k in range(HEADS):
                    down(d, k).wait_send()

        for plane in range(planes):
            stack_across(plane).wait()
            for k in range(HEADS):
                across(plane, k).wait()
        writes.append(written(1 - core, 3))
        writes[-1].start()
        for copy in writes:
            copy.wait()

    sides = count + 4 + 12
    vmem = pl.BlockSpec(memory_space=pltpu.VMEM)
    sizes = (6, 7, 6, 3, 9, 9, sides, sides) + (hops * (HEADS + 1),) * 4 + (planes * (HEADS + 1),) * 2
    shares = jax.ShapeDtypeStruct((count, 8, 128), f32)
    logits = jax.ShapeDtypeStruct((HEADS, tokens_rows, SLOTS), codes.dtype)
    return pl.pallas_call(
        kernel,
        out_shape=[
            shares,
            logits,
            jax.ShapeDtypeStruct((count * strip, 4 * part), bf16),
            jax.ShapeDtypeStruct((HEADS * strip, 2 * feed_part), bf16),
            jax.ShapeDtypeStruct((HEADS * strip, feed_part), bf16),
            jax.ShapeDtypeStruct((HEADS * tokens_rows, width), bf16),
        ],
        in_specs=[vmem] * 4 + [ANY] * 3 + [vmem] + [ANY] * 3 + [vmem],
        out_specs=[vmem] * 2 + [ANY] * 4,
        scratch_shapes=[
            pltpu.VMEM((1, width), f32),
            pltpu.VMEM(tokens.shape, bf16),
            pltpu.VMEM((8, 128), f32),
            pltpu.VMEM((HEADS, tokens_rows, SLOTS), codes.dtype),
        ]
        + [pltpu.VMEM(x.shape, bf16) for x in (*weights, *feed)]
        + [
            pltpu.VMEM((count * strip, 4 * part), bf16),
            pltpu.VMEM((HEADS * strip, 2 * feed_part), bf16),
            pltpu.VMEM((HEADS * strip, feed_part), bf16),
            pltpu.SemaphoreType.DMA((4,)),
        ]
        + [pltpu.SemaphoreType.DMA((n,)) for n in sizes],
        compiler_params=pltpu.CompilerParams(
            collective_id=cid, has_side_effects=True, vmem_limit_bytes=58 << 20
        ),
        cost_estimate=lasting(85),
    )(*(g[None] for g in gains), codes, *weights, output_rows, *feed, tokens)


def return_columns(cid, x, pieces, part, planes, gains=None, own_rows=False):
    rows = x.shape[0] // HEADS
    shared = gains is not None
    count = planes * PLANE

    def kernel(*refs):
        src, refs = refs[0], refs[1:]
        shares, refs = (refs[0], refs[1:]) if shared else (None, refs)
        outs, refs = refs[:pieces], refs[pieces:]
        extra, refs = (refs[0], refs[1:]) if own_rows else (None, refs)
        gain_out, refs = (refs[0], refs[1:]) if shared else (None, refs)
        send, recv, gain_in, gain_send, gain_recv, tail, tail_sem = refs
        me = lax.axis_index("seq")
        h = chip_of(me)
        targets = [chip_on(me, h, k) for k in (3, 1, 2)]
        everyone = [lax.rem(me + k, count) for k in range(1, count)]
        peers = everyone if shared else [device for device, _ in targets]
        barrier = pltpu.get_barrier_semaphore()
        for device in peers:
            pl.semaphore_signal(barrier, inc=1, device_id=(device,), device_id_type=MESH)
        pl.semaphore_wait(barrier, len(peers))

        def to(device, source, dst, sends, recvs, n):
            return pltpu.make_async_remote_copy(
                src_ref=source, dst_ref=dst, send_sem=sends.at[n], recv_sem=recvs.at[n],
                device_id=(device,), device_id_type=MESH,
            )

        def place(j):
            return columns_at(outs[j], h, part)

        copies = []
        for k, (device, other) in enumerate(targets):
            for j in range(pieces):
                source = src.at[
                    pl.ds(pl.multiple_of(other * rows, rows), rows), pl.ds(j * part, part)
                ]
                copies.append(to(device, source, place(j), send, recv, k * pieces + j))
        if shared:
            for n, device in enumerate(everyone):
                copies.append(to(device, shares.at[device], gain_in.at[me], gain_send, gain_recv, n))
        own = pl.ds(pl.multiple_of(h * rows, rows), rows)
        for j in range(pieces):
            copies.append(
                pltpu.make_async_copy(src.at[own, pl.ds(j * part, part)], place(j), send.at[3 * pieces + j])
            )
        for copy in copies:
            copy.start()
        if shared:
            gain_in[me] = shares[me]
        if own_rows:
            fetch = pltpu.make_async_copy(src.at[:, pl.ds(pieces * part, part)], tail, tail_sem.at[0])
            fetch.start()
            fetch.wait()
            blocks = [tail[pl.ds(k * rows, rows), :] for k in range(HEADS)]
            extra[...] = reorder(jnp.concatenate(blocks, axis=1), planes, True)
        for copy in copies:
            copy.wait()
        if shared:
            total = gain_in[0]
            for k in range(1, count):
                total = total + gain_in[k]
            gain_out[...] = total

    vmem = pl.BlockSpec(memory_space=pltpu.VMEM)
    shapes = [jax.ShapeDtypeStruct((rows, HEADS * part), bf16)] * (pieces + int(own_rows))
    shapes += [jax.ShapeDtypeStruct((8, 128), f32)] * int(shared)
    return pl.pallas_call(
        kernel,
        out_shape=shapes,
        in_specs=[ANY if own_rows else vmem] + [vmem] * int(shared),
        out_specs=[vmem] * len(shapes),
        scratch_shapes=[
            pltpu.SemaphoreType.DMA((4 * pieces,)),
            pltpu.SemaphoreType.DMA((3 * pieces,)),
            pltpu.VMEM((count if shared else 1, 8, 128), f32),
            pltpu.SemaphoreType.DMA((count if shared else 1,)),
            pltpu.SemaphoreType.DMA((count if shared else 1,)),
            pltpu.VMEM((x.shape[0], part) if own_rows else (16, 128), bf16),
            pltpu.SemaphoreType.DMA((1,)),
        ],
        compiler_params=pltpu.CompilerParams(
            collective_id=cid, has_side_effects=True, vmem_limit_bytes=40 << 20
        ),
        cost_estimate=lasting(14),
    )(*([x, gains] if shared else [x]))


def finished(narrow, others):
    arrays = [*narrow, *others]
    kinds = [f32] * len(narrow) + [x.dtype for x in others]

    def kernel(*refs):
        for src, dst in zip(refs[: len(arrays)], refs[len(arrays) :]):
            dst[...] = src[...].astype(dst.dtype)

    specs = [pl.BlockSpec((x.shape[0] // 2, x.shape[1]), lambda i: (i, 0)) for x in arrays]
    if any(x.shape[0] % 32 for x in arrays):
        specs = [pl.BlockSpec(x.shape, lambda i: (0, 0)) for x in arrays]
    return pl.pallas_call(
        kernel,
        out_shape=[jax.ShapeDtypeStruct(x.shape, kind) for x, kind in zip(arrays, kinds)],
        grid=(2 if specs[0].block_shape[0] < arrays[0].shape[0] else 1,),
        in_specs=specs,
        out_specs=specs,
        compiler_params=pltpu.CompilerParams(vmem_limit_bytes=40 << 20),
        cost_estimate=lasting(3),
    )(*arrays)


STEP = 16


def reorder(x, planes, back):
    chips = planes * HEADS
    strip = x.shape[1] // (2 * chips)
    pieces = []
    for i in range(2 * chips):
        n = (i % 2) * chips + i // 2 if back else (i % chips) * 2 + i // chips
        pieces.append(x[:, n * strip : (n + 1) * strip])
    return jnp.concatenate(pieces, axis=1)


def reordered(arrays, planes):
    def kernel(*refs):
        for src, dst in zip(refs[: len(arrays)], refs[len(arrays) :]):

            def step(i, carry, src=src, dst=dst):
                at = pl.ds(pl.multiple_of(i * STEP, STEP), STEP)
                dst[at, :] = reorder(src[at, :], planes, False)
                return carry

            lax.fori_loop(0, src.shape[0] // STEP, step, 0)

    vmem = pl.BlockSpec(memory_space=pltpu.VMEM)
    return pl.pallas_call(
        kernel,
        out_shape=[jax.ShapeDtypeStruct(x.shape, x.dtype) for x in arrays],
        in_specs=[vmem] * len(arrays),
        out_specs=[vmem] * len(arrays),
        compiler_params=pltpu.CompilerParams(vmem_limit_bytes=32 << 20),
    )(*arrays)


def plane_stage(cid, partial, blocks, body, own, gathered, product=None):
    rows, width = blocks[0].shape
    half = rows // 2
    has = int(partial is not None)
    low, high = pl.ds(0, half), pl.ds(half, half)

    def kernel(*refs):
        part = refs[0] if has else None
        block_refs = refs[has : has + len(blocks)]
        rest = refs[has + len(blocks) :]
        factors, rest = (rest[:2], rest[2:]) if product else (None, rest)
        own_refs, rest = rest[: len(own)], rest[len(own) :]
        everything, rest = (rest[0], rest[1:]) if gathered else (None, rest)
        results, rest = (rest[:HEADS], rest[HEADS:]) if product else (None, rest)
        (left, right, load), rest = (rest[:3], rest[3:]) if product else ((None,) * 3, rest)
        by_x, by_y, over_x, over_y, sum_x, sum_y, mine, send, recv, out_send, out_recv = rest
        me = lax.axis_index("seq")
        h = chip_of(me)
        x_side, y_side = chip_on(me, h, 1)[0], chip_on(me, h, 2)[0]
        barrier = pltpu.get_barrier_semaphore()
        for device in (x_side, y_side):
            pl.semaphore_signal(barrier, inc=1, device_id=(device,), device_id_type=MESH)
        pl.semaphore_wait(barrier, 2)

        def to(device, src, dst, sends, recvs, n):
            return pltpu.make_async_remote_copy(
                src_ref=src, dst_ref=dst, send_sem=sends.at[n], recv_sem=recvs.at[n],
                device_id=(device,), device_id_type=MESH,
            )

        def block(k, first):
            return pl.ds(k * rows + (0 if first else half), half)

        loads = []
        if product:
            loads = [
                pltpu.make_async_copy(src, dst, load.at[n])
                for n, (src, dst) in enumerate(zip(factors, (left, right)))
            ]

        def multiply(k):
            if product:
                results[k][...] = lax.dot_general(
                    left[pl.ds(k * rows, rows), :], right[...], (((1,), (1,)), ((), ())),
                    preferred_element_type=f32,
                ).astype(bf16)

        if has:
            copies = [
                to(x_side, part.at[block(3, True)], over_x, send, recv, 0),
                to(y_side, part.at[block(3, False)], over_y, send, recv, 1),
                to(x_side, part.at[block(1, True)], by_x.at[low], send, recv, 2),
                to(y_side, part.at[block(2, False)], by_y.at[high], send, recv, 3),
                to(y_side, sum_y, by_y.at[low], send, recv, 4),
                to(x_side, sum_x, by_x.at[high], send, recv, 5),
            ]
            for copy in copies[:4]:
                copy.start()
            for copy in loads:
                copy.start()
            for copy in loads:
                copy.wait()
            multiply(0)
            copies[0].wait_recv()
            sum_y[...] = (part[block(2, True), :].astype(f32) + over_x[...].astype(f32)).astype(bf16)
            copies[4].start()
            copies[1].wait_recv()
            sum_x[...] = (part[block(1, False), :].astype(f32) + over_y[...].astype(f32)).astype(bf16)
            copies[5].start()
            multiply(1)
            for copy in copies[:2]:
                copy.wait_send()
            for copy in copies[2:]:
                copy.wait()

        def step(i, carry):
            at = pl.ds(pl.multiple_of(i * STEP, STEP), STEP)
            total = None
            if has:
                total = part[at, :].astype(f32) + by_x[at, :].astype(f32) + by_y[at, :].astype(f32)
            body(i, at, total, block_refs, own_refs, mine)
            return carry

        lax.fori_loop(0, rows // STEP, step, 0)
        if gathered:
            from_x, from_y = everything.at[block(1, True)], everything.at[block(2, False)]
            copies = [
                to(x_side, mine.at[low], from_x, out_send, out_recv, 0),
                to(y_side, mine.at[high], from_y, out_send, out_recv, 1),
                to(x_side, mine.at[high], everything.at[block(1, False)], out_send, out_recv, 2),
                to(y_side, mine.at[low], everything.at[block(2, True)], out_send, out_recv, 3),
                to(y_side, from_x, everything.at[block(3, True)], out_send, out_recv, 4),
                to(x_side, from_y, everything.at[block(3, False)], out_send, out_recv, 5),
            ]
            keep = pltpu.make_async_copy(mine, everything.at[pl.ds(0, rows)], out_send.at[6])
            for copy in copies[:4]:
                copy.start()
            keep.start()
            multiply(2)
            copies[0].wait_recv()
            copies[4].start()
            copies[1].wait_recv()
            copies[5].start()
            multiply(3)
            for copy in copies[:2]:
                copy.wait_send()
            for copy in copies[2:]:
                copy.wait()
            keep.wait()

    vmem = pl.BlockSpec(memory_space=pltpu.VMEM)
    shapes = [jax.ShapeDtypeStruct(s, d) for s, d in own]
    if gathered:
        shapes.append(jax.ShapeDtypeStruct((HEADS * rows, width), bf16))
    factors_in, loaded = [], []
    if product:
        shapes += [jax.ShapeDtypeStruct((rows, width), bf16)] * HEADS
        factors_in = list(product)
        loaded = [pltpu.VMEM(x.shape, x.dtype) for x in product] + [pltpu.SemaphoreType.DMA((2,))]
    whole, part_of = ((rows, width), (half, width)) if has else ((STEP, 128), (STEP, 128))
    return pl.pallas_call(
        kernel,
        out_shape=shapes,
        in_specs=[vmem] * (has + len(blocks)) + [ANY] * len(factors_in),
        out_specs=[vmem] * len(own) + [ANY] * int(gathered) + [vmem] * (HEADS if product else 0),
        scratch_shapes=loaded + [pltpu.VMEM(s, bf16) for s in (whole, whole, part_of, part_of, part_of, part_of)]
        + [pltpu.VMEM((rows, width), bf16)]
        + [pltpu.SemaphoreType.DMA((n,)) for n in (6, 6, 7, 6)],
        compiler_params=pltpu.CompilerParams(
            collective_id=cid, has_side_effects=True, vmem_limit_bytes=40 << 20
        ),
        cost_estimate=lasting(25 * has + 25 * int(gathered)),
    )(*([partial] if has else []), *blocks, *factors_in)


def chip_sum(core, left, right, other_left, other_right, extra=None):
    tokens, columns = right.shape
    half = left.shape[1] // 2
    block = min(half, 256)
    steps = half // block
    more = 0 if extra is None else extra.shape[1]
    contract = (((0,), (0,)), ((), ()))
    pieces = 2 if columns % 256 == 0 and columns > 2048 else 1
    size = columns // pieces

    def kernel(which, a, b, c, d, *rest):
        out = rest[-1]
        for n in range(pieces):
            at = pl.ds(n * size, size)
            total = lax.dot_general(a[...], b[:, at], contract, preferred_element_type=f32)
            total += lax.dot_general(c[...], d[:, at], contract, preferred_element_type=f32)
            out[:, at] = total.astype(bf16)
        if more:
            out[:, pl.ds(columns, more)] = rest[0][...]

    whole = pl.BlockSpec((tokens, columns), lambda i, w: (0, 0), pipeline_mode=pl.Buffered(1))
    specs = [
        pl.BlockSpec((tokens, block), lambda i, w: (0, w[0] * steps + i)),
        whole,
        pl.BlockSpec((tokens, block), lambda i, w: (0, i)),
        whole,
    ]
    if more:
        specs.append(pl.BlockSpec((block, more), lambda i, w: (i, 0)))
    return pl.pallas_call(
        kernel,
        out_shape=jax.ShapeDtypeStruct((half, columns + more), bf16),
        grid_spec=pltpu.PrefetchScalarGridSpec(
            num_scalar_prefetch=1,
            grid=(steps,),
            in_specs=specs,
            out_specs=pl.BlockSpec((block, columns + more), lambda i, w: (i, 0)),
        ),
        compiler_params=pltpu.CompilerParams(vmem_limit_bytes=40 << 20),
        cost_estimate=pl.CostEstimate(
            flops=4 * tokens * half * columns,
            bytes_accessed=4 * tokens * (half + columns) + 2 * half * columns,
            transcendentals=0,
        ),
    )(core.reshape(1), left, right, other_left, other_right, *(() if extra is None else (extra,)))


def factor_of(x):
    return lax.rsqrt(jnp.mean(x * x, axis=-1, keepdims=True) + epsilon)


def residual_body(i, at, total, blocks, own, mine):
    tokens, gain = blocks
    x = tokens[at, :].astype(f32) + total
    own[0][at, :] = x
    mine[at, :] = (x * factor_of(x) * gain[...]).astype(bf16)


def accumulate(i, ref, product):
    part = product[:8] + product[8:]

    @pl.when(i == 0)
    def _():
        ref[...] = part

    @pl.when(i > 0)
    def _():
        ref[...] += part


def residual_grad_body(i, at, total, blocks, own, mine):
    residual, cotangent, gain = blocks
    x = residual[at, :]
    factor = factor_of(x)
    normed = x * factor
    accumulate(i, own[1], normed * total)
    scaled = total * gain[...]
    grad = cotangent[at, :].astype(f32) + factor * (
        scaled - normed * jnp.mean(normed * scaled, axis=-1, keepdims=True)
    )
    own[0][at, :] = grad
    mine[at, :] = grad.astype(bf16)


def last_body(planes):
    def body(i, at, total, blocks, own, mine):
        tokens, later, gain, residual, *outs = blocks
        x = tokens[at, :].astype(f32)
        factor = factor_of(x)
        normed = x * factor
        accumulate(i, own[1], normed * total)
        scaled = total * gain[...]
        grad = later[at, :] + factor * (
            scaled - normed * jnp.mean(normed * scaled, axis=-1, keepdims=True)
        )
        own[0][at, :] = reorder(grad, planes, True)
        result = residual[at, :]
        for out in outs:
            result = result + out[at, :].astype(f32)
        own[2][at, :] = reorder(result.astype(bf16), planes, True)

    return body


def carry_states(cid, keys, values, gains, planes, reverse, rows_out=None, line=None):
    lined = line is not None
    more = int(rows_out is not None or lined)
    sent = bf16 if reverse else f32
    _, slots, size = keys.shape
    half = slots // 2
    if lined:
        quarter, strip = planes // HEADS, line.shape[0] // (planes * PLANE)
        landing, result = (HEADS, 2 * quarter, HEADS * strip, size), (size, HEADS * size)
        links = 2 * quarter
    elif more:
        quarter, _, strip, _ = rows_out.shape
        landing, result = (HEADS, quarter, strip, HEADS * size), (HEADS * quarter * HEADS * strip, size)
        links = quarter

    def kernel(k_in, v_in, g_in, *refs):
        r_in, refs = (refs[0], refs[1:]) if more else (None, refs)
        k_out, v_out, refs = refs[0], refs[1], refs[2:]
        r_out, refs = (refs[0], refs[1:]) if more else (None, refs)
        r_all, r_send, r_recv, refs = (*refs[:3], refs[3:]) if more else (None, None, None, refs)
        main(k_in, v_in, g_in, k_out, v_out, *refs, r_in=r_in, r_out=r_out, r_all=r_all, r_send=r_send, r_recv=r_recv)

    def main(k_in, v_in, g_in, k_out, v_out, k_all, v_all, g_all, k_pre, v_pre, g_pre, k_run, v_run, g_run,
               k_far, v_far, g_far, k_base, v_base, k_mine, v_mine, s_send, s_recv, z_send, z_recv, b_send, b_recv,
             *, r_in, r_out, r_all, r_send, r_recv):
        me = lax.axis_index("seq")
        h = chip_of(me)
        core = lax.rem(me, 2)
        z = lax.div(me, PLANE)
        sibling = me + 1 - 2 * core
        barrier = pltpu.get_barrier_semaphore()
        others = [me + PLANE * (lax.rem(z + k, planes) - z) for k in range(1, planes)]
        chips = [chip_on(me, h, k) for k in (1, 2, 3)]
        greeted = [sibling, *others] + ([device for device, _ in chips] if more else [])
        for device in greeted:
            pl.semaphore_signal(barrier, inc=1, device_id=(device,), device_id_type=MESH)
        pl.semaphore_wait(barrier, len(greeted))

        def remote(src, dst, s, r, device):
            return pltpu.make_async_remote_copy(
                src_ref=src, dst_ref=dst, send_sem=s, recv_sem=r, device_id=(device,), device_id_type=MESH
            )

        k_base[...] = jnp.zeros_like(k_base)
        v_base[...] = jnp.zeros_like(v_base)
        copies = []
        for k in range(HEADS):
            chip = chip_on(me, h, k)[1]
            for j, (src, dst) in enumerate(((g_in, g_all), (k_in, k_all), (v_in, v_all))):
                n = 3 * k + j
                copies.append(remote(src.at[k], dst.at[chip, core], s_send.at[n], s_recv.at[n], sibling))
        for copy in copies:
            copy.start()
        swaps = []

        def sent_rows(chip, n):
            if not lined:
                return r_in.at[n, chip]
            at = ((n // quarter * planes) + chip * quarter + n % quarter) * HEADS * strip
            return r_in.at[pl.ds(pl.multiple_of(at, HEADS * strip), HEADS * strip), pl.ds(3 * size, size)]

        if more:
            for n, (device, chip) in enumerate(chips):
                for q in range(links):
                    at = links * n + q
                    swaps.append(
                        remote(sent_rows(chip, q), r_all.at[h, q], r_send.at[at], r_recv.at[at], device)
                    )
            for q in range(links):
                swaps.append(
                    pltpu.make_async_copy(sent_rows(h, q), r_all.at[h, q], r_send.at[3 * links + q])
                )
            for swap in swaps:
                swap.start()
        for k in range(HEADS):
            chip = chip_on(me, h, k)[1]
            for src, dst in ((g_in, g_all), (k_in, k_all), (v_in, v_all)):
                dst[chip, core] = src[k]
        for copy in copies:
            copy.wait()
        k_run[...] = jnp.zeros_like(k_run)
        v_run[...] = jnp.zeros_like(v_run)
        g_run[...] = jnp.ones_like(g_run)
        order = [(c, d) for c in range(HEADS) for d in range(2)]
        for c, d in reversed(order) if reverse else order:
            k_pre[c, d] = k_run[...]
            v_pre[c, d] = v_run[...]
            g_pre[c, d] = g_run[...]
            gain = g_all[c, d]
            k_run[...] = gain[:, :1] * k_run[...] + k_all[c, d]
            v_run[...] = gain[:, :1] * v_run[...] + v_all[c, d]
            g_run[...] = gain * g_run[...]
        mine = pl.ds(pl.multiple_of(core * half, half), half)
        k_mine[...] = k_run[mine, :].astype(sent)
        v_mine[...] = v_run[mine, :].astype(sent)

        def along(k, go):
            step = -PLANE * k if reverse else PLANE * k
            device = me + step if go else me - step
            return [
                remote(src, dst.at[k - 1], z_send.at[n], z_recv.at[n], device)
                for n, src, dst in (
                    (3 * k - 3, g_run.at[mine], g_far),
                    (3 * k - 2, k_mine, k_far),
                    (3 * k - 1, v_mine, v_far),
                )
            ]

        def ahead(k):
            return z - k >= 0 if reverse else z + k < planes

        def behind(k):
            return z + k < planes if reverse else z - k >= 0

        for k in range(1, planes):
            @pl.when(ahead(k))
            def _(k=k):
                for copy in along(k, True):
                    copy.start()

        for k in reversed(range(1, planes)):
            @pl.when(behind(k))
            def _(k=k):
                for copy in along(k, False):
                    copy.wait_recv()
                gain = g_far[k - 1][:, :1]
                k_base[mine, :] = gain * k_base[mine, :] + k_far[k - 1].astype(f32)
                v_base[mine, :] = gain * v_base[mine, :] + v_far[k - 1].astype(f32)

        copies = [
            remote(k_base.at[mine], k_base.at[mine], b_send.at[0], b_recv.at[0], sibling),
            remote(v_base.at[mine], v_base.at[mine], b_send.at[1], b_recv.at[1], sibling),
        ]
        for copy in copies:
            copy.start()
        for copy in copies:
            copy.wait()
        for k in range(HEADS):
            chip = chip_on(me, h, k)[1]
            gain = g_pre[chip, core][:, :1]
            k_out[k] = gain * k_base[...] + k_pre[chip, core]
            v_out[k] = gain * v_base[...] + v_pre[chip, core]
        for swap in swaps:
            swap.wait()
        if lined:
            for c in range(HEADS):
                for n in range(links):
                    for b in range(HEADS):
                        at = ((n % quarter * HEADS + c) * 2 + n // quarter) * strip
                        r_out[pl.ds(at, strip), pl.ds(b * size, size)] = r_all[c, n, pl.ds(b * strip, strip), :]
        elif more:
            for c in range(HEADS):
                for q in range(quarter):
                    for b in range(HEADS):
                        at = ((c * quarter + q) * HEADS + b) * strip
                        r_out[pl.ds(at, strip), :] = r_all[c, q, :, pl.ds(b * size, size)]
        for k in range(1, planes):
            @pl.when(ahead(k))
            def _(k=k):
                for copy in along(k, True):
                    copy.wait_send()

    vmem = pl.BlockSpec(memory_space=pltpu.VMEM)
    wide = [pltpu.VMEM((HEADS, 2, slots, n), f32) for n in (size, size, 128)]
    state = [pltpu.VMEM((slots, n), f32) for n in (size, size, 128)]
    far = [pltpu.VMEM((planes - 1, half, n), d) for n, d in ((size, sent), (size, sent), (128, f32))]
    sends = [pltpu.VMEM((half, size), sent)] * 2
    side = []
    if more:
        side = [pltpu.VMEM(landing, bf16)] + [pltpu.SemaphoreType.DMA((4 * links,))] * 2
    semaphores = [12, 12, 3 * planes - 3, 3 * planes - 3, 2, 2]
    return pl.pallas_call(
        kernel,
        out_shape=[jax.ShapeDtypeStruct(keys.shape, f32)] * 2
        + ([jax.ShapeDtypeStruct(result, bf16)] if more else []),
        in_specs=[vmem] * 3 + [ANY] * more,
        out_specs=[vmem] * (2 + more),
        scratch_shapes=side + wide + wide + state + far + state[:2] + sends
        + [pltpu.SemaphoreType.DMA((n,)) for n in semaphores],
        compiler_params=pltpu.CompilerParams(
            collective_id=cid, has_side_effects=True, vmem_limit_bytes=32 << 20
        ),
        cost_estimate=lasting(22),
    )(keys, values, gains, *([line if lined else rows_out] if more else []))


def rms_factor(value_rows):
    return lax.rsqrt(jnp.mean(value_rows * value_rows, axis=-1, keepdims=True) + epsilon)


def precise(form, left, right):
    return jnp.einsum(form, left, right, precision=highest, preferred_element_type=f32)


def plain(form, left, right):
    return jnp.einsum(form, left, right, preferred_element_type=f32)


def local(
    tokens,
    cotangent,
    gate_codes,
    lengths,
    mixer_gain,
    query_weight,
    key_weight,
    value_weight,
    head_gain,
    output_weight,
    feed_gain,
    gate_weight,
    up_weight,
    down_weight,
):
    count = lax.axis_size("seq")
    planes = count // PLANE
    me = lax.axis_index("seq")
    z, h, core = me // PLANE, (me // 2) % HEADS, me % 2
    rows, width = tokens.shape
    strip = query_weight.shape[0]
    head_size = width // HEADS
    lines = [
        [p * PLANE + c * 2 + k for k in range(2) for p in range(planes)] for c in range(HEADS)
    ]

    def gather_line(x):
        return lax.all_gather(x, "seq", axis=0, tiled=True, axis_index_groups=lines)

    columns = [[p * PLANE + k for p in range(planes)] for k in range(PLANE)]

    def scatter_column(x):
        return lax.psum_scatter(
            x, "seq", scatter_dimension=0, tiled=True, axis_index_groups=columns
        )

    def to_sibling(x):
        return lax.ppermute(x, "seq", [(d, d ^ 1) for d in range(count)])

    def cut(x, side):
        part_width = x.shape[1] // 2
        return lax.dynamic_slice_in_dim(x, (core ^ side) * part_width, part_width, axis=1)


    def shuffled(x):
        y = x.reshape(*x.shape[:-1], planes * HEADS, 2, strip)
        return jnp.swapaxes(y, -3, -2).reshape(x.shape)

    def restored(x):
        y = x.reshape(*x.shape[:-1], 2, planes * HEADS, strip)
        return jnp.swapaxes(y, -3, -2).reshape(x.shape)

    turns = [
        [(d, d - 2 * (d // 2 % HEADS) + 2 * (d // 2 % HEADS ^ k)) for d in range(count)]
        for k in range(HEADS)
    ]

    def send_on(x, k):
        return lax.ppermute(x, "seq", turns[k])

    gains_all, codes_all, mixer_line, feed_rows, down_rows, h1 = opening(
        0,
        (mixer_gain, head_gain, feed_gain),
        gate_codes,
        (query_weight, key_weight, value_weight),
        output_weight,
        (gate_weight, up_weight, down_weight),
        tokens,
        planes,
    )
    feed_weight = gather_line(feed_rows)
    down_line = gather_line(down_rows)
    gain_of = gains_all[:, :3, :strip].swapaxes(0, 1).reshape(3, width)
    gain_one, gain_two = shuffled(gain_of[0])[None], shuffled(gain_of[2])[None]
    head_gain_f = lax.dynamic_slice(gain_of[1], (h * head_size,), (head_size,))

    tokens_own, cotangent_own = reordered([tokens, cotangent], planes)
    h1_other = to_sibling(cut(h1, 1))
    cotangent_parts = [cotangent_own] + [send_on(cotangent_own, k) for k in (1, 2, 3)]

    decay = jax.nn.log_sigmoid(codes_all.astype(f32) / 256.0)
    block = z * PLANE + 2 * ((h ^ jnp.arange(HEADS))) + core
    first = (block * rows)[:, None]
    position = first + jnp.arange(rows)[None, :]
    order = jnp.arange(lengths.shape[0])
    first_token = jnp.sum(
        jnp.where(order[:, None] > order[None, :], lengths[None, :], 0), axis=1
    )
    seen = jnp.sum(
        jnp.where(
            (first_token[None, None, :] <= position[:, :, None])
            & (first_token[None, None, :] >= first[:, :, None]),
            1,
            0,
        ),
        axis=2,
    )
    places = jnp.arange(rows)
    before = places[:, None] >= places[None, :]
    same = jnp.where(before[None] & (seen[:, :, None] == seen[:, None, :]), 1.0, 0.0).astype(f32)
    fresh = jnp.where(seen == 0, 1.0, 0.0).astype(f32)[:, :, None]
    logsum = precise("ts,bsm->btm", before.astype(f32), decay)
    grow = jnp.exp(logsum)
    back = jnp.exp(-logsum) * -jnp.expm1(decay)
    tail = jnp.where(seen == seen[:, -1:], 1.0, 0.0).astype(f32)[:, :, None]
    weights = grow[:, -1:] * back * tail
    carried = fresh[:, -1] * grow[:, -1]
    carried = jnp.broadcast_to(carried[:, :, None], (HEADS, SLOTS, 128))

    blocked = (HEADS, rows, head_size)
    mixer_weight = mixer_line[:, : 3 * head_size]
    projected = jnp.dot(h1, mixer_weight, preferred_element_type=f32).astype(bf16)
    query = projected[:, :head_size].reshape(blocked)
    key = projected[:, head_size : 2 * head_size].reshape(blocked)
    value = projected[:, 2 * head_size :].reshape(blocked)
    query_f = query.astype(f32)

    key_state, value_state, out_weight = carry_states(
        3,
        precise("bsm,bsd->bmd", weights, key.astype(f32)),
        precise("bsm,bsd->bmd", weights, value.astype(f32)),
        carried,
        planes,
        False,
        None,
        mixer_line,
    )

    affinity = plain("btd,bsd->bts", query, key) * same
    score = grow * precise("bts,bsm->btm", affinity, back) + grow * fresh * precise(
        "btd,bmd->btm", query_f, key_state
    )
    probs = jax.nn.softmax(score, axis=-1)
    lifted = probs * grow
    mixing = (precise("btm,bsm->bts", lifted, back) * same).astype(bf16)
    entry = lifted * fresh
    slot_out = plain("bts,bsd->btd", mixing, value) + precise("btm,bmd->btd", entry, value_state)
    head_factor = rms_factor(slot_out)
    unit_heads = slot_out * head_factor
    normed_heads = (unit_heads * head_gain_f).astype(bf16).reshape(HEADS * rows, head_size)

    quarter = planes // HEADS
    mixed = jnp.dot(normed_heads, out_weight, preferred_element_type=f32).astype(bf16)
    residual, h2 = plane_stage(
        4, mixed, [tokens_own, gain_two], residual_body, [((rows, width), f32)], True
    )

    h2, *cotangent_parts = lax.optimization_barrier((h2, *cotangent_parts))
    cotangent_all = jnp.concatenate(cotangent_parts)
    cotangent_other = to_sibling(cut(cotangent_all, 1))
    part = down_line.shape[1]
    both = jnp.dot(h2, feed_weight, preferred_element_type=f32)
    sigma = jax.nn.sigmoid(both[:, :part])
    hidden = (both[:, :part] * sigma * both[:, part:]).astype(bf16)
    hidden, both = lax.optimization_barrier((hidden, both))
    down_part = chip_sum(
        core, cotangent_all, hidden, cotangent_other, to_sibling(hidden)
    )
    down_sums = scatter_column(down_part)
    h2_other = to_sibling(cut(h2, 1))
    (heads_cut,) = reordered([normed_heads], quarter)
    heads_other = to_sibling(cut(heads_cut, 1))
    _, down_line, out_weight, h2_other, heads_other = lax.optimization_barrier(
        (down_part, down_line, out_weight, h2_other, heads_other)
    )
    gate, upward = both[:, :part], both[:, part:]
    sigma = jax.nn.sigmoid(gate)
    hidden_grad = jnp.dot(cotangent_all, down_line, preferred_element_type=f32)
    gate_back = (hidden_grad * upward * sigma * (1.0 + gate * (1.0 - sigma))).astype(bf16)
    up_back = (hidden_grad * (gate * sigma)).astype(bf16)
    both_back = jnp.concatenate([gate_back, up_back], axis=1)
    both_other = to_sibling(both_back)
    feed_in = plain("tf,df->td", both_back, feed_weight).astype(bf16)
    both_other, feed_in = lax.optimization_barrier((both_other, feed_in))
    feed_part = chip_sum(core, h2, both_back, h2_other, both_other)
    feed_part, feed_in = lax.optimization_barrier((feed_part, feed_in))
    feed_sums = scatter_column(feed_part)
    residual_grad, feed_gain_part, mixed_grad, *feed_out = plane_stage(
        5,
        feed_in,
        [residual, cotangent_own, gain_two],
        residual_grad_body,
        [((rows, width), f32), ((8, width), f32)],
        True,
        (hidden, down_line),
    )
    mixed_other = to_sibling(mixed_grad)
    feed_outs = [feed_out[0]] + [send_on(feed_out[k], k) for k in (1, 2, 3)]

    mixed_grad, down_sums = lax.optimization_barrier((mixed_grad, down_sums))
    heads_grad = plain("td,fd->tf", mixed_grad, out_weight).reshape(blocked)
    head_gain_part = jnp.sum(unit_heads * heads_grad, axis=(0, 1))
    scaled_heads = heads_grad * head_gain_f
    out_back = (
        head_factor
        * (scaled_heads - unit_heads * jnp.mean(unit_heads * scaled_heads, axis=-1, keepdims=True))
    ).astype(bf16)
    out_back_f = out_back.astype(f32)
    mixing_grad = plain("btd,bsd->bts", out_back, value) * same
    local_value = plain("bts,btd->bsd", mixing, out_back)
    lifted_grad = grow * precise("bts,bsm->btm", mixing_grad, back) + grow * fresh * precise(
        "btd,bmd->btm", out_back_f, value_state
    )
    score_grad = probs * (lifted_grad - jnp.sum(probs * lifted_grad, axis=-1, keepdims=True))
    inner_grad = grow * score_grad
    state_grad = inner_grad * fresh
    affinity_grad = (precise("btm,bsm->bts", inner_grad, back) * same).astype(bf16)
    first_key = precise("btm,btd->bmd", state_grad, query_f)
    first_value = precise("btm,btd->bmd", entry, out_back_f)
    out_part = chip_sum(core, heads_cut, mixed_grad, heads_other, mixed_other)
    out_part = out_part.reshape(quarter, HEADS, strip, width)
    later_key, later_value, out_part = carry_states(
        6, first_key, first_value, carried, planes, True, out_part
    )
    later_key, feed_outs = lax.optimization_barrier((later_key, feed_outs))

    query_back = plain("bts,bsd->btd", affinity_grad, key) + precise(
        "btm,bmd->btd", state_grad, key_state
    )
    key_back = plain("bts,btd->bsd", affinity_grad, query) + precise(
        "bsm,bmd->bsd", weights, later_key
    )
    value_back = local_value + precise("bsm,bmd->bsd", weights, later_value)
    backs = jnp.concatenate(
        [
            x.astype(bf16).reshape(HEADS * rows, head_size)
            for x in (query_back, key_back, value_back)
        ],
        axis=1,
    )
    backs_other = to_sibling(backs)
    mixer_part = chip_sum(core, h1, backs, h1_other, backs_other, out_part)
    (down_grad,) = return_columns(8, down_sums, 1, part, planes)
    mixer_part, feed_sums, backs, down_grad = lax.optimization_barrier(
        (mixer_part, feed_sums, backs, down_grad)
    )
    mixer_sums = scatter_column(mixer_part)
    mixer_in = plain("tf,df->td", backs, mixer_weight).astype(bf16)
    input_grad, mixer_gain_part, block_out = plane_stage(
        7,
        mixer_in,
        [tokens_own, residual_grad, gain_one, residual, *feed_outs],
        last_body(planes),
        [((rows, width), f32), ((8, width), f32), ((rows, width), bf16)],
        False,
    )

    head_whole = lax.dynamic_update_slice(
        jnp.zeros((width,), f32), head_gain_part, (h * head_size,)
    )
    gain_parts = jnp.stack(
        [
            restored(jnp.sum(mixer_gain_part, axis=0)),
            head_whole,
            restored(jnp.sum(feed_gain_part, axis=0)),
        ]
    )
    gain_parts = gain_parts.reshape(3, count, strip).swapaxes(0, 1)
    gain_parts = jnp.pad(gain_parts, ((0, 0), (0, 5), (0, 128 - strip)))
    gate_grad, up_grad, gain_sums = return_columns(9, feed_sums, 2, part, planes, gain_parts)
    down_grad, gate_grad, up_grad, input_grad, block_out = finished(
        [down_grad, gate_grad, up_grad], [input_grad, block_out]
    )
    mixer_sums, _ = lax.optimization_barrier((mixer_sums, block_out))
    query_grad, key_grad, value_grad, output_grad = return_columns(
        10, mixer_sums, 3, head_size, planes, None, True
    )
    query_grad, key_grad, value_grad, output_grad = finished(
        [query_grad, key_grad, value_grad, output_grad], []
    )
    gain_sums = gain_sums[:3, :strip]
    return (
        block_out,
        input_grad,
        gain_sums[0],
        query_grad,
        key_grad,
        value_grad,
        gain_sums[1],
        output_grad,
        gain_sums[2],
        gate_grad,
        up_grad,
        down_grad,
    )


def solution(mesh):
    split, line = P("seq", None), P("seq")
    return jax.shard_map(
        local,
        mesh=mesh,
        in_specs=(split, split, split, P(), line, split, split, split, line, split, line, split, split, split),
        out_specs=(split, split, line, split, split, split, line, split, line, split, split, split),
        check_vma=False,
    )
```
